256 devices in a mesh: ctx: 64 (over x, z, y_lo), head: 4 (over y_hi, core).
Axes of the slice: x: 4, y: 4 (y_hi: 2, y_lo: 2; y = y_hi * 2 + y_lo), z: 8, core: 2. Of those that a mesh axis runs over, the one named last changes fastest.
Arguments:
- queries: bfloat16 [16384, 2048], P('ctx', 'head'), may hold values from -32 to 32
- key_heads: bfloat16 [16384, 2048], P('ctx', 'head'), may hold values from -32 to 32
- value_heads: bfloat16 [16384, 2048], P('ctx', 'head'), may hold values from -6 to 6
- out_weight: bfloat16 [4096, 2048], P('ctx', 'head'), may hold values from -0.5 to 0.5
- block_lists: int32 [128, 3], replicated, may hold values from 0 to 127, as said below
- out_grad: bfloat16 [16384, 4096], P('ctx', 'head'), may hold values from -16 to 16
Outputs:
- attended: bfloat16 [16384, 4096], P('ctx', 'head')
- query_grad: bfloat16 [16384, 2048], P('ctx', 'head')
- key_grad: bfloat16 [16384, 2048], P('ctx', 'head')
- value_grad: bfloat16 [16384, 2048], P('ctx', 'head')
- weight_grad: float32 [4096, 2048], P('ctx', 'head')
The draws below stay inside these ranges and needn't reach their ends.
Inputs may be any that keep to these rules, and one draw needn't show every extreme that they name: `block_lists`: every entry of row b lies within 4 blocks of b, and the first entry of each row lies exactly 4 blocks away from b.
All inputs are finite; a program needn't handle non-finite values.
Results may differ from the reference program's by a relative error of at most 0.028.
Values may be sent and summed in bfloat16 or wider, within the bound.
A program may use at most 128 MiB of HBM per device.

```python
import jax
import jax.numpy as jnp
from jax import lax

D = 4096
HEADS = 16
HD = 128
BLK = 128
RANDS = 3
NQB = 128
TOKENS = 16384
REACH = 4


def draw_queries(key, part):
    drawn = jnp.clip(jax.random.normal(jax.random.fold_in(key, 11), (TOKENS, HEADS * HD), jnp.float32), -4.0, 4.0)
    return drawn.astype(jnp.bfloat16)


def draw_key_heads(key, part):
    drawn = jnp.clip(jax.random.normal(jax.random.fold_in(key, 21), (TOKENS, HEADS * HD), jnp.float32), -4.0, 4.0)
    return drawn.astype(jnp.bfloat16)


def draw_block_lists(key, part):
    rows = jnp.arange(NQB, dtype=jnp.int32)[:, None]
    offsets = jax.random.randint(jax.random.fold_in(key, 31), (NQB, RANDS), -REACH, REACH + 1)
    signs = jax.random.randint(jax.random.fold_in(key, 32), (NQB, 1), 0, 2) * 2 - 1
    offsets = jnp.concatenate([signs * REACH, offsets[:, 1:]], axis=1).astype(jnp.int32)
    picks = rows + offsets
    return jnp.where((picks < 0) | (picks >= NQB), rows - offsets, picks).astype(jnp.int32)


def with_spikes(result, rng, source, target, shards_of, factor):
    def block_of(dim):
        return (jnp.arange(result.shape[dim]) // (result.shape[dim] // shards_of)).reshape((-1,) + (1,) * (result.ndim - 1 - dim))

    one_side = jax.random.permutation(rng, shards_of)[block_of(target)]
    second = (block_of(target) + shards_of // 2) % shards_of
    return jnp.where((block_of(source) == one_side) | (block_of(source) == second), factor * result, result)


def steps_of(own_key, extent, cuts, low, largest):
    factor_of = 1.0
    for axis_at, blocks in cuts:
        steps = jax.random.uniform(jax.random.fold_in(jax.random.fold_in(own_key, 6), axis_at), (blocks,), jnp.float32, low / len(cuts), largest / len(cuts))
        factor_of = factor_of * jnp.repeat(jnp.exp(steps), extent[axis_at] // blocks).reshape((-1,) + (1,) * (len(extent) - 1 - axis_at))
    return factor_of


def centred(stream_key, shape, scale, reach, shards=(), kind=jnp.bfloat16):
    drawn = jax.random.normal(stream_key, shape, jnp.float32) * scale
    if len(shards) > 0:
        drawn = steps_of(stream_key, shape, shards, -0.22, 0.18) * drawn
    return jnp.clip(drawn, min=-reach, max=reach).astype(kind)


def gaussian_with(key, extent, scale, limit, split, heavy, kind=jnp.bfloat16):
    drawn = scale * jax.random.normal(key, extent, jnp.float32)
    if split:
        drawn = drawn * steps_of(key, extent, split, -0.22, 0.18)
    return jnp.clip(with_spikes(drawn, jax.random.fold_in(key, 3), *heavy), -limit, limit).astype(kind)


def setup_inputs(seed: int = 0) -> dict:
    streams_of = jax.random.split(jax.random.key(seed), 7)
    queries = draw_queries(jax.random.fold_in(streams_of[6], 71), 0)
    key_heads = draw_key_heads(jax.random.fold_in(streams_of[6], 71), 0)
    value_heads = centred(streams_of[2], (TOKENS, HEADS * HD), 1.0, 6.0, ((0, 64), (1, 4)))
    out_weight = centred(streams_of[3], (D, HEADS * HD), HD ** -0.5, 0.5, ((0, 64), (1, 4)))
    block_lists = draw_block_lists(jax.random.fold_in(streams_of[6], 71), 0)
    out_grad = gaussian_with(streams_of[5], (TOKENS, D), 1.0, 16.0, ((0, 64), (1, 4)), (0, 1, 64, 4.0))
    return {"queries": queries, "key_heads": key_heads, "value_heads": value_heads, "out_weight": out_weight, "block_lists": block_lists, "out_grad": out_grad}


def block_table(block_lists):
    total_blocks = block_lists.shape[0]
    rows = jnp.arange(total_blocks, dtype=jnp.int32)[:, None]
    table = jnp.concatenate([jnp.zeros_like(rows), rows - 1, rows, rows + 1, block_lists.astype(jnp.int32)], axis=1)
    width = table.shape[1]
    earlier = jnp.arange(width)[None, :] < jnp.arange(width)[:, None]
    repeated = jnp.any((table[:, :, None] == table[:, None, :]) & earlier[None], axis=2)
    fresh = (table >= 0) & (table < total_blocks) & jnp.logical_not(repeated)
    return jnp.clip(table, 0, total_blocks - 1).astype(jnp.int32), fresh


def block_probs(query_block, key_block, fresh_row, scale):
    scores = jnp.einsum("qhd,khd->hqk", query_block.astype(jnp.float32), key_block.astype(jnp.float32)) * scale
    keep = jnp.repeat(fresh_row, BLK)
    scores = jnp.where(keep[None, None, :], scores, -jnp.inf)
    row_top = jnp.max(scores, axis=2, keepdims=True)
    expo = jnp.exp(scores - row_top)
    return expo / jnp.sum(expo, axis=2, keepdims=True)


def reference(queries, key_heads, value_heads, out_weight, block_lists, out_grad):
    scale = HD ** -0.5
    total_blocks = block_lists.shape[0]
    table, fresh = block_table(block_lists)
    query_blocks = queries.reshape(total_blocks, BLK, HEADS, HD)
    key_blocks = key_heads.reshape(total_blocks, BLK, HEADS, HD)
    value_blocks = value_heads.reshape(total_blocks, BLK, HEADS, HD)
    indices = jnp.arange(total_blocks, dtype=jnp.int32)

    def forward_block(index):
        picks = table[index]
        probs = block_probs(query_blocks[index], key_blocks[picks].reshape(-1, HEADS, HD), fresh[index], scale)
        low = lax.optimization_barrier(probs.astype(jnp.bfloat16)).astype(jnp.float32)
        values_here = value_blocks[picks].reshape(-1, HEADS, HD).astype(jnp.float32)
        return jnp.einsum("hqk,khd->qhd", low, values_here).astype(jnp.bfloat16)

    mixed = lax.map(forward_block, indices).reshape(-1, HEADS * HD)
    attended = jnp.dot(mixed, out_weight.T, preferred_element_type=jnp.float32).astype(jnp.bfloat16)
    mixed_grad = jnp.dot(out_grad, out_weight, preferred_element_type=jnp.float32).astype(jnp.bfloat16)
    weight_grad = jnp.dot(out_grad.T, mixed, preferred_element_type=jnp.float32)
    delta = jnp.sum(mixed_grad.astype(jnp.float32).reshape(-1, HEADS, HD) * mixed.astype(jnp.float32).reshape(-1, HEADS, HD), axis=2)
    delta_blocks = delta.reshape(total_blocks, BLK, HEADS)
    grad_blocks = mixed_grad.reshape(total_blocks, BLK, HEADS, HD)

    def backward_block(carry, index):
        key_acc, value_acc = carry
        picks = table[index]
        keys_here = key_blocks[picks].reshape(-1, HEADS, HD).astype(jnp.float32)
        values_here = value_blocks[picks].reshape(-1, HEADS, HD).astype(jnp.float32)
        probs = block_probs(query_blocks[index], keys_here, fresh[index], scale)
        low = lax.optimization_barrier(probs.astype(jnp.bfloat16)).astype(jnp.float32)
        grad_here = grad_blocks[index].astype(jnp.float32)
        dots = jnp.einsum("qhd,khd->hqk", grad_here, values_here)
        slopes = probs * (dots - delta_blocks[index].T[:, :, None])
        slopes = lax.optimization_barrier(slopes.astype(jnp.bfloat16)).astype(jnp.float32)
        query_here = query_blocks[index].astype(jnp.float32)
        query_grad = (jnp.einsum("hqk,khd->qhd", slopes, keys_here) * scale).astype(jnp.bfloat16)
        key_part = jnp.einsum("hqk,qhd->khd", slopes, query_here).reshape(-1, BLK, HEADS, HD)
        value_part = jnp.einsum("hqk,qhd->khd", low, grad_here).reshape(-1, BLK, HEADS, HD)
        key_acc = key_acc.at[picks].add(key_part)
        value_acc = value_acc.at[picks].add(value_part)
        return (key_acc, value_acc), query_grad

    zeros = jnp.zeros((total_blocks, BLK, HEADS, HD), jnp.float32)
    (key_acc, value_acc), query_grad = lax.scan(backward_block, (zeros, zeros), indices)
    key_grad = (key_acc * scale).reshape(-1, HEADS * HD).astype(jnp.bfloat16)
    value_grad = value_acc.reshape(-1, HEADS * HD).astype(jnp.bfloat16)
    query_grad = query_grad.reshape(-1, HEADS * HD)
    return attended, query_grad, key_grad, value_grad, weight_grad
```

```python
import jax
import jax.numpy as jnp
from jax import lax
from jax.experimental import pallas as pl
from jax.experimental.pallas import tpu as pltpu
from jax.sharding import PartitionSpec as P

HD = 128
BLK = 128
SCALE = HD ** -0.5
BF = jnp.bfloat16
F32 = jnp.float32
NX, NZ, NY = 4, 8, 4
N_COPIES_A = 80
N_COPIES_B = 64


def place():
    i = lax.axis_index("ctx")
    h = lax.axis_index("head")
    cell = i // 2
    return cell // NZ, cell % NZ, (h // 2) * 2 + i % 2, h % 2, cell


def device(x, z, y, core):
    return ((x * NZ + z) * 2 + y % 2, (y // 2) * 2 + core)


def rows(start, size):
    return pl.ds(pl.multiple_of(start, size), size)


class Copies:
    def __init__(self, send, recv):
        self.send, self.recv, self.count = send, recv, 0

    def make(self, src, dst, target):
        k = self.count
        self.count += 1
        return pltpu.make_async_remote_copy(
            src_ref=src,
            dst_ref=dst,
            send_sem=self.send.at[k],
            recv_sem=self.recv.at[k],
            device_id=target,
            device_id_type=pl.DeviceIdType.MESH,
        )

    def start(self, src, dst, target):
        c = self.make(src, dst, target)
        c.start()
        return c


def greet(peers):
    barrier = pltpu.get_barrier_semaphore()
    for peer in peers:
        pl.semaphore_signal(
            barrier, inc=1, device_id=peer, device_id_type=pl.DeviceIdType.MESH
        )
    pl.semaphore_wait(barrier, len(peers))


def all_peers(x, z, y, core, cell):
    up, down = (cell + 1) % (NX * NZ), (cell + NX * NZ - 1) % (NX * NZ)
    peers = [device((x + d) % NX, z, y, core) for d in range(1, NX)]
    peers += [device(x, (z + d) % NZ, y, core) for d in range(1, NZ)]
    peers += [device(x, z, (y + d) % NY, core) for d in (1, NY - 1)]
    peers += [device(x, z, y, 1 - core)]
    peers += [device(c // NZ, c % NZ, y, core) for c in (up, down)]
    return peers


def gather_kernel(q, k, v, w, og, q2, kb, vb, b0, wf, ogf, send, recv, lsem):
    x, z, y, core, cell = place()
    ylo = y % 2
    h = (y // 2) * 2 + core
    x_up, x_dn = (x + 1) % NX, (x + NX - 1) % NX
    z_up, z_dn = (z + 1) % NZ, (z + NZ - 1) % NZ
    y_up, y_dn = (y + 1) % NY, (y + NY - 1) % NY
    c_up, c_dn = (cell + 1) % (NX * NZ), (cell + NX * NZ - 1) % (NX * NZ)
    mate = device(x, z, (y // 2) * 2 + 1 - ylo, core)
    twin = device(x, z, y, 1 - core)
    xu, xd = device(x_up, z, y, core), device(x_dn, z, y, core)
    zu, zd = device(x, z_up, y, core), device(x, z_dn, y, core)
    yu, yd = device(x, z, y_up, core), device(x, z, y_dn, core)
    cu, cd = device(c_up // NZ, c_up % NZ, y, core), device(c_dn // NZ, c_dn % NZ, y, core)
    net = Copies(send, recv)
    mine, other = rows(256 * ylo, 256), rows(256 * (1 - ylo), 256)

    locals_ = [
        pltpu.make_async_copy(w.at[:, mine], wf.at[x, z, rows(64 * ylo, 64), :], lsem.at[0]),
        pltpu.make_async_copy(k.at[:, mine], kb.at[1, mine, :], lsem.at[1]),
        pltpu.make_async_copy(v.at[:, mine], vb.at[1, mine, :], lsem.at[2]),
        pltpu.make_async_copy(q.at[:, mine], q2.at[mine, :], lsem.at[3]),
        pltpu.make_async_copy(og, ogf.at[ylo, h], lsem.at[4]),
    ]
    for c in locals_:
        c.start()
    greet(all_peers(x, z, y, core, cell))

    ends = []

    def go(src, dst, target):
        c = net.start(src, dst, target)
        ends.append(c)
        return c

    w_mate = go(w.at[:, other], wf.at[x, z, rows(64 * ylo, 64), :], mate)
    k_mate = go(k.at[:, other], kb.at[1, mine, :], mate)
    v_mate = go(v.at[:, other], vb.at[1, mine, :], mate)
    og_up = go(og, ogf.at[ylo, h], yu)
    og_dn = go(og, ogf.at[ylo, h], yd)
    og_tw = [go(og, ogf.at[ylo, h], twin)]
    q_mate = go(q.at[:, other], q2.at[mine, :], mate)

    locals_[0].wait()
    w_mate.wait_recv()

    x_plus, x_minus = {}, {}

    def to_x(off):
        zz = (z + off) % NZ
        x_plus[off] = go(wf.at[x, zz], wf.at[x, zz], xu)
        x_minus[off] = go(wf.at[x, zz], wf.at[x, zz], xd)

    up = go(wf.at[x, z], wf.at[x, z], zu)
    dn = go(wf.at[x, z], wf.at[x, z], zd)
    to_x(0)
    halo = [
        go(k.at[:, mine], kb.at[0, mine, :], cu),
        go(k.at[:, mine], kb.at[2, mine, :], cd),
    ]

    def ring_step(s, up, dn):
        zm, zp = (z + NZ - s) % NZ, (z + s) % NZ
        up.wait_recv()
        if s < 3:
            up = go(wf.at[x, zm], wf.at[x, zm], zu)
        else:
            up = go(wf.at[x, zm, 0:64, :], wf.at[x, zm, 0:64, :], zu)
        to_x(NZ - s)
        dn.wait_recv()
        if s < 3:
            dn = go(wf.at[x, zp], wf.at[x, zp], zd)
        else:
            dn = go(wf.at[x, zp, 64:128, :], wf.at[x, zp, 64:128, :], zd)
        to_x(s)
        return up, dn

    up, dn = ring_step(1, up, dn)
    halo += [
        go(v.at[:, mine], vb.at[0, mine, :], cu),
        go(v.at[:, mine], vb.at[2, mine, :], cd),
    ]
    k_mate.wait_recv()
    v_mate.wait_recv()
    locals_[1].wait()
    locals_[2].wait()

    along_z = []
    for d in range(1, NZ):
        target = device(x, (z + d) % NZ, y, core)
        along_z.append(
            (
                net.make(kb.at[1, 0:BLK, :], b0.at[0], target),
                net.make(vb.at[1, 0:BLK, :], b0.at[1], target),
            )
        )
    b_loc = [
        pltpu.make_async_copy(kb.at[1, 0:BLK, :], b0.at[0], lsem.at[5]),
        pltpu.make_async_copy(vb.at[1, 0:BLK, :], b0.at[1], lsem.at[6]),
    ]

    @pl.when(cell == 0)
    def _():
        for d in (4, 5, 3, 6, 2, 7, 1):
            for c in along_z[d - 1]:
                c.start()
        for c in b_loc:
            c.start()

    up, dn = ring_step(2, up, dn)
    halo += [
        go(kb.at[1, other, :], kb.at[0, other, :], cu),
        go(kb.at[1, other, :], kb.at[2, other, :], cd),
    ]
    up, dn = ring_step(3, up, dn)
    halo += [
        go(vb.at[1, other, :], vb.at[0, other, :], cu),
        go(vb.at[1, other, :], vb.at[2, other, :], cd),
    ]

    og_up.wait_recv()
    src_dn = ogf.at[y_dn % 2, (y_dn // 2) * 2 + core]
    fwd_up = go(src_dn.at[0:128, :], src_dn.at[0:128, :], yu)
    og_tw.append(go(src_dn, src_dn, twin))
    og_dn.wait_recv()
    src_up = ogf.at[y_up % 2, (y_up // 2) * 2 + core]
    fwd_dn = go(src_up.at[128:256, :], src_up.at[128:256, :], yd)
    og_tw.append(go(src_up, src_up, twin))

    up.wait_recv()
    dn.wait_recv()
    to_x(4)

    along_x = []
    for d in range(1, NX):
        along_x.append(net.make(b0, b0, device((x + d) % NX, z, y, core)))

    x_fwd = []
    for off in (0, 7, 1, 6, 2, 5, 3, 4):
        zz = (z + off) % NZ
        x_plus[off].wait_recv()
        if off in (0, 6, 2, 4):
            x_fwd.append(go(wf.at[x_dn, zz], wf.at[x_dn, zz], xu))
        x_minus[off].wait_recv()
        if off in (7, 1, 5, 3):
            x_fwd.append(go(wf.at[x_up, zz], wf.at[x_up, zz], xd))
        if off == 1:

            @pl.when((x == 0) & (z != 0))
            def _():
                for d in range(1, NZ):

                    @pl.when(z == d)
                    def _():
                        for c in along_z[d - 1]:
                            c.wait_recv()

            @pl.when(cell == 0)
            def _():
                for c in b_loc:
                    c.wait()

            @pl.when(x == 0)
            def _():
                for c in along_x:
                    c.start()

    fwd_up.wait_recv()
    fwd_dn.wait_recv()
    far = ogf.at[y % 2, ((y + 2) % NY // 2) * 2 + core]
    og_tw.append(go(far, far, twin))

    for c in halo + [q_mate] + x_fwd + og_tw:
        c.wait_recv()

    for d in range(1, NX):

        @pl.when(x == d)
        def _():
            along_x[d - 1].wait_recv()

    for c in ends:
        c.wait_send()

    @pl.when(cell == 0)
    def _():
        for pair in along_z:
            for c in pair:
                c.wait_send()

    @pl.when(x == 0)
    def _():
        for c in along_x:
            c.wait_send()

    locals_[3].wait()
    locals_[4].wait()


def compute_kernel(
    lists, q2, kb, vb, b0, wf, ogf, at, wg, dq, dke, dko, dve, dvo, d0, probs, mixed, mgrad, dk, dv
):
    cell = lax.axis_index("ctx") // 2
    nt = (((1,), (1,)), ((), ()))
    tn = (((0,), (0,)), ((), ()))

    def dot(a, b, dims=(((1,), (0,)), ((), ()))):
        return lax.dot_general(a, b, dims, preferred_element_type=F32)

    def picks(b):
        i = b - 4 * cell
        near = [(i + 4 + d, (b + d >= 1) & (b + d <= 127)) for d in (-1, 0, 1)]
        named = [lists[b, r] for r in range(3)]
        far = []
        for r, n in enumerate(named):
            good = (n >= 1) & ((n < b - 1) | (n > b + 1))
            for m in named[:r]:
                good = good & (n != m)
            far.append((n - 4 * cell + 4, good))
        return near + far

    def tiles(ref, first, found, lanes):
        return jnp.concatenate([first[:, lanes]] + [ref[j, :, lanes] for j, _ in found], axis=0)

    def forward(n, carry):
        i, head = n // 2, n % 2
        lanes = rows(128 * head, 128)
        toks = rows(128 * i, 128)
        found = picks(4 * cell + i)
        keys = tiles(kb, b0.at[0], found, lanes)
        values = tiles(vb, b0.at[1], found, lanes)
        bias = jnp.concatenate(
            [jnp.zeros((1, BLK), F32)]
            + [jnp.full((1, BLK), jnp.where(good, 0.0, -jnp.inf), F32) for _, good in found],
            axis=1,
        )
        s = dot(q2[toks, lanes], keys, nt) * SCALE + bias
        e = jnp.exp(s - jnp.max(s, axis=1, keepdims=True))
        p = e / jnp.sum(e, axis=1, keepdims=True)
        probs[n] = p
        mixed[toks, lanes] = dot(p.astype(BF), values).astype(BF)
        return carry

    lax.fori_loop(0, 8, forward, 0)

    for t in range(2):
        total = jnp.zeros((256, 256), F32)
        for h in range(4):
            total = total + dot(ogf[t, h], wf[h])
        mgrad[256 * t : 256 * (t + 1), :] = total.astype(BF)

    def project(h, carry):
        for t in range(2):
            at[t, h] = dot(mixed[256 * t : 256 * (t + 1), :], wf[h], nt).astype(BF)
        total = dot(mixed[0:256, :], ogf[0, h], tn) + dot(mixed[256:512, :], ogf[1, h], tn)
        for n in range(8):
            wg[h, n] = total[:, 128 * n : 128 * (n + 1)].astype(BF)
        return carry

    lax.fori_loop(0, 4, project, 0)

    dk[...] = jnp.zeros_like(dk)
    dv[...] = jnp.zeros_like(dv)

    def backward(n, carry):
        i, head = n // 2, n % 2
        lanes = rows(128 * head, 128)
        toks = rows(128 * i, 128)
        found = picks(4 * cell + i)
        keys = tiles(kb, b0.at[0], found, lanes)
        values = tiles(vb, b0.at[1], found, lanes)
        g = mgrad[toks, lanes]
        delta = jnp.sum(
            g.astype(F32) * mixed[toks, lanes].astype(F32), axis=1, keepdims=True
        )
        p = probs[n]
        slopes = (p * (dot(g, values, nt) - delta)).astype(BF)
        dq[toks, lanes] = (dot(slopes, keys) * SCALE).astype(BF)
        part_k = dot(slopes, q2[toks, lanes], tn)
        part_v = dot(p.astype(BF), g, tn)
        for m, j in enumerate([12] + [j for j, _ in found]):
            dk[j, :, lanes] += part_k[BLK * m : BLK * (m + 1)]
            dv[j, :, lanes] += part_v[BLK * m : BLK * (m + 1)]
        return carry

    lax.fori_loop(0, 8, backward, 0)
    for n in range(4):
        toks = slice(128 * n, 128 * (n + 1))
        dke[0, toks, :] = (dk[n] * SCALE).astype(BF)
        dko[toks, :] = dk[n + 4] * SCALE
        dke[1, toks, :] = (dk[n + 8] * SCALE).astype(BF)
        dve[0, toks, :] = dv[n].astype(BF)
        dvo[toks, :] = dv[n + 4]
        dve[1, toks, :] = dv[n + 8].astype(BF)
    d0[0] = (dk[12] * SCALE).astype(BF)
    d0[1] = dv[12].astype(BF)


def reduce_kernel(
    at, wg, dq, dke, dko, dve, dvo, d0,
    o_at, o_dq, o_dk, o_dv, o_wg,
    at_core, at_sum, at_r1, at_r2, wg_r1, wg_s, wg_r2, wg_x, wz_s, wz_r, w_out,
    dk_r, dv_r, d0_xr, d0_s, d0_zr, dkv_s, send, recv, lsem,
):
    x, z, y, core, cell = place()
    ylo = y % 2
    x_up, x_dn, x_far = (x + 1) % NX, (x + NX - 1) % NX, (x + 2) % NX
    z_up, z_dn = (z + 1) % NZ, (z + NZ - 1) % NZ
    y_up, y_dn, y_far = (y + 1) % NY, (y + NY - 1) % NY, (y + 2) % NY
    c_up, c_dn = (cell + 1) % (NX * NZ), (cell + NX * NZ - 1) % (NX * NZ)
    mate = device(x, z, (y // 2) * 2 + 1 - ylo, core)
    twin = device(x, z, y, 1 - core)
    xu, xd = device(x_up, z, y, core), device(x_dn, z, y, core)
    zu, zd = device(x, z_up, y, core), device(x, z_dn, y, core)
    yu, yd = device(x, z, y_up, core), device(x, z, y_dn, core)
    cu, cd = device(c_up // NZ, c_up % NZ, y, core), device(c_dn // NZ, c_dn % NZ, y, core)
    net = Copies(send, recv)
    mine, other = rows(256 * ylo, 256), rows(256 * (1 - ylo), 256)
    ends = []

    def go(src, dst, target):
        c = net.start(src, dst, target)
        ends.append(c)
        return c

    q_loc = pltpu.make_async_copy(dq.at[mine, :], o_dq.at[:, mine], lsem.at[0])
    q_loc.start()
    greet(all_peers(x, z, y, core, cell))

    w1u = go(wg.at[x_far, 0:4], wg_r1.at[0], xu)
    w1d = go(wg.at[x_far, 4:8], wg_r1.at[1], xd)
    order = (y_far, y_up, y_dn, y)
    cores = [
        go(at.at[t % 2, (t // 2) * 2 + 1 - core], at_core.at[t], twin) for t in order
    ]
    w2u = [go(wg.at[x_up, 4:8], wg_r2.at[0, 4:8], xu)]
    w2d = [go(wg.at[x_dn, 0:4], wg_r2.at[1, 0:4], xd)]
    to_x0 = [net.make(d0, d0_xr.at[d - 1], device(0, z, y, core)) for d in range(1, NX)]
    for d in range(1, NX):

        @pl.when(x == d)
        def _():
            to_x0[d - 1].start()

    edges = [
        go(dke.at[0], dk_r.at[1], cd),
        go(dke.at[1], dk_r.at[0], cu),
        go(dve.at[0], dv_r.at[1], cd),
        go(dve.at[1], dv_r.at[0], cu),
    ]
    q_mate = go(dq.at[other, :], o_dq.at[:, mine], mate)

    def add(n, dst, *srcs):
        def body(i, carry):
            r = rows(32 * i, 32)
            total = srcs[0][r, :].astype(F32)
            for s in srcs[1:]:
                total = total + s[r, :].astype(F32)
            dst[r, :] = total.astype(dst.dtype)
            return carry

        lax.fori_loop(0, n, body, 0)

    for n, t in enumerate(order):
        cores[n].wait_recv()
        add(8, at_sum.at[t], at.at[t % 2, (t // 2) * 2 + core], at_core.at[t])
        if n == 0:
            a1u = go(at_sum.at[t, 0:128, :], at_r1.at[0], yu)
            a1d = go(at_sum.at[t, 128:256, :], at_r1.at[1], yd)
        if n == 1:
            a2u = [go(at_sum.at[t, 128:256, :], at_r2.at[0, 128:256, :], yu)]
        if n == 2:
            a2d = [go(at_sum.at[t, 0:128, :], at_r2.at[1, 0:128, :], yd)]

    w1u.wait_recv()
    for n in range(4):
        add(8, wg_s.at[0, n], wg.at[x_up, n], wg_r1.at[0, n])
    w2u.append(go(wg_s.at[0], wg_r2.at[0, 0:4], xu))
    w1d.wait_recv()
    for n in range(4):
        add(8, wg_s.at[1, n], wg.at[x_dn, 4 + n], wg_r1.at[1, n])
    w2d.append(go(wg_s.at[1], wg_r2.at[1, 4:8], xd))

    a1u.wait_recv()
    add(4, at_s2_up := at_core.at[0, 0:128, :], at_sum.at[y_up, 0:128, :], at_r1.at[0])
    a2u.append(go(at_s2_up, at_r2.at[0, 0:128, :], yu))
    a1d.wait_recv()
    add(4, at_s2_dn := at_core.at[1, 128:256, :], at_sum.at[y_dn, 128:256, :], at_r1.at[1])
    a2d.append(go(at_s2_dn, at_r2.at[1, 128:256, :], yd))

    to_z0 = [net.make(d0_s, d0_zr.at[d - 1], device(x, 0, y, core)) for d in range(1, NZ)]

    @pl.when(x == 0)
    def _():
        for c in to_x0:
            c.wait_recv()
        for n in range(2):
            add(4, d0_s.at[n], d0.at[n], d0_xr.at[0, n], d0_xr.at[1, n], d0_xr.at[2, n])
        for d in range(1, NZ):

            @pl.when(z == d)
            def _():
                to_z0[d - 1].start()

    for c in w2u + w2d:
        c.wait_recv()
    for n in range(NZ):
        add(8, wg_x.at[n], wg.at[x, n], wg_r2.at[0, n], wg_r2.at[1, n])

    zf = (z + 4) % NZ
    add(4, wz_s.at[0, 0, 0:128, :], wg_x.at[zf, 0:128, :])
    up = go(wz_s.at[0, 0, 0:128, :], wz_r.at[0, 0, 0:128, :], zu)
    add(4, wz_s.at[1, 0, 128:256, :], wg_x.at[zf, 128:256, :])
    dn = go(wz_s.at[1, 0, 128:256, :], wz_r.at[1, 0, 128:256, :], zd)

    for c in edges:
        c.wait_recv()
    kv_mate = []

    @pl.when(cell == 0)
    def _():
        for c in to_z0:
            c.wait_recv()

    for n, (own, got) in enumerate(((dko, dk_r), (dvo, dv_r))):
        add(12, dkv_s.at[n, 128:512, :], own.at[128:512, :], got.at[0, 128:512, :], got.at[1, 128:512, :])

        @pl.when(cell == 0)
        def _():
            add(
                4, dkv_s.at[n, 0:128, :], own.at[0:128, :], got.at[0, 0:128, :],
                got.at[1, 0:128, :], d0_s.at[n], *[d0_zr.at[d, n] for d in range(NZ - 1)],
            )

        @pl.when(cell != 0)
        def _():
            add(4, dkv_s.at[n, 0:128, :], own.at[0:128, :], got.at[0, 0:128, :], got.at[1, 0:128, :])

    for s in (2, 3, 4):
        lo = 5 - s
        tu, td = (z + lo) % NZ, (z + NZ - lo) % NZ
        up.wait_recv()
        if s == 2:
            add(4, wz_s.at[0, 1, 0:128, :], wg_x.at[tu, 0:128, :], wz_r.at[0, 0, 0:128, :])
            add(4, wz_s.at[0, 1, 128:256, :], wg_x.at[tu, 128:256, :])
        else:
            add(8, wz_s.at[0, s - 1], wg_x.at[tu], wz_r.at[0, s - 2])
        up = go(wz_s.at[0, s - 1], wz_r.at[0, s - 1], zu)
        dn.wait_recv()
        if s == 2:
            add(4, wz_s.at[1, 1, 128:256, :], wg_x.at[td, 128:256, :], wz_r.at[1, 0, 128:256, :])
            add(4, wz_s.at[1, 1, 0:128, :], wg_x.at[td, 0:128, :])
        else:
            add(8, wz_s.at[1, s - 1], wg_x.at[td], wz_r.at[1, s - 2])
        dn = go(wz_s.at[1, s - 1], wz_r.at[1, s - 1], zd)
        if s == 2:
            for n, out in enumerate((o_dk, o_dv)):
                kv_mate.append(go(dkv_s.at[n, other, :], out.at[:, mine], mate))
                out[:, mine] = dkv_s[n, mine, :]
    up.wait_recv()
    dn.wait_recv()
    add(8, wg_x.at[z], wg_x.at[z], wz_r.at[0, 3], wz_r.at[1, 3])
    w_out[...] = wg_x[z].T
    w_mate = go(w_out.at[rows(64 * (1 - ylo), 64), :], o_wg.at[:, mine], mate)
    o_wg[:, mine] = w_out[rows(64 * ylo, 64), :]

    for c in a2u + a2d:
        c.wait_recv()
    add(8, o_at, at_sum.at[y], at_r2.at[0], at_r2.at[1])
    for c in kv_mate + [w_mate, q_mate]:
        c.wait_recv()
    q_loc.wait()

    for c in ends:
        c.wait_send()
    for d in range(1, NX):

        @pl.when(x == d)
        def _():
            to_x0[d - 1].wait_send()

    for d in range(1, NZ):

        @pl.when((x == 0) & (z == d))
        def _():
            to_z0[d - 1].wait_send()


def vmem(n):
    return [pl.BlockSpec(memory_space=pltpu.VMEM)] * n


def shape(dims, dtype=BF):
    return jax.ShapeDtypeStruct(dims, dtype)


def local(queries, key_heads, value_heads, out_weight, block_lists, out_grad):
    limit = 60 * 1024 * 1024
    q2, kb, vb, b0, wf, ogf = pl.pallas_call(
        gather_kernel,
        out_shape=(
            shape((512, 256)),
            shape((3, 512, 256)),
            shape((3, 512, 256)),
            shape((2, 128, 256)),
            shape((NX, NZ, 128, 256)),
            shape((2, 4, 256, 1024)),
        ),
        in_specs=vmem(5),
        out_specs=tuple(vmem(6)),
        scratch_shapes=[
            pltpu.SemaphoreType.DMA((N_COPIES_A,)),
            pltpu.SemaphoreType.DMA((N_COPIES_A,)),
            pltpu.SemaphoreType.DMA((8,)),
        ],
        compiler_params=pltpu.CompilerParams(
            collective_id=0, has_side_effects=True, vmem_limit_bytes=limit
        ),
        name="gather",
    )(queries, key_heads, value_heads, out_weight, out_grad)

    at, wg, dq, dke, dko, dve, dvo, d0 = pl.pallas_call(
        compute_kernel,
        out_shape=(
            shape((2, 4, 256, 1024)),
            shape((4, 8, 256, 128)),
            shape((512, 256)),
            shape((2, 512, 256)),
            shape((512, 256), F32),
            shape((2, 512, 256)),
            shape((512, 256), F32),
            shape((2, 128, 256)),
        ),
        in_specs=[pl.BlockSpec(memory_space=pltpu.SMEM)] + vmem(6),
        out_specs=tuple(vmem(8)),
        scratch_shapes=[
            pltpu.VMEM((8, 128, 896), F32),
            pltpu.VMEM((512, 256), BF),
            pltpu.VMEM((512, 256), BF),
            pltpu.VMEM((13, 128, 256), F32),
            pltpu.VMEM((13, 128, 256), F32),
        ],
        compiler_params=pltpu.CompilerParams(vmem_limit_bytes=limit),
        name="layer",
    )(
        block_lists,
        q2,
        kb.reshape(12, 128, 256),
        vb.reshape(12, 128, 256),
        b0,
        wf.reshape(4, 1024, 256),
        ogf,
    )

    return pl.pallas_call(
        reduce_kernel,
        out_shape=(
            shape((256, 1024)),
            shape((256, 512)),
            shape((256, 512)),
            shape((256, 512)),
            shape((64, 512), F32),
        ),
        in_specs=vmem(8),
        out_specs=tuple(vmem(5)),
        scratch_shapes=[
            pltpu.VMEM((4, 256, 1024), BF),
            pltpu.VMEM((4, 256, 1024), BF),
            pltpu.VMEM((2, 128, 1024), BF),
            pltpu.VMEM((2, 256, 1024), BF),
            pltpu.VMEM((2, 4, 256, 128), BF),
            pltpu.VMEM((2, 4, 256, 128), BF),
            pltpu.VMEM((2, 8, 256, 128), BF),
            pltpu.VMEM((8, 256, 128), F32),
            pltpu.VMEM((2, 4, 256, 128), BF),
            pltpu.VMEM((2, 4, 256, 128), BF),
            pltpu.VMEM((128, 256), F32),
            pltpu.VMEM((2, 512, 256), BF),
            pltpu.VMEM((2, 512, 256), BF),
            pltpu.VMEM((3, 2, 128, 256), BF),
            pltpu.VMEM((2, 128, 256), BF),
            pltpu.VMEM((7, 2, 128, 256), BF),
            pltpu.VMEM((2, 512, 256), BF),
            pltpu.SemaphoreType.DMA((N_COPIES_B,)),
            pltpu.SemaphoreType.DMA((N_COPIES_B,)),
            pltpu.SemaphoreType.DMA((2,)),
        ],
        compiler_params=pltpu.CompilerParams(
            collective_id=1, has_side_effects=True, vmem_limit_bytes=limit
        ),
        name="reduce",
    )(at, wg, dq, dke, dko, dve, dvo, d0)


def solution(mesh):
    placed = P("ctx", "head")
    return jax.shard_map(
        local,
        mesh=mesh,
        in_specs=(placed, placed, placed, placed, P(), placed),
        out_specs=(placed,) * 5,
        check_vma=False,
    )
```

```python
import jax
import jax.numpy as jnp
from jax import lax
from jax.experimental import pallas as pl
from jax.experimental.pallas import tpu as pltpu
from jax.sharding import PartitionSpec as P

HD = 128
BLK = 128
SCALE = HD ** -0.5
BF = jnp.bfloat16
F32 = jnp.float32
NX, NZ, NY = 4, 8, 4
N_COPIES = 160


def place():
    i = lax.axis_index("ctx")
    h = lax.axis_index("head")
    cell = i // 2
    return cell // NZ, cell % NZ, (h // 2) * 2 + i % 2, h % 2, cell


def device(x, z, y, core):
    return ((x * NZ + z) * 2 + y % 2, (y // 2) * 2 + core)


def rows(start, size):
    return pl.ds(pl.multiple_of(start, size), size)


class Copies:
    def __init__(self, send, recv):
        self.send, self.recv, self.count = send, recv, 0

    def make(self, src, dst, target):
        k = self.count
        self.count += 1
        return pltpu.make_async_remote_copy(
            src_ref=src,
            dst_ref=dst,
            send_sem=self.send.at[k],
            recv_sem=self.recv.at[k],
            device_id=target,
            device_id_type=pl.DeviceIdType.MESH,
        )

    def start(self, src, dst, target):
        c = self.make(src, dst, target)
        c.start()
        return c


def greet(peers):
    barrier = pltpu.get_barrier_semaphore()
    for peer in peers:
        pl.semaphore_signal(
            barrier, inc=1, device_id=peer, device_id_type=pl.DeviceIdType.MESH
        )
    pl.semaphore_wait(barrier, len(peers))


def all_peers(x, z, y, core, cell):
    up, down = (cell + 1) % (NX * NZ), (cell + NX * NZ - 1) % (NX * NZ)
    peers = [device((x + d) % NX, z, y, core) for d in range(1, NX)]
    peers += [device(x, (z + d) % NZ, y, core) for d in range(1, NZ)]
    peers += [device(x, z, (y + d) % NY, core) for d in (1, NY - 1)]
    peers += [device(x, z, y, 1 - core)]
    peers += [device(c // NZ, c % NZ, y, core) for c in (up, down)]
    return peers


def dot(a, b, dims=(((1,), (0,)), ((), ()))):
    return lax.dot_general(a, b, dims, preferred_element_type=F32)


NT = (((1,), (1,)), ((), ()))
TN = (((0,), (0,)), ((), ()))


def add(dst, *srcs):
    n, lanes = dst.shape
    step = min(n, 16384 // lanes)

    def body(i, carry):
        r = rows(step * i, step)
        total = srcs[0][r, :].astype(F32)
        for s in srcs[1:]:
            total = total + s[r, :].astype(F32)
        dst[r, :] = total.astype(dst.dtype)
        return carry

    lax.fori_loop(0, n // step, body, 0)


def layer_kernel(
    q, k, v, w, lists_hbm, og,
    o_at, o_dq, o_dk, o_dv, o_wg,
    lists, q2, kb, vb, b0, wf, ogf, at, wg, probs, mixed, mgrad, dk, dv, d0, dq,
    at_core, at_sum, at_r1, at_r2, at_o, wg_r1, wg_s, wg_r2, wg_x, wz_s, wz_r, w_out,
    dke, dk_r, d0_b, d0_xr, d0_s, d0_zr, d0_t, d0_z0, dkv_s, d_out, send, recv, lsem,
):
    x, z, y, core, cell = place()
    ylo = y % 2
    h = (y // 2) * 2 + core
    x_up, x_dn, x_far = (x + 1) % NX, (x + NX - 1) % NX, (x + 2) % NX
    z_up, z_dn = (z + 1) % NZ, (z + NZ - 1) % NZ
    c_up, c_dn = (cell + 1) % (NX * NZ), (cell + NX * NZ - 1) % (NX * NZ)
    y_mate = y + 1 - 2 * ylo
    y_next = (y + NY - 1 + 2 * ylo) % NY
    y_far = (y + 2) % NY
    mate, nxt = device(x, z, y_mate, core), device(x, z, y_next, core)
    twin = device(x, z, y, 1 - core)
    xu, xd = device(x_up, z, y, core), device(x_dn, z, y, core)
    zu, zd = device(x, z_up, y, core), device(x, z_dn, y, core)
    cu, cd = device(c_up // NZ, c_up % NZ, y, core), device(c_dn // NZ, c_dn % NZ, y, core)
    net = Copies(send, recv)
    mine, other = rows(256 * ylo, 256), rows(256 * (1 - ylo), 256)
    band_mine, band_other = rows(512 + 256 * ylo, 256), rows(512 + 256 * (1 - ylo), 256)
    lo_mine, lo_other = mine, other
    hi_mine, hi_other = rows(1024 + 256 * ylo, 256), rows(1024 + 256 * (1 - ylo), 256)
    ends, n_local = [], [0]

    def go(src, dst, target):
        c = net.start(src, dst, target)
        ends.append(c)
        return c

    def here(src, dst):
        c = pltpu.make_async_copy(src, dst, lsem.at[n_local[0]])
        n_local[0] += 1
        return c

    def here_now(src, dst):
        c = here(src, dst)
        c.start()
        return c

    w_loc = here_now(w.at[:, mine], wf.at[x, z, rows(64 * ylo, 64), :])
    k_loc = here_now(k.at[:, mine], kb.at[band_mine, :])
    v_loc = here_now(v.at[:, mine], vb.at[band_mine, :])
    og_loc = here_now(og, ogf.at[ylo, h])
    q_loc = here_now(q.at[:, mine], q2.at[mine, :])
    list_loc = here_now(lists_hbm, lists)
    greet(all_peers(x, z, y, core, cell))

    w_mate = go(w.at[:, other], wf.at[x, z, rows(64 * ylo, 64), :], mate)
    k_mate = go(k.at[:, other], kb.at[band_mine, :], mate)
    v_mate = go(v.at[:, other], vb.at[band_mine, :], mate)
    og_next = go(og, ogf.at[ylo, h], nxt)
    og_mate = go(og, ogf.at[ylo, h], mate)
    og_tw = [go(og, ogf.at[ylo, h], twin)]
    q_mate = go(q.at[:, other], q2.at[mine, :], mate)

    w_loc.wait()
    w_mate.wait_recv()

    x_plus, x_minus = {}, {}

    def to_x(off):
        zz = (z + off) % NZ
        x_plus[off] = go(wf.at[x, zz], wf.at[x, zz], xu)
        x_minus[off] = go(wf.at[x, zz], wf.at[x, zz], xd)

    up = go(wf.at[x, z], wf.at[x, z], zu)
    dn = go(wf.at[x, z], wf.at[x, z], zd)
    to_x(0)
    halo = [
        go(k.at[:, mine], kb.at[lo_mine, :], cu),
        go(k.at[:, mine], kb.at[hi_mine, :], cd),
    ]

    def ring_step(s, up, dn):
        zm, zp = (z + NZ - s) % NZ, (z + s) % NZ
        up.wait_recv()
        if s < 3:
            up = go(wf.at[x, zm], wf.at[x, zm], zu)
        else:
            up = go(wf.at[x, zm, 0:64, :], wf.at[x, zm, 0:64, :], zu)
        to_x(NZ - s)
        dn.wait_recv()
        if s < 3:
            dn = go(wf.at[x, zp], wf.at[x, zp], zd)
        else:
            dn = go(wf.at[x, zp, 64:128, :], wf.at[x, zp, 64:128, :], zd)
        to_x(s)
        return up, dn

    up, dn = ring_step(1, up, dn)
    halo += [
        go(v.at[:, mine], vb.at[lo_mine, :], cu),
        go(v.at[:, mine], vb.at[hi_mine, :], cd),
    ]
    k_mate.wait_recv()
    v_mate.wait_recv()
    k_loc.wait()
    v_loc.wait()

    own_k0, own_v0 = kb.at[512 : 512 + BLK, :], vb.at[512 : 512 + BLK, :]
    tree = [
        (
            net.make(own_k0, b0.at[0], device(x, (z + d) % NZ, y, core)),
            net.make(own_v0, b0.at[1], device(x, (z + d) % NZ, y, core)),
        )
        for d in (1, 3, 5, 7)
    ]
    z_leaf = jnp.where(z == 7, 6, (z + 1) % NZ)
    leaf = net.make(b0, b0, device(x, z_leaf, y, core))
    b_loc = [here(own_k0, b0.at[0]), here(own_v0, b0.at[1])]
    along_x = [net.make(b0, b0, device((x + d) % NX, z, y, core)) for d in range(1, NX)]

    @pl.when(cell == 0)
    def _():
        for n in (1, 2, 0, 3):
            for c in tree[n]:
                c.start()
        for c in b_loc:
            c.start()

    up, dn = ring_step(2, up, dn)
    halo += [
        go(kb.at[band_other, :], kb.at[lo_other, :], cu),
        go(kb.at[band_other, :], kb.at[hi_other, :], cd),
    ]
    up, dn = ring_step(3, up, dn)
    halo += [
        go(vb.at[band_other, :], vb.at[lo_other, :], cu),
        go(vb.at[band_other, :], vb.at[hi_other, :], cd),
    ]

    cut = 224
    og_mate.wait_recv()
    from_mate = ogf.at[y_mate % 2, (y_mate // 2) * 2 + core]
    fwd_next = go(from_mate.at[0:cut, :], from_mate.at[0:cut, :], nxt)
    og_tw.append(go(from_mate, from_mate, twin))

    @pl.when(x == 0)
    def _():
        for n, d in enumerate((1, 3, 5, 7)):

            @pl.when(z == d)
            def _():
                for c in tree[n]:
                    c.wait_recv()

        @pl.when((z == 1) | (z == 3) | (z == 7))
        def _():
            leaf.start()

    up.wait_recv()
    dn.wait_recv()
    to_x(4)
    og_next.wait_recv()
    from_next = ogf.at[y_next % 2, (y_next // 2) * 2 + core]
    fwd_mate = go(from_next.at[cut:256, :], from_next.at[cut:256, :], mate)
    og_tw.append(go(from_next, from_next, twin))

    x_fwd = []

    def pass_x(off):
        zz = (z + off) % NZ
        x_plus[off].wait_recv()
        if off in (0, 6, 2, 4):
            x_fwd.append(go(wf.at[x_dn, zz], wf.at[x_dn, zz], xu))
        x_minus[off].wait_recv()
        if off in (7, 1, 5, 3):
            x_fwd.append(go(wf.at[x_up, zz], wf.at[x_up, zz], xd))

    for off in (0, 7, 1):
        pass_x(off)

    @pl.when((x == 0) & ((z == 2) | (z == 4) | (z == 6)))
    def _():
        leaf.wait_recv()

    @pl.when(cell == 0)
    def _():
        for c in b_loc:
            c.wait()

    @pl.when(x == 0)
    def _():
        for c in along_x:
            c.start()

    for off in (6, 2):
        pass_x(off)
    for c in halo + [q_mate]:
        c.wait_recv()
    q_loc.wait()
    list_loc.wait()
    for d in range(1, NX):

        @pl.when(x == d)
        def _():
            along_x[d - 1].wait_recv()

    def window(n):
        i, head = n % 4, n // 4
        return i, head, rows(128 * i, 128), pl.ds(pl.multiple_of(128 * i, 128), 1152), rows(128 * head, 128)

    def forward(n, carry):
        i, head, toks, win, lanes = window(n)
        b = 4 * cell + i
        bias = []
        for j in range(9):
            kbl = b - 4 + j
            good = (kbl >= 1) & (kbl <= 127)
            if j not in (3, 4, 5):
                named = (lists[b, 0] == kbl) | (lists[b, 1] == kbl) | (lists[b, 2] == kbl)
                good = good & named
            bias.append(jnp.full((1, BLK), jnp.where(good, 0.0, -jnp.inf), F32))
        bias = jnp.concatenate(bias, axis=1)
        qq = q2[toks, lanes]
        s0 = dot(qq, b0[0, :, lanes], NT) * SCALE
        s1 = dot(qq, kb[win, lanes], NT) * SCALE + bias
        top = jnp.maximum(jnp.max(s0, axis=1, keepdims=True), jnp.max(s1, axis=1, keepdims=True))
        e0, e1 = jnp.exp(s0 - top), jnp.exp(s1 - top)
        inv = 1.0 / (jnp.sum(e0, axis=1, keepdims=True) + jnp.sum(e1, axis=1, keepdims=True))
        p0, p1 = e0 * inv, e1 * inv
        probs[n, :, 0:BLK] = p0
        probs[n, :, BLK:] = p1
        out = dot(p0.astype(BF), b0[1, :, lanes]) + dot(p1.astype(BF), vb[win, lanes])
        mixed[toks, lanes] = out.astype(BF)
        return carry

    lax.fori_loop(0, 4, forward, 0)
    for off in (5, 3, 4):
        pass_x(off)
    fwd_next.wait_recv()
    fwd_mate.wait_recv()
    far = ogf.at[y_far % 2, (y_far // 2) * 2 + core]
    og_tw.append(go(far, far, twin))
    lax.fori_loop(4, 8, forward, 0)
    og_loc.wait()
    for c in og_tw:
        c.wait_recv()

    def weight_part(xx):
        total = dot(mixed[0:256, :], ogf[0, xx], TN) + dot(mixed[256:512, :], ogf[1, xx], TN)
        for n in range(8):
            wg[xx, n] = total[:, 128 * n : 128 * (n + 1)].astype(BF)

    def attended_part(t, c):
        hh = (t // 2) * 2 + c
        part = dot(mixed[rows(256 * (t % 2), 256), :], wf[hh].reshape(1024, 256), NT)
        at[t % 2, hh] = part.astype(BF)

    weight_part(x_far)
    w1u = go(wg.at[x_far, 0:4], wg_r1.at[0], xu)
    w1d = go(wg.at[x_far, 4:8], wg_r1.at[1], xd)
    weight_part(x_up)
    w2u = [go(wg.at[x_up, 4:8], wg_r2.at[0, 4:8], xu)]
    weight_part(x_dn)
    w2d = [go(wg.at[x_dn, 0:4], wg_r2.at[1, 0:4], xd)]
    for c in x_fwd:
        c.wait_recv()
    order = (y_far, y_mate, y_next, y)
    cores = []
    for t in order:
        attended_part(t, 1 - core)
        cores.append(go(at.at[t % 2, (t // 2) * 2 + 1 - core], at_core.at[t], twin))
    for t in order:
        attended_part(t, core)

    w1u.wait_recv()
    for n in range(4):
        add(wg_s.at[0, n], wg.at[x_up, n], wg_r1.at[0, n])
    w2u.append(go(wg_s.at[0], wg_r2.at[0, 0:4], xu))
    w1d.wait_recv()
    for n in range(4):
        add(wg_s.at[1, n], wg.at[x_dn, 4 + n], wg_r1.at[1, n])
    w2d.append(go(wg_s.at[1], wg_r2.at[1, 4:8], xd))

    for n, t in enumerate(order):
        cores[n].wait_recv()
        add(at_sum.at[t], at.at[t % 2, (t // 2) * 2 + core], at_core.at[t])
        if n == 0:
            a1n = go(at_sum.at[t, 0:128, :], at_r1.at[0], nxt)
            a1m = go(at_sum.at[t, 128:256, :], at_r1.at[1], mate)
        if n == 1:
            a2m = [go(at_sum.at[t, 128:256, :], at_r2.at[0, 128:256, :], mate)]
        if n == 2:
            a2n = [go(at_sum.at[t, 0:128, :], at_r2.at[1, 0:128, :], nxt)]
    weight_part(x)

    for t in range(2):
        total = jnp.zeros((256, 256), F32)
        for hh in range(4):
            total = total + dot(ogf[t, hh], wf[hh].reshape(1024, 256))
        mgrad[256 * t : 256 * (t + 1), :] = total.astype(BF)
    dk[...] = jnp.zeros_like(dk)
    dv[...] = jnp.zeros_like(dv)
    d0[...] = jnp.zeros_like(d0)

    def backward(n, carry):
        i, head, toks, win, lanes = window(n)
        g = mgrad[toks, lanes]
        delta = jnp.sum(
            g.astype(F32) * mixed[toks, lanes].astype(F32), axis=1, keepdims=True
        )
        p0, p1 = probs[n, :, 0:BLK], probs[n, :, BLK:]
        sl0 = (p0 * (dot(g, b0[1, :, lanes], NT) - delta)).astype(BF)
        sl1 = (p1 * (dot(g, vb[win, lanes], NT) - delta)).astype(BF)
        out = dot(sl0, b0[0, :, lanes]) + dot(sl1, kb[win, lanes])
        dq[toks, lanes] = (out * SCALE).astype(BF)
        qq = q2[toks, lanes]
        dk[win, lanes] += dot(sl1, qq, TN)
        dv[win, lanes] += dot(p1.astype(BF), g, TN)
        d0[0, :, lanes] += dot(sl0, qq, TN)
        d0[1, :, lanes] += dot(p0.astype(BF), g, TN)
        return carry

    edges, to_x0, q_out = [], [], []

    def leave(head):
        lanes = slice(128 * head, 128 * (head + 1))
        for n, (acc, factor) in enumerate(((dk, SCALE), (dv, 1.0))):
            dke[head, n, 0] = (acc[0:512, lanes] * factor).astype(BF)
            dke[head, n, 1] = (acc[1024:1536, lanes] * factor).astype(BF)
            d0_b[head, n] = (d0[n, :, lanes] * factor).astype(BF)
        edges.append(
            [go(dke.at[head, n, 0], dk_r.at[head, n, 1], cd) for n in range(2)]
            + [go(dke.at[head, n, 1], dk_r.at[head, n, 0], cu) for n in range(2)]
        )
        to_x0.append(
            [
                net.make(d0_b.at[head], d0_xr.at[head, d - 1], device(0, z, y, core))
                for d in range(1, NX)
            ]
        )
        for d in range(1, NX):

            @pl.when(x == d)
            def _():
                to_x0[head][d - 1].start()

        cols = rows(256 * ylo + 128 * head, 128)
        q_out.append(go(dq.at[other, lanes], o_dq.at[:, cols], mate))
        locals_out.append(here_now(dq.at[mine, lanes], o_dq.at[:, cols]))

    locals_out = []
    lax.fori_loop(0, 2, backward, 0)

    a1n.wait_recv()
    to_mate = at_core.at[0, 0:128, :]
    add(to_mate, at_sum.at[y_mate, 0:128, :], at_r1.at[0])
    a2m.append(go(to_mate, at_r2.at[0, 0:128, :], mate))
    a1m.wait_recv()
    to_next = at_core.at[1, 128:256, :]
    add(to_next, at_sum.at[y_next, 128:256, :], at_r1.at[1])
    a2n.append(go(to_next, at_r2.at[1, 128:256, :], nxt))

    lax.fori_loop(2, 4, backward, 0)
    leave(0)
    lax.fori_loop(4, 8, backward, 0)
    leave(1)

    for c in w2u + w2d:
        c.wait_recv()
    for n in range(NZ):
        add(wg_x.at[n], wg.at[x, n], wg_r2.at[0, n], wg_r2.at[1, n])

    zf = (z + 4) % NZ
    add(wz_s.at[0, 0, 0:128, :], wg_x.at[zf, 0:128, :])
    up = go(wz_s.at[0, 0, 0:128, :], wz_r.at[0, 0, 0:128, :], zu)
    add(wz_s.at[1, 0, 128:256, :], wg_x.at[zf, 128:256, :])
    dn = go(wz_s.at[1, 0, 128:256, :], wz_r.at[1, 0, 128:256, :], zd)

    z_stem = jnp.where(z == 6, 7, (z + NZ - 1) % NZ)
    stem = [net.make(d0_s.at[a], d0_zr.at[a], device(x, z_stem, y, core)) for a in range(2)]
    root = [
        [net.make(d0_t.at[a], d0_z0.at[a, n], device(x, 0, y, core)) for n in range(4)]
        for a in range(2)
    ]

    def sum_x(a):
        @pl.when(x == 0)
        def _():
            for c in to_x0[a]:
                c.wait_recv()
            for n in range(2):
                add(d0_s.at[a, n], d0_b.at[a, n], *[d0_xr.at[a, d, n] for d in range(3)])

            @pl.when((z == 2) | (z == 4) | (z == 6))
            def _():
                stem[a].start()

    def sum_z(a):
        @pl.when(x == 0)
        def _():
            @pl.when((z == 1) | (z == 3) | (z == 7))
            def _():
                stem[a].wait_recv()
                for n in range(2):
                    add(d0_t.at[a, n], d0_s.at[a, n], d0_zr.at[a, n])

            @pl.when(z == 5)
            def _():
                for n in range(2):
                    add(d0_t.at[a, n], d0_s.at[a, n])

            for n in range(4):

                @pl.when(z == 2 * n + 1)
                def _():
                    root[a][n].start()

    def z_step(s, up, dn):
        lo = 5 - s
        tu, td = (z + lo) % NZ, (z + NZ - lo) % NZ
        up.wait_recv()
        if s == 2:
            add(wz_s.at[0, 1, 0:128, :], wg_x.at[tu, 0:128, :], wz_r.at[0, 0, 0:128, :])
            add(wz_s.at[0, 1, 128:256, :], wg_x.at[tu, 128:256, :])
        else:
            add(wz_s.at[0, s - 1], wg_x.at[tu], wz_r.at[0, s - 2])
        up = go(wz_s.at[0, s - 1], wz_r.at[0, s - 1], zu)
        dn.wait_recv()
        if s == 2:
            add(wz_s.at[1, 1, 128:256, :], wg_x.at[td, 128:256, :], wz_r.at[1, 0, 128:256, :])
            add(wz_s.at[1, 1, 0:128, :], wg_x.at[td, 0:128, :])
        else:
            add(wz_s.at[1, s - 1], wg_x.at[td], wz_r.at[1, s - 2])
        dn = go(wz_s.at[1, s - 1], wz_r.at[1, s - 1], zd)
        return up, dn

    kv_mate, kv_here = [[], []], [[], []]

    def finish(head):
        for c in edges[head]:
            c.wait_recv()
        lanes = slice(128 * head, 128 * (head + 1))
        cols = rows(256 * ylo + 128 * head, 128)
        for n, (acc, factor) in enumerate(((dk, SCALE), (dv, 1.0))):
            dkv_s[n, :, lanes] = (
                acc[512:1024, lanes] * factor
                + dk_r[head, n, 0].astype(F32)
                + dk_r[head, n, 1].astype(F32)
            )
            out = (o_dk, o_dv)[n]
            kv_mate[head].append(net.make(d_out.at[n, other, lanes], out.at[:, cols], mate))
            kv_here[head].append(here(d_out.at[n, mine, lanes], out.at[:, cols]))

        @pl.when(cell != 0)
        def _():
            d_out[:, :, lanes] = dkv_s[:, :, lanes].astype(BF)
            for c in kv_mate[head] + kv_here[head]:
                c.start()

    sum_x(0)
    up, dn = z_step(2, up, dn)
    sum_x(1)
    finish(0)
    up, dn = z_step(3, up, dn)
    sum_z(0)
    sum_z(1)
    finish(1)
    up, dn = z_step(4, up, dn)

    @pl.when(cell == 0)
    def _():
        for head in range(2):
            lanes = slice(128 * head, 128 * (head + 1))
            for c in root[head]:
                c.wait_recv()
            for n in range(2):
                total = dkv_s[n, 0:BLK, lanes] + d0_s[head, n].astype(F32)
                for m in range(4):
                    total = total + d0_z0[head, m, n].astype(F32)
                dkv_s[n, 0:BLK, lanes] = total
            d_out[:, :, lanes] = dkv_s[:, :, lanes].astype(BF)
            for c in kv_mate[head] + kv_here[head]:
                c.start()

    for c in a2m + a2n:
        c.wait_recv()
    add(at_o, at_sum.at[y], at_r2.at[0], at_r2.at[1])
    locals_out.append(here_now(at_o, o_at))

    up.wait_recv()
    dn.wait_recv()
    add(wg_x.at[z], wg_x.at[z], wz_r.at[0, 3], wz_r.at[1, 3])
    w_out[...] = wg_x[z].T
    w_last = go(w_out.at[rows(64 * (1 - ylo), 64), :], o_wg.at[:, mine], mate)
    locals_out.append(here_now(w_out.at[rows(64 * ylo, 64), :], o_wg.at[:, mine]))

    for c in kv_mate[0] + kv_mate[1] + q_out + [w_last]:
        c.wait_recv()
    for c in locals_out + kv_here[0] + kv_here[1]:
        c.wait()
    for c in ends + kv_mate[0] + kv_mate[1]:
        c.wait_send()

    @pl.when(cell == 0)
    def _():
        for pair in tree:
            for c in pair:
                c.wait_send()

    @pl.when(x == 0)
    def _():
        for c in along_x:
            c.wait_send()

        @pl.when((z == 1) | (z == 3) | (z == 7))
        def _():
            leaf.wait_send()

        @pl.when((z == 2) | (z == 4) | (z == 6))
        def _():
            for c in stem:
                c.wait_send()

        for n in range(4):

            @pl.when(z == 2 * n + 1)
            def _():
                for a in range(2):
                    root[a][n].wait_send()

    for d in range(1, NX):

        @pl.when(x == d)
        def _():
            for a in range(2):
                to_x0[a][d - 1].wait_send()


def hand_over_kernel(*refs):
    n = 5
    ins, outs, bufs, sem = refs[:n], refs[n : 2 * n], refs[2 * n : 3 * n], refs[3 * n]
    reads = [pltpu.make_async_copy(ins[i], bufs[i], sem.at[0, i]) for i in range(n)]
    writes = [pltpu.make_async_copy(bufs[i], outs[i], sem.at[1, i]) for i in range(n)]
    for c in reads:
        c.start()
    for i in range(n):
        reads[i].wait()
        writes[i].start()
    for c in writes:
        c.wait()


def anywhere(n):
    return [pl.BlockSpec(memory_space=pl.ANY)] * n


def local(queries, key_heads, value_heads, out_weight, block_lists, out_grad):
    results = (
        jax.ShapeDtypeStruct((256, 1024), BF),
        jax.ShapeDtypeStruct((256, 512), BF),
        jax.ShapeDtypeStruct((256, 512), BF),
        jax.ShapeDtypeStruct((256, 512), BF),
        jax.ShapeDtypeStruct((64, 512), F32),
    )
    b, f = (lambda *s: pltpu.VMEM(s, BF)), (lambda *s: pltpu.VMEM(s, F32))
    scratch = [
        pltpu.SMEM((128, 3), jnp.int32),
        b(512, 256),
        b(1536, 256),
        b(1536, 256),
        b(2, 128, 256),
        b(NX, NZ, 128, 256),
        b(2, 4, 256, 1024),
        b(2, 4, 256, 1024),
        b(4, 8, 256, 128),
        f(8, 128, 1280),
        b(512, 256),
        b(512, 256),
        f(1536, 256),
        f(1536, 256),
        f(2, 128, 256),
        b(512, 256),
        b(4, 256, 1024),
        b(4, 256, 1024),
        b(2, 128, 1024),
        b(2, 256, 1024),
        b(256, 1024),
        b(2, 4, 256, 128),
        b(2, 4, 256, 128),
        b(2, 8, 256, 128),
        f(8, 256, 128),
        b(2, 4, 256, 128),
        b(2, 4, 256, 128),
        f(128, 256),
        b(2, 2, 2, 512, 128),
        b(2, 2, 2, 512, 128),
        b(2, 2, 128, 128),
        b(2, 3, 2, 128, 128),
        b(2, 2, 128, 128),
        b(2, 2, 128, 128),
        b(2, 2, 128, 128),
        b(2, 4, 2, 128, 128),
        f(2, 512, 256),
        b(2, 512, 256),
        pltpu.SemaphoreType.DMA((N_COPIES,)),
        pltpu.SemaphoreType.DMA((N_COPIES,)),
        pltpu.SemaphoreType.DMA((24,)),
    ]
    outs = pl.pallas_call(
        layer_kernel,
        out_shape=results,
        in_specs=anywhere(6),
        out_specs=tuple(anywhere(5)),
        scratch_shapes=scratch,
        compiler_params=pltpu.CompilerParams(
            collective_id=0, has_side_effects=True, vmem_limit_bytes=60 * 1024 * 1024
        ),
        name="layer",
    )(queries, key_heads, value_heads, out_weight, block_lists, out_grad)
    return pl.pallas_call(
        hand_over_kernel,
        out_shape=results,
        in_specs=anywhere(5),
        out_specs=tuple(anywhere(5)),
        scratch_shapes=[pltpu.VMEM(r.shape, r.dtype) for r in results]
        + [pltpu.SemaphoreType.DMA((2, 5))],
        name="hand_over",
    )(*outs)


def solution(mesh):
    placed = P("ctx", "head")
    return jax.shard_map(
        local,
        mesh=mesh,
        in_specs=(placed, placed, placed, placed, P(), placed),
        out_specs=(placed,) * 5,
        check_vma=False,
    )
```

```python
import jax
import jax.numpy as jnp
from jax import lax
from jax.experimental import pallas as pl
from jax.experimental.pallas import tpu as pltpu
from jax.sharding import PartitionSpec as P

HD = 128
BLK = 128
SCALE = HD ** -0.5
BF = jnp.bfloat16
F32 = jnp.float32
NX, NZ, NY = 4, 8, 4
N_COPIES = 240


def place():
    i = lax.axis_index("ctx")
    h = lax.axis_index("head")
    cell = i // 2
    return cell // NZ, cell % NZ, (h // 2) * 2 + i % 2, h % 2, cell


def device(x, z, y, core):
    return ((x * NZ + z) * 2 + y % 2, (y // 2) * 2 + core)


def rows(start, size):
    return pl.ds(pl.multiple_of(start, size), size)


class Copies:
    def __init__(self, send, recv):
        self.send, self.recv, self.count = send, recv, 0

    def make(self, src, dst, target):
        k = self.count
        self.count += 1
        return pltpu.make_async_remote_copy(
            src_ref=src,
            dst_ref=dst,
            send_sem=self.send.at[k],
            recv_sem=self.recv.at[k],
            device_id=target,
            device_id_type=pl.DeviceIdType.MESH,
        )

    def start(self, src, dst, target):
        c = self.make(src, dst, target)
        c.start()
        return c


def greet(peers):
    barrier = pltpu.get_barrier_semaphore()
    for peer in peers:
        pl.semaphore_signal(
            barrier, inc=1, device_id=peer, device_id_type=pl.DeviceIdType.MESH
        )
    pl.semaphore_wait(barrier, len(peers))


def all_peers(x, z, y, core, cell):
    up, down = (cell + 1) % (NX * NZ), (cell + NX * NZ - 1) % (NX * NZ)
    peers = [device((x + d) % NX, z, y, core) for d in range(1, NX)]
    peers += [device(x, (z + d) % NZ, y, core) for d in range(1, NZ)]
    peers += [device(x, z, (y + d) % NY, core) for d in (1, NY - 1)]
    peers += [device(x, z, y, 1 - core)]
    peers += [device(c // NZ, c % NZ, y, core) for c in (up, down)]
    return peers


def dot(a, b, dims=(((1,), (0,)), ((), ()))):
    return lax.dot_general(a, b, dims, preferred_element_type=F32)


NT = (((1,), (1,)), ((), ()))
TN = (((0,), (0,)), ((), ()))


def add(dst, *srcs):
    n, lanes = dst.shape
    step = min(n, 16384 // lanes)

    def body(i, carry):
        r = rows(step * i, step)
        total = srcs[0][r, :].astype(F32)
        for s in srcs[1:]:
            total = total + s[r, :].astype(F32)
        dst[r, :] = total.astype(dst.dtype)
        return carry

    lax.fori_loop(0, n // step, body, 0)


def layer_kernel(
    q, k, v, w, lists_hbm, og,
    o_at, o_dq, o_dk, o_dv, o_wg,
    lists, q2, kb, vb, b0, wf, ogf, at, wg, probs, mixed, mgrad, dk, dv, d0, dq,
    at_core, at_sum, at_r1, at_r2, at_o, wg_r1, wg_s, wg_r2, wg_x, wz_s, wz_r, w_out,
    dke, dk_r, d0_b, d0_xr, d0_s, d0_zr, d0_t, d0_q, dkv_s, d_out, send, recv, lsem,
):
    x, z, y, core, cell = place()
    ylo = y % 2
    h = (y // 2) * 2 + core
    x_up, x_dn, x_far = (x + 1) % NX, (x + NX - 1) % NX, (x + 2) % NX
    z_up, z_dn = (z + 1) % NZ, (z + NZ - 1) % NZ
    c_up, c_dn = (cell + 1) % (NX * NZ), (cell + NX * NZ - 1) % (NX * NZ)
    y_mate = y + 1 - 2 * ylo
    y_next = (y + NY - 1 + 2 * ylo) % NY
    y_far = (y + 2) % NY
    mate, nxt = device(x, z, y_mate, core), device(x, z, y_next, core)
    twin = device(x, z, y, 1 - core)
    xu, xd = device(x_up, z, y, core), device(x_dn, z, y, core)
    zu, zd = device(x, z_up, y, core), device(x, z_dn, y, core)
    cu, cd = device(c_up // NZ, c_up % NZ, y, core), device(c_dn // NZ, c_dn % NZ, y, core)
    net = Copies(send, recv)
    mine, other = rows(256 * ylo, 256), rows(256 * (1 - ylo), 256)
    band_mine, band_other = rows(512 + 256 * ylo, 256), rows(512 + 256 * (1 - ylo), 256)
    lo_mine, lo_other = mine, other
    hi_mine, hi_other = rows(1024 + 256 * ylo, 256), rows(1024 + 256 * (1 - ylo), 256)
    ends, n_local = [], [0]

    def go(src, dst, target):
        c = net.start(src, dst, target)
        ends.append(c)
        return c

    def here(src, dst):
        c = pltpu.make_async_copy(src, dst, lsem.at[n_local[0]])
        n_local[0] += 1
        return c

    def here_now(src, dst):
        c = here(src, dst)
        c.start()
        return c

    w_loc = here_now(w.at[:, mine], wf.at[x, z, rows(64 * ylo, 64), :])
    k_loc = here_now(k.at[:, mine], kb.at[band_mine, :])
    v_loc = here_now(v.at[:, mine], vb.at[band_mine, :])
    og_loc = here_now(og, ogf.at[ylo, h])
    q_loc = here_now(q.at[:, mine], q2.at[mine, :])
    list_loc = here_now(lists_hbm, lists)
    greet(all_peers(x, z, y, core, cell))

    quarter = rows(64 * x, 64)
    b_mate = [
        net.make(k.at[0:BLK, other], b0.at[0:BLK, :], mate),
        net.make(v.at[0:BLK, other], b0.at[BLK : 2 * BLK, :], mate),
    ]
    b_loc = [
        here(k.at[0:BLK, mine], b0.at[0:BLK, :]),
        here(v.at[0:BLK, mine], b0.at[BLK : 2 * BLK, :]),
    ]
    b_to_x = [
        net.make(
            b0.at[rows(64 * ((x + d) % NX), 64), :],
            b0.at[rows(64 * ((x + d) % NX), 64), :],
            device((x + d) % NX, z, y, core),
        )
        for d in range(1, NX)
    ]
    b_along_z = [
        net.make(b0.at[quarter, :], b0.at[quarter, :], device(x, (z + d) % NZ, y, core))
        for d in range(1, NZ)
    ]

    @pl.when((cell == 0) & (ylo == 0))
    def _():
        for c in b_mate + b_loc:
            c.start()

    w_mate = go(w.at[:, other], wf.at[x, z, rows(64 * ylo, 64), :], mate)
    k_mate = go(k.at[:, other], kb.at[band_mine, :], mate)
    v_mate = go(v.at[:, other], vb.at[band_mine, :], mate)
    og_next = go(og, ogf.at[ylo, h], nxt)
    half, cut = 112, 224
    og_here = ogf.at[ylo, h]
    og_mate = [go(og.at[0:half, :], og_here.at[0:half, :], mate)]
    q_mate = go(q.at[:, other], q2.at[mine, :], mate)
    og_mate.append(go(og.at[half:256, :], og_here.at[half:256, :], mate))
    og_tw = [go(og, og_here, twin)]

    own_half, mate_half = rows(64 * ylo, 64), rows(64 * (1 - ylo), 64)
    first = [go(w.at[:, mine], wf.at[x, z, own_half, :], t) for t in (zu, zd, xu, xd)]
    halo = [
        go(k.at[:, mine], kb.at[lo_mine, :], cu),
        go(k.at[:, mine], kb.at[hi_mine, :], cd),
    ]
    w_mate.wait_recv()
    w_loc.wait()

    x_plus, x_minus, x_fwd = {}, {}, []

    def to_x(off):
        zz = (z + off) % NZ
        x_plus[off] = go(wf.at[x, zz], wf.at[x, zz], xu)
        x_minus[off] = go(wf.at[x, zz], wf.at[x, zz], xd)

    def either(cond, fn, then, other):
        @pl.when(cond)
        def _():
            fn(then)

        @pl.when(jnp.logical_not(cond))
        def _():
            fn(other)

    def goes_up(is_up):
        return (z == 7) | (z != 0) if is_up else z == 7

    def pass_x(off):
        zz = (z + off) % NZ
        if off == 0:
            first[2].wait_recv()
            first[3].wait_recv()
        x_plus[off].wait_recv()
        x_minus[off].wait_recv()
        pair = (
            goes_up(off in (0, 6, 2, 4)),
            net.make(wf.at[x_dn, zz], wf.at[x_dn, zz], xu),
            net.make(wf.at[x_up, zz], wf.at[x_up, zz], xd),
        )
        either(pair[0], lambda c: c.start(), pair[1], pair[2])
        x_fwd.append(pair)

    def ring_step(s, up, dn):
        zm, zp = (z + NZ - s) % NZ, (z + s) % NZ
        if s == 1:
            first[0].wait_recv()
            first[1].wait_recv()
        up.wait_recv()
        if s < 3:
            up = go(wf.at[x, zm], wf.at[x, zm], zu)
        else:
            up = go(wf.at[x, zm, 0:64, :], wf.at[x, zm, 0:64, :], zu)
        to_x(NZ - s)
        dn.wait_recv()
        if s < 3:
            dn = go(wf.at[x, zp], wf.at[x, zp], zd)
        else:
            dn = go(wf.at[x, zp, 64:128, :], wf.at[x, zp, 64:128, :], zd)
        to_x(s)
        return up, dn

    second = wf.at[x, z, mate_half, :]
    up = go(second, second, zu)
    dn = go(second, second, zd)
    x_plus[0] = go(second, second, xu)
    x_minus[0] = go(second, second, xd)

    @pl.when(cell == 0)
    def _():
        @pl.when(ylo == 0)
        def _():
            for c in b_loc:
                c.wait()

        @pl.when(ylo == 1)
        def _():
            for c in b_mate:
                c.wait_recv()

        for c in b_to_x:
            c.start()

    up, dn = ring_step(1, up, dn)
    halo += [
        go(v.at[:, mine], vb.at[lo_mine, :], cu),
        go(v.at[:, mine], vb.at[hi_mine, :], cd),
    ]

    @pl.when(z == 0)
    def _():
        for d in range(1, NX):

            @pl.when(x == d)
            def _():
                b_to_x[d - 1].wait_recv()

        for n in (3, 4, 2, 5, 1, 6, 0):
            b_along_z[n].start()

    k_mate.wait_recv()
    k_loc.wait()
    up, dn = ring_step(2, up, dn)
    halo += [
        go(kb.at[band_other, :], kb.at[lo_other, :], cu),
        go(kb.at[band_other, :], kb.at[hi_other, :], cd),
    ]
    pass_x(0)
    v_mate.wait_recv()
    v_loc.wait()
    up, dn = ring_step(3, up, dn)
    halo += [
        go(vb.at[band_other, :], vb.at[lo_other, :], cu),
        go(vb.at[band_other, :], vb.at[hi_other, :], cd),
    ]
    for d in range(1, NZ):

        @pl.when(z == d)
        def _():
            b_along_z[d - 1].wait_recv()

    b_along_x = [
        net.make(b0.at[quarter, :], b0.at[quarter, :], device((x + d) % NX, z, y, core))
        for d in range(1, NX)
    ]

    def to_x_peers(fn):
        for d in range(1, NX):

            @pl.when((z != 0) | ((x + d) % NX != 0))
            def _():
                fn(b_along_x[d - 1])

    to_x_peers(lambda c: c.start())

    from_mate = ogf.at[y_mate % 2, (y_mate // 2) * 2 + core]
    from_next = ogf.at[y_next % 2, (y_next // 2) * 2 + core]
    far = ogf.at[y_far % 2, (y_far // 2) * 2 + core]
    og_mate[0].wait_recv()
    fwd_next = [go(from_mate.at[0:half, :], from_mate.at[0:half, :], nxt)]
    og_tw.append(go(from_mate.at[0:half, :], from_mate.at[0:half, :], twin))
    og_next.wait_recv()
    fwd_mate = go(from_next.at[cut:256, :], from_next.at[cut:256, :], mate)
    og_tw.append(go(from_next, from_next, twin))
    pass_x(7)
    pass_x(1)
    up.wait_recv()
    dn.wait_recv()
    to_x(4)
    pass_x(6)
    pass_x(2)
    q_mate.wait_recv()
    q_loc.wait()
    list_loc.wait()

    @pl.when(cell != 0)
    def _():
        for d in range(1, NX):
            b_along_x[d - 1].wait_recv()

    for c in halo:
        c.wait_recv()

    def window(n):
        i, head = n % 4, n // 4
        return i, head, rows(128 * i, 128), pl.ds(pl.multiple_of(128 * i, 128), 1152), rows(128 * head, 128)

    def forward(n, carry):
        i, head, toks, win, lanes = window(n)
        b = 4 * cell + i
        bias = []
        for j in range(9):
            kbl = b - 4 + j
            good = (kbl >= 1) & (kbl <= 127)
            if j not in (3, 4, 5):
                named = (lists[0, b] == kbl) | (lists[1, b] == kbl) | (lists[2, b] == kbl)
                good = good & named
            bias.append(jnp.full((1, BLK), jnp.where(good, 0.0, -jnp.inf), F32))
        bias = jnp.concatenate(bias, axis=1)
        qq = q2[toks, lanes]
        s0 = dot(qq, b0[0:BLK, lanes], NT) * SCALE
        s1 = dot(qq, kb[win, lanes], NT) * SCALE + bias
        top = jnp.maximum(jnp.max(s0, axis=1, keepdims=True), jnp.max(s1, axis=1, keepdims=True))
        e0, e1 = jnp.exp(s0 - top), jnp.exp(s1 - top)
        inv = 1.0 / (jnp.sum(e0, axis=1, keepdims=True) + jnp.sum(e1, axis=1, keepdims=True))
        p0, p1 = e0 * inv, e1 * inv
        probs[n, :, 0:BLK] = p0
        probs[n, :, BLK:] = p1
        out = dot(p0.astype(BF), b0[BLK : 2 * BLK, lanes]) + dot(p1.astype(BF), vb[win, lanes])
        mixed[toks, lanes] = out.astype(BF)
        return carry

    og_mate[1].wait_recv()
    fwd_next.append(go(from_mate.at[half:cut, :], from_mate.at[half:cut, :], nxt))
    og_tw.append(go(from_mate.at[half:256, :], from_mate.at[half:256, :], twin))
    lax.fori_loop(0, 2, forward, 0)
    pass_x(5)
    pass_x(3)
    lax.fori_loop(2, 4, forward, 0)
    pass_x(4)
    lax.fori_loop(4, 5, forward, 0)
    fwd_mate.wait_recv()
    og_tw.append(go(far.at[cut:256, :], far.at[cut:256, :], twin))
    fwd_next[0].wait_recv()
    og_tw.append(go(far.at[0:half, :], far.at[0:half, :], twin))
    lax.fori_loop(5, 8, forward, 0)
    fwd_next[1].wait_recv()
    og_tw.append(go(far.at[half:cut, :], far.at[half:cut, :], twin))
    og_loc.wait()
    for c in og_tw:
        c.wait_recv()

    def weight_part(xx):
        total = dot(mixed[0:256, :], ogf[0, xx], TN) + dot(mixed[256:512, :], ogf[1, xx], TN)
        for n in range(8):
            wg[xx, n] = total[:, 128 * n : 128 * (n + 1)].astype(BF)

    def attended_part(t, c):
        hh = (t // 2) * 2 + c
        part = dot(mixed[rows(256 * (t % 2), 256), :], wf[hh].reshape(1024, 256), NT)
        at[t % 2, hh] = part.astype(BF)

    w1, w2u, w2d = {}, {}, {}

    def piece(xx, off):
        return wg.at[xx, (z + off) % NZ]

    def straight(off):
        if off < 4:
            w2u[off] = go(piece(x_up, off), wg_r2.at[0, off], xu)
        else:
            w2d[off] = go(piece(x_dn, off), wg_r2.at[1, off], xd)

    def relay(off):
        w1[off].wait_recv()
        if off >= 4:
            add(wg_s.at[off], piece(x_up, off), wg_r1.at[off])
            w2u[off] = go(wg_s.at[off], wg_r2.at[0, off], xu)
        else:
            add(wg_s.at[off], piece(x_dn, off), wg_r1.at[off])
            w2d[off] = go(wg_s.at[off], wg_r2.at[1, off], xd)

    weight_part(x_far)
    for off in (4, 3, 5, 2, 6, 1, 7, 0):
        w1[off] = go(piece(x_far, off), wg_r1.at[off], xu if off >= 4 else xd)
    for pair in x_fwd:
        either(pair[0], lambda c: c.wait_recv(), pair[1], pair[2])
    order = (y_far, y_mate, y_next, y)
    cores = []
    for t in order:
        attended_part(t, 1 - core)
        cores.append(go(at.at[t % 2, (t // 2) * 2 + 1 - core], at_core.at[t], twin))
    weight_part(x_up)
    weight_part(x_dn)
    for off in (4, 3, 5, 2):
        straight(off)
    for t in order:
        attended_part(t, core)
    weight_part(x)
    for t in range(2):
        total = jnp.zeros((256, 256), F32)
        for hh in range(4):
            total = total + dot(ogf[t, hh], wf[hh].reshape(1024, 256))
        mgrad[256 * t : 256 * (t + 1), :] = total.astype(BF)
    dk[...] = jnp.zeros_like(dk)
    dv[...] = jnp.zeros_like(dv)
    d0[...] = jnp.zeros_like(d0)
    for off in (4, 3, 5, 2):
        relay(off)
    for off in (6, 1, 7, 0):
        straight(off)

    for n, t in enumerate(order):
        cores[n].wait_recv()
        add(at_sum.at[t], at.at[t % 2, (t // 2) * 2 + core], at_core.at[t])
        if n == 0:
            a1n = go(at_sum.at[t, 0:128, :], at_r1.at[0], nxt)
            a1m = go(at_sum.at[t, 128:256, :], at_r1.at[1], mate)
        if n == 1:
            a2m = [go(at_sum.at[t, 128:256, :], at_r2.at[0, 128:256, :], mate)]
        if n == 2:
            a2n = [go(at_sum.at[t, 0:128, :], at_r2.at[1, 0:128, :], nxt)]

    def backward(n, carry):
        i, head, toks, win, lanes = window(n)
        g = mgrad[toks, lanes]
        delta = jnp.sum(
            g.astype(F32) * mixed[toks, lanes].astype(F32), axis=1, keepdims=True
        )
        p0, p1 = probs[n, :, 0:BLK], probs[n, :, BLK:]
        sl0 = (p0 * (dot(g, b0[BLK : 2 * BLK, lanes], NT) - delta)).astype(BF)
        sl1 = (p1 * (dot(g, vb[win, lanes], NT) - delta)).astype(BF)
        out = dot(sl0, b0[0:BLK, lanes]) + dot(sl1, kb[win, lanes])
        dq[toks, lanes] = (out * SCALE).astype(BF)
        qq = q2[toks, lanes]
        dk[win, lanes] += dot(sl1, qq, TN)
        dv[win, lanes] += dot(p1.astype(BF), g, TN)
        d0[0, :, lanes] += dot(sl0, qq, TN)
        d0[1, :, lanes] += dot(p0.astype(BF), g, TN)
        return carry

    edges, q_out, locals_out = [[], []], [], []

    def leave(head, n):
        acc, factor = ((dk, SCALE), (dv, 1.0))[n]
        lanes = slice(128 * head, 128 * (head + 1))
        dke[head, n, 0] = (acc[0:512, lanes] * factor).astype(BF)
        dke[head, n, 1] = (acc[1024:1536, lanes] * factor).astype(BF)
        edges[head] += [
            go(dke.at[head, n, 0], dk_r.at[head, n, 1], cd),
            go(dke.at[head, n, 1], dk_r.at[head, n, 0], cu),
        ]

    def leave_q(head):
        lanes = slice(128 * head, 128 * (head + 1))
        cols = rows(256 * ylo + 128 * head, 128)
        q_out.append(go(dq.at[other, lanes], o_dq.at[:, cols], mate))
        locals_out.append(here_now(dq.at[mine, lanes], o_dq.at[:, cols]))

    def sum_x(off):
        w2u[off].wait_recv()
        w2d[off].wait_recv()
        add(wg_x.at[off], piece(x, off), wg_r2.at[0, off], wg_r2.at[1, off])

    def z_step(s, up, dn):
        tu, td = 5 - s, 3 + s
        up.wait_recv()
        if s == 2:
            add(wz_s.at[0, 1, 0:128, :], wg_x.at[tu, 0:128, :], wz_r.at[0, 0, 0:128, :])
            add(wz_s.at[0, 1, 128:256, :], wg_x.at[tu, 128:256, :])
        else:
            add(wz_s.at[0, s - 1], wg_x.at[tu], wz_r.at[0, s - 2])
        up = go(wz_s.at[0, s - 1], wz_r.at[0, s - 1], zu)
        dn.wait_recv()
        if s == 2:
            add(wz_s.at[1, 1, 128:256, :], wg_x.at[td, 128:256, :], wz_r.at[1, 0, 128:256, :])
            add(wz_s.at[1, 1, 0:128, :], wg_x.at[td, 0:128, :])
        else:
            add(wz_s.at[1, s - 1], wg_x.at[td], wz_r.at[1, s - 2])
        dn = go(wz_s.at[1, s - 1], wz_r.at[1, s - 1], zd)
        return up, dn

    lax.fori_loop(0, 4, backward, 0)
    for off in (6, 1, 7, 0):
        relay(off)
    leave(0, 0)
    leave_q(0)
    lax.fori_loop(4, 8, backward, 0)

    d0_b[0:BLK, :] = (d0[0] * SCALE).astype(BF)
    d0_b[BLK : 2 * BLK, :] = d0[1].astype(BF)
    d0_x = [
        go(
            d0_b.at[rows(64 * ((x + d) % NX), 64), :],
            d0_xr.at[d - 1],
            device((x + d) % NX, z, y, core),
        )
        for d in range(1, NX)
    ]
    d0_z = [net.make(d0_s, d0_zr.at[d - 1], device(x, 0, y, core)) for d in range(1, NZ)]
    d0_o = [net.make(d0_t, d0_q.at[d - 1], device(0, z, y, core)) for d in range(1, NX)]

    sum_x(4)
    add(wz_s.at[0, 0, 0:128, :], wg_x.at[4, 0:128, :])
    up = go(wz_s.at[0, 0, 0:128, :], wz_r.at[0, 0, 0:128, :], zu)
    add(wz_s.at[1, 0, 128:256, :], wg_x.at[4, 128:256, :])
    dn = go(wz_s.at[1, 0, 128:256, :], wz_r.at[1, 0, 128:256, :], zd)
    leave(0, 1)
    leave_q(1)
    sum_x(3)
    sum_x(5)
    up, dn = z_step(2, up, dn)
    leave(1, 0)

    a1n.wait_recv()
    to_mate = at_core.at[0, 0:128, :]
    add(to_mate, at_sum.at[y_mate, 0:128, :], at_r1.at[0])
    a2m.append(go(to_mate, at_r2.at[0, 0:128, :], mate))
    a1m.wait_recv()
    to_next = at_core.at[1, 128:256, :]
    add(to_next, at_sum.at[y_next, 128:256, :], at_r1.at[1])
    a2n.append(go(to_next, at_r2.at[1, 128:256, :], nxt))

    sum_x(2)
    sum_x(6)
    up, dn = z_step(3, up, dn)
    leave(1, 1)

    for c in d0_x:
        c.wait_recv()
    add(d0_s, d0_b.at[quarter, :], *[d0_xr.at[d] for d in range(3)])
    for d in range(1, NZ):

        @pl.when(z == d)
        def _():
            d0_z[d - 1].start()

    kv_mate, kv_here = [[], []], [[], []]

    def finish(head):
        for c in edges[head]:
            c.wait_recv()
        lanes = slice(128 * head, 128 * (head + 1))
        cols = rows(256 * ylo + 128 * head, 128)
        for n, (acc, factor) in enumerate(((dk, SCALE), (dv, 1.0))):
            dkv_s[n, :, lanes] = (
                acc[512:1024, lanes] * factor
                + dk_r[head, n, 0].astype(F32)
                + dk_r[head, n, 1].astype(F32)
            )
            out = (o_dk, o_dv)[n]
            for r in (0, BLK):
                src = d_out.at[n, rows(256 * (1 - ylo) + r, BLK), lanes]
                kv_mate[head].append(net.make(src, out.at[r : r + BLK, cols], mate))
            kv_here[head].append(here(d_out.at[n, mine, lanes], out.at[:, cols]))

        d_out[:, :, lanes] = dkv_s[:, :, lanes].astype(BF)
        for m, c in enumerate(kv_mate[head]):
            if m % 2 == 1:
                c.start()
            else:
                pl.when((cell != 0) | (ylo == 0))(c.start)
        for c in kv_here[head]:
            pl.when(cell != 0)(c.start)

    finish(0)
    sum_x(1)
    sum_x(7)
    up, dn = z_step(4, up, dn)

    @pl.when(z == 0)
    def _():
        for c in d0_z:
            c.wait_recv()
        add(d0_t, d0_s, *[d0_zr.at[d] for d in range(NZ - 1)])
        for d in range(1, NX):

            @pl.when(x == d)
            def _():
                d0_o[d - 1].start()

    finish(1)
    sum_x(0)
    up.wait_recv()
    dn.wait_recv()
    add(wg_x.at[0], wg_x.at[0], wz_r.at[0, 3], wz_r.at[1, 3])
    w_out[...] = wg_x[0].T
    w_last = go(w_out.at[rows(64 * (1 - ylo), 64), :], o_wg.at[:, mine], mate)
    locals_out.append(here_now(w_out.at[rows(64 * ylo, 64), :], o_wg.at[:, mine]))

    @pl.when(cell == 0)
    def _():
        for c in d0_o:
            c.wait_recv()
        for m in range(4):
            part = d0_t[...] if m == 0 else d0_q[m - 1]
            dkv_s[m // 2, 64 * (m % 2) : 64 * (m % 2) + 64, :] += part.astype(F32)
        d_out[:, 0:BLK, :] = dkv_s[:, 0:BLK, :].astype(BF)

        @pl.when(ylo == 1)
        def _():
            for head in range(2):
                for c in kv_mate[head][0::2]:
                    c.start()

        for c in kv_here[0] + kv_here[1]:
            c.start()

    for c in a2m + a2n:
        c.wait_recv()
    add(at_o, at_sum.at[y], at_r2.at[0], at_r2.at[1])
    locals_out.append(here_now(at_o, o_at))

    for c in kv_mate[0] + kv_mate[1] + q_out + [w_last]:
        c.wait_recv()
    for c in locals_out + kv_here[0] + kv_here[1]:
        c.wait()
    for c in ends + kv_mate[0] + kv_mate[1]:
        c.wait_send()
    for pair in x_fwd:
        either(pair[0], lambda c: c.wait_send(), pair[1], pair[2])

    @pl.when(cell == 0)
    def _():
        @pl.when(ylo == 0)
        def _():
            for c in b_mate:
                c.wait_send()

        for c in b_to_x:
            c.wait_send()

    to_x_peers(lambda c: c.wait_send())

    @pl.when(z == 0)
    def _():
        for c in b_along_z:
            c.wait_send()

        for d in range(1, NX):

            @pl.when(x == d)
            def _():
                d0_o[d - 1].wait_send()

    for d in range(1, NZ):

        @pl.when(z == d)
        def _():
            d0_z[d - 1].wait_send()


def hand_over_kernel(*refs):
    n = 5
    ins, outs, bufs, sem = refs[:n], refs[n : 2 * n], refs[2 * n : 3 * n], refs[3 * n]
    reads = [pltpu.make_async_copy(ins[i], bufs[i], sem.at[0, i]) for i in range(n)]
    writes = [pltpu.make_async_copy(bufs[i], outs[i], sem.at[1, i]) for i in range(n)]
    for c in reads:
        c.start()
    for i in range(n):
        reads[i].wait()
        writes[i].start()
    for c in writes:
        c.wait()


def anywhere(n):
    return [pl.BlockSpec(memory_space=pl.ANY)] * n


def local(queries, key_heads, value_heads, out_weight, block_lists, out_grad):
    results = (
        jax.ShapeDtypeStruct((256, 1024), BF),
        jax.ShapeDtypeStruct((256, 512), BF),
        jax.ShapeDtypeStruct((256, 512), BF),
        jax.ShapeDtypeStruct((256, 512), BF),
        jax.ShapeDtypeStruct((64, 512), F32),
    )
    b, f = (lambda *s: pltpu.VMEM(s, BF)), (lambda *s: pltpu.VMEM(s, F32))
    scratch = [
        pltpu.SMEM((3, 128), jnp.int32),
        b(512, 256),
        b(1536, 256),
        b(1536, 256),
        b(256, 256),
        b(NX, NZ, 128, 256),
        b(2, 4, 256, 1024),
        b(2, 4, 256, 1024),
        b(4, 8, 256, 128),
        f(8, 128, 1280),
        b(512, 256),
        b(512, 256),
        f(1536, 256),
        f(1536, 256),
        f(2, 128, 256),
        b(512, 256),
        b(4, 256, 1024),
        b(4, 256, 1024),
        b(2, 128, 1024),
        b(2, 256, 1024),
        b(256, 1024),
        b(8, 256, 128),
        b(8, 256, 128),
        b(2, 8, 256, 128),
        f(8, 256, 128),
        b(2, 4, 256, 128),
        b(2, 4, 256, 128),
        f(128, 256),
        b(2, 2, 2, 512, 128),
        b(2, 2, 2, 512, 128),
        b(256, 256),
        b(3, 64, 256),
        b(64, 256),
        b(7, 64, 256),
        b(64, 256),
        b(3, 64, 256),
        f(2, 512, 256),
        b(2, 512, 256),
        pltpu.SemaphoreType.DMA((N_COPIES,)),
        pltpu.SemaphoreType.DMA((N_COPIES,)),
        pltpu.SemaphoreType.DMA((24,)),
    ]
    outs = pl.pallas_call(
        layer_kernel,
        out_shape=results,
        in_specs=anywhere(6),
        out_specs=tuple(anywhere(5)),
        scratch_shapes=scratch,
        compiler_params=pltpu.CompilerParams(
            collective_id=0, has_side_effects=True, vmem_limit_bytes=60 * 1024 * 1024
        ),
        name="layer",
    )(queries, key_heads, value_heads, out_weight, block_lists.T, out_grad)
    return pl.pallas_call(
        hand_over_kernel,
        out_shape=results,
        in_specs=anywhere(5),
        out_specs=tuple(anywhere(5)),
        scratch_shapes=[pltpu.VMEM(r.shape, r.dtype) for r in results]
        + [pltpu.SemaphoreType.DMA((2, 5))],
        name="hand_over",
    )(*outs)


def solution(mesh):
    placed = P("ctx", "head")
    return jax.shard_map(
        local,
        mesh=mesh,
        in_specs=(placed, placed, placed, placed, P(), placed),
        out_specs=(placed,) * 5,
        check_vma=False,
    )
```

```python
import jax
import jax.numpy as jnp
from jax import lax
from jax.experimental import pallas as pl
from jax.experimental.pallas import tpu as pltpu
from jax.sharding import PartitionSpec as P

HD = 128
BLK = 128
SCALE = HD ** -0.5
BF = jnp.bfloat16
F32 = jnp.float32
NX, NZ, NY = 4, 8, 4
POOL = 40
COUNTS = N_SEND, N_RECV, N_LOCAL = 106, 150, 16


def place():
    i = lax.axis_index("ctx")
    h = lax.axis_index("head")
    cell = i // 2
    return cell // NZ, cell % NZ, (h // 2) * 2 + i % 2, h % 2, cell


def device(x, z, y, core):
    return ((x * NZ + z) * 2 + y % 2, (y // 2) * 2 + core)


def rows(start, size):
    return pl.ds(pl.multiple_of(start, size), size)


class Copies:
    def __init__(self, send, recv):
        self.send, self.recv = send, recv
        self.n_send, self.n_recv, self.live = POOL, 0, []

    def numbers(self):
        self.n_send += 1
        self.n_recv += 1
        return self.n_send - 1, self.n_recv - 1

    def make(self, src, dst, target, numbers=None):
        k_send, k_recv = numbers or self.numbers()
        return pltpu.make_async_remote_copy(
            src_ref=src,
            dst_ref=dst,
            send_sem=self.send.at[k_send],
            recv_sem=self.recv.at[k_recv],
            device_id=target,
            device_id_type=pl.DeviceIdType.MESH,
        )

    def start(self, src, dst, target):
        k_send = len(self.live)
        if k_send == POOL:
            k_send, oldest = self.live.pop(0)
            oldest.wait_send()
        self.n_recv += 1
        c = self.make(src, dst, target, (k_send, self.n_recv - 1))
        c.start()
        self.live.append((k_send, c))
        return c

    def drain(self):
        for _, c in self.live:
            c.wait_send()


def greet(peers):
    barrier = pltpu.get_barrier_semaphore()
    for peer in peers:
        pl.semaphore_signal(
            barrier, inc=1, device_id=peer, device_id_type=pl.DeviceIdType.MESH
        )
    pl.semaphore_wait(barrier, len(peers))


def all_peers(x, z, y, core, cell):
    up, down = (cell + 1) % (NX * NZ), (cell + NX * NZ - 1) % (NX * NZ)
    peers = [device((x + d) % NX, z, y, core) for d in range(1, NX)]
    peers += [device(x, (z + d) % NZ, y, core) for d in range(1, NZ)]
    peers += [device(x, z, (y + d) % NY, core) for d in (1, NY - 1)]
    peers += [device(x, z, y, 1 - core)]
    peers += [device(c // NZ, c % NZ, y, core) for c in (up, down)]
    return peers


def dot(a, b, dims=(((1,), (0,)), ((), ()))):
    return lax.dot_general(a, b, dims, preferred_element_type=F32)


NT = (((1,), (1,)), ((), ()))
TN = (((0,), (0,)), ((), ()))


def add(dst, *srcs):
    n, lanes = dst.shape
    step = min(n, 16384 // lanes)

    def body(i, carry):
        r = rows(step * i, step)
        total = srcs[0][r, :].astype(F32)
        for s in srcs[1:]:
            total = total + s[r, :].astype(F32)
        dst[r, :] = total.astype(dst.dtype)
        return carry

    lax.fori_loop(0, n // step, body, 0)


def layer_kernel(
    q, k, v, w, lists_hbm, og,
    o_at, o_dq, o_dk, o_dv, o_wg,
    lists, q2, kb, vb, b0, wf, ogf, at, wg, probs, mixed, mgrad, dk, dv, d0, dq,
    at_core, at_sum, at_r1, at_r2, at_o, wg_r1, wg_s, wg_r2, wg_x, wz_s, wz_r, w_out,
    dke, dk_r, d0_b, d0_xr, d0_s, d0_zr, d0_t, d0_q, dkv_s, d_out, send, recv, lsem,
):
    x, z, y, core, cell = place()
    ylo = y % 2
    h = (y // 2) * 2 + core
    x_up, x_dn, x_far = (x + 1) % NX, (x + NX - 1) % NX, (x + 2) % NX
    z_up, z_dn = (z + 1) % NZ, (z + NZ - 1) % NZ
    c_up, c_dn = (cell + 1) % (NX * NZ), (cell + NX * NZ - 1) % (NX * NZ)
    y_mate = y + 1 - 2 * ylo
    y_next = (y + NY - 1 + 2 * ylo) % NY
    y_far = (y + 2) % NY
    mate, nxt = device(x, z, y_mate, core), device(x, z, y_next, core)
    twin = device(x, z, y, 1 - core)
    xu, xd = device(x_up, z, y, core), device(x_dn, z, y, core)
    zu, zd = device(x, z_up, y, core), device(x, z_dn, y, core)
    cu, cd = device(c_up // NZ, c_up % NZ, y, core), device(c_dn // NZ, c_dn % NZ, y, core)
    net = Copies(send, recv)
    mine, other = rows(256 * ylo, 256), rows(256 * (1 - ylo), 256)
    band_mine, band_other = rows(512 + 256 * ylo, 256), rows(512 + 256 * (1 - ylo), 256)
    lo_mine, lo_other = mine, other
    hi_mine, hi_other = rows(1024 + 256 * ylo, 256), rows(1024 + 256 * (1 - ylo), 256)
    n_local = [0]

    def go(src, dst, target):
        return net.start(src, dst, target)

    def here(src, dst):
        c = pltpu.make_async_copy(src, dst, lsem.at[n_local[0]])
        n_local[0] += 1
        return c

    def here_now(src, dst):
        c = here(src, dst)
        c.start()
        return c

    w_loc = here_now(w.at[:, mine], wf.at[x, z, rows(64 * ylo, 64), :])
    k_loc = here_now(k.at[:, mine], kb.at[band_mine, :])
    v_loc = here_now(v.at[:, mine], vb.at[band_mine, :])
    og_loc = here_now(og, ogf.at[ylo, h])
    q_loc = here_now(q.at[:, mine], q2.at[mine, :])
    list_loc = here_now(lists_hbm, lists)
    greet(all_peers(x, z, y, core, cell))

    quarter = rows(64 * x, 64)
    b_mate = [
        net.make(k.at[0:BLK, other], b0.at[0:BLK, :], mate),
        net.make(v.at[0:BLK, other], b0.at[BLK : 2 * BLK, :], mate),
    ]
    b_loc = [
        here(k.at[0:BLK, mine], b0.at[0:BLK, :]),
        here(v.at[0:BLK, mine], b0.at[BLK : 2 * BLK, :]),
    ]
    b_to_x = [
        net.make(
            b0.at[rows(64 * ((x + d) % NX), 64), :],
            b0.at[rows(64 * ((x + d) % NX), 64), :],
            device((x + d) % NX, z, y, core),
        )
        for d in range(1, NX)
    ]
    b_along_z = [
        net.make(b0.at[quarter, :], b0.at[quarter, :], device(x, (z + d) % NZ, y, core))
        for d in range(1, NZ)
    ]

    @pl.when((cell == 0) & (ylo == 0))
    def _():
        for c in b_mate + b_loc:
            c.start()

    w_mate = go(w.at[:, other], wf.at[x, z, rows(64 * ylo, 64), :], mate)
    k_mate = go(k.at[:, other], kb.at[band_mine, :], mate)
    v_mate = go(v.at[:, other], vb.at[band_mine, :], mate)
    og_next = go(og, ogf.at[ylo, h], nxt)
    half, cut = 160, 208
    og_here = ogf.at[ylo, h]
    og_mate = [go(og.at[0:half, :], og_here.at[0:half, :], mate)]
    q_mate = go(q.at[:, other], q2.at[mine, :], mate)
    og_mate.append(go(og.at[half:256, :], og_here.at[half:256, :], mate))
    og_tw = [go(og, og_here, twin)]

    own_half, mate_half = rows(64 * ylo, 64), rows(64 * (1 - ylo), 64)
    first = [go(w.at[:, mine], wf.at[x, z, own_half, :], t) for t in (zu, zd, xu, xd)]
    halo = [
        go(k.at[:, mine], kb.at[lo_mine, :], cu),
        go(k.at[:, mine], kb.at[hi_mine, :], cd),
    ]
    w_mate.wait_recv()
    w_loc.wait()

    x_plus, x_minus, x_fwd = {}, {}, []

    def to_x(off):
        zz = (z + off) % NZ
        x_plus[off] = go(wf.at[x, zz], wf.at[x, zz], xu)
        x_minus[off] = go(wf.at[x, zz], wf.at[x, zz], xd)

    def either(cond, fn, then, other):
        @pl.when(cond)
        def _():
            fn(then)

        @pl.when(jnp.logical_not(cond))
        def _():
            fn(other)

    def goes_up(is_up):
        return (z == 7) | (z != 0) if is_up else z == 7

    def pass_x(off):
        zz = (z + off) % NZ
        if off == 0:
            first[2].wait_recv()
            first[3].wait_recv()
        x_plus[off].wait_recv()
        x_minus[off].wait_recv()
        ks = net.numbers()
        pair = (
            goes_up(off in (0, 6, 2, 4)),
            net.make(wf.at[x_dn, zz], wf.at[x_dn, zz], xu, ks),
            net.make(wf.at[x_up, zz], wf.at[x_up, zz], xd, ks),
        )
        either(pair[0], lambda c: c.start(), pair[1], pair[2])
        x_fwd.append(pair)

    def ring_step(s, up, dn):
        zm, zp = (z + NZ - s) % NZ, (z + s) % NZ
        if s == 1:
            first[0].wait_recv()
            first[1].wait_recv()
        up.wait_recv()
        if s < 3:
            up = go(wf.at[x, zm], wf.at[x, zm], zu)
        else:
            up = go(wf.at[x, zm, 0:64, :], wf.at[x, zm, 0:64, :], zu)
        to_x(NZ - s)
        dn.wait_recv()
        if s < 3:
            dn = go(wf.at[x, zp], wf.at[x, zp], zd)
        else:
            dn = go(wf.at[x, zp, 64:128, :], wf.at[x, zp, 64:128, :], zd)
        to_x(s)
        return up, dn

    second = wf.at[x, z, mate_half, :]
    up = go(second, second, zu)
    dn = go(second, second, zd)
    x_plus[0] = go(second, second, xu)
    x_minus[0] = go(second, second, xd)

    @pl.when(cell == 0)
    def _():
        @pl.when(ylo == 0)
        def _():
            for c in b_loc:
                c.wait()

        @pl.when(ylo == 1)
        def _():
            for c in b_mate:
                c.wait_recv()

        for c in b_to_x:
            c.start()

    up, dn = ring_step(1, up, dn)

    @pl.when(z == 0)
    def _():
        for d in range(1, NX):

            @pl.when(x == d)
            def _():
                b_to_x[d - 1].wait_recv()

        for n in (3, 4, 2, 5, 1, 6, 0):
            b_along_z[n].start()

    halo += [
        go(v.at[:, mine], vb.at[lo_mine, :], cu),
        go(v.at[:, mine], vb.at[hi_mine, :], cd),
    ]
    k_mate.wait_recv()
    k_loc.wait()
    up, dn = ring_step(2, up, dn)
    halo += [
        go(kb.at[band_other, :], kb.at[lo_other, :], cu),
        go(kb.at[band_other, :], kb.at[hi_other, :], cd),
    ]
    pass_x(0)
    for d in range(1, NZ):

        @pl.when(z == d)
        def _():
            b_along_z[d - 1].wait_recv()

    b_along_x = [
        net.make(b0.at[quarter, :], b0.at[quarter, :], device((x + d) % NX, z, y, core))
        for d in range(1, NX)
    ]

    def to_x_peers(fn):
        for d in range(1, NX):

            @pl.when((z != 0) | ((x + d) % NX != 0))
            def _():
                fn(b_along_x[d - 1])

    to_x_peers(lambda c: c.start())

    v_mate.wait_recv()
    v_loc.wait()
    up, dn = ring_step(3, up, dn)
    halo += [
        go(vb.at[band_other, :], vb.at[lo_other, :], cu),
        go(vb.at[band_other, :], vb.at[hi_other, :], cd),
    ]
    from_mate = ogf.at[y_mate % 2, (y_mate // 2) * 2 + core]
    from_next = ogf.at[y_next % 2, (y_next // 2) * 2 + core]
    far = ogf.at[y_far % 2, (y_far // 2) * 2 + core]
    og_mate[0].wait_recv()
    fwd_next = [go(from_mate.at[0:half, :], from_mate.at[0:half, :], nxt)]
    og_tw.append(go(from_mate.at[0:half, :], from_mate.at[0:half, :], twin))
    og_next.wait_recv()
    fwd_mate = go(from_next.at[cut:256, :], from_next.at[cut:256, :], mate)
    og_tw.append(go(from_next, from_next, twin))
    pass_x(7)
    up.wait_recv()
    dn.wait_recv()
    to_x(4)
    pass_x(1)
    q_mate.wait_recv()
    q_loc.wait()
    list_loc.wait()

    @pl.when(cell != 0)
    def _():
        for d in range(1, NX):
            b_along_x[d - 1].wait_recv()

    for c in halo:
        c.wait_recv()

    def window(n):
        i, head = n % 4, n // 4
        return i, head, rows(128 * i, 128), pl.ds(pl.multiple_of(128 * i, 128), 1152), rows(128 * head, 128)

    def forward(n, carry):
        i, head, toks, win, lanes = window(n)
        b = 4 * cell + i
        bias = []
        for j in range(9):
            kbl = b - 4 + j
            good = (kbl >= 1) & (kbl <= 127)
            if j not in (3, 4, 5):
                named = (lists[0, b] == kbl) | (lists[1, b] == kbl) | (lists[2, b] == kbl)
                good = good & named
            bias.append(jnp.full((1, BLK), jnp.where(good, 0.0, -jnp.inf), F32))
        bias = jnp.concatenate(bias, axis=1)
        qq = q2[toks, lanes]
        s0 = dot(qq, b0[0:BLK, lanes], NT) * SCALE
        s1 = dot(qq, kb[win, lanes], NT) * SCALE + bias
        top = jnp.maximum(jnp.max(s0, axis=1, keepdims=True), jnp.max(s1, axis=1, keepdims=True))
        e0, e1 = jnp.exp(s0 - top), jnp.exp(s1 - top)
        inv = 1.0 / (jnp.sum(e0, axis=1, keepdims=True) + jnp.sum(e1, axis=1, keepdims=True))
        p0, p1 = e0 * inv, e1 * inv
        probs[n, :, 0:BLK] = p0
        probs[n, :, BLK:] = p1
        out = dot(p0.astype(BF), b0[BLK : 2 * BLK, lanes]) + dot(p1.astype(BF), vb[win, lanes])
        mixed[toks, lanes] = out.astype(BF)
        return carry

    lax.fori_loop(0, 1, forward, 0)
    pass_x(6)
    og_mate[1].wait_recv()
    fwd_next.append(go(from_mate.at[half:cut, :], from_mate.at[half:cut, :], nxt))
    og_tw.append(go(from_mate.at[half:256, :], from_mate.at[half:256, :], twin))
    pass_x(2)
    lax.fori_loop(1, 3, forward, 0)
    pass_x(5)
    pass_x(3)
    lax.fori_loop(3, 5, forward, 0)
    pass_x(4)
    fwd_mate.wait_recv()
    og_tw.append(go(far.at[cut:256, :], far.at[cut:256, :], twin))
    fwd_next[0].wait_recv()
    og_tw.append(go(far.at[0:half, :], far.at[0:half, :], twin))
    lax.fori_loop(5, 8, forward, 0)
    fwd_next[1].wait_recv()
    og_tw.append(go(far.at[half:cut, :], far.at[half:cut, :], twin))
    og_loc.wait()
    for c in og_tw:
        c.wait_recv()

    def weight_part(xx):
        total = dot(mixed[0:256, :], ogf[0, xx], TN) + dot(mixed[256:512, :], ogf[1, xx], TN)
        for n in range(8):
            wg[xx, n] = total[:, 128 * n : 128 * (n + 1)].astype(BF)

    def attended_part(t, c):
        hh = (t // 2) * 2 + c
        part = dot(mixed[rows(256 * (t % 2), 256), :], wf[hh].reshape(1024, 256), NT)
        at[t % 2, hh] = part.astype(BF)

    w1, w2u, w2d = {}, {}, {}

    def piece(xx, off):
        return wg.at[xx, (z + off) % NZ]

    first_group, second_group = (4, 3, 5, 2), (6, 1, 7, 0)
    for off in first_group + second_group:
        ks, ku, kd = net.numbers(), net.numbers(), net.numbers()
        w1[off] = (
            off >= 4 if off in first_group else goes_up(off >= 4),
            net.make(piece(x_far, off), wg_r1.at[off], xu, ks),
            net.make(piece(x_far, off), wg_r1.at[off], xd, ks),
        )
        w2u[off] = (
            net.make(piece(x_up, off), wg_r2.at[0, off], xu, ku),
            net.make(wg_s.at[off], wg_r2.at[0, off], xu, ku),
        )
        w2d[off] = (
            net.make(piece(x_dn, off), wg_r2.at[1, off], xd, kd),
            net.make(wg_s.at[off], wg_r2.at[1, off], xd, kd),
        )

    def either_way(off, up_way, down_way):
        is_up = w1[off][0]
        if isinstance(is_up, bool):
            (up_way if is_up else down_way)()
        else:
            pl.when(is_up)(up_way)
            pl.when(jnp.logical_not(is_up))(down_way)

    def straight(off):
        either_way(off, w2d[off][0].start, w2u[off][0].start)

    def relay(off):
        def up_way():
            w1[off][1].wait_recv()
            add(wg_s.at[off], piece(x_up, off), wg_r1.at[off])
            w2u[off][1].start()

        def down_way():
            w1[off][2].wait_recv()
            add(wg_s.at[off], piece(x_dn, off), wg_r1.at[off])
            w2d[off][1].start()

        either_way(off, up_way, down_way)

    weight_part(x_far)
    for off in first_group + second_group:
        either_way(off, w1[off][1].start, w1[off][2].start)
    for pair in x_fwd:
        either(pair[0], lambda c: c.wait_recv(), pair[1], pair[2])
    order = (y_far, y_mate, y_next, y)
    cores = []
    for t in order:
        attended_part(t, 1 - core)
        cores.append(go(at.at[t % 2, (t // 2) * 2 + 1 - core], at_core.at[t], twin))
    weight_part(x_up)
    weight_part(x_dn)
    for off in (4, 3, 5, 2):
        straight(off)
    for t in order:
        attended_part(t, core)
    weight_part(x)
    for t in range(2):
        total = jnp.zeros((256, 256), F32)
        for hh in range(4):
            total = total + dot(ogf[t, hh], wf[hh].reshape(1024, 256))
        mgrad[256 * t : 256 * (t + 1), :] = total.astype(BF)
    dk[...] = jnp.zeros_like(dk)
    dv[...] = jnp.zeros_like(dv)
    d0[...] = jnp.zeros_like(d0)
    for off in (4, 3, 5, 2):
        relay(off)
    for off in (6, 1, 7, 0):
        straight(off)

    for n, t in enumerate(order):
        cores[n].wait_recv()
        add(at_sum.at[t], at.at[t % 2, (t // 2) * 2 + core], at_core.at[t])
        if n == 0:
            a1n = go(at_sum.at[t, 0:128, :], at_r1.at[0], nxt)
            a1m = go(at_sum.at[t, 128:256, :], at_r1.at[1], mate)
        if n == 1:
            a2m = [go(at_sum.at[t, 128:256, :], at_r2.at[0, 128:256, :], mate)]
        if n == 2:
            a2n = [go(at_sum.at[t, 0:128, :], at_r2.at[1, 0:128, :], nxt)]

    def backward(n, carry):
        i, head, toks, win, lanes = window(n)
        g = mgrad[toks, lanes]
        delta = jnp.sum(
            g.astype(F32) * mixed[toks, lanes].astype(F32), axis=1, keepdims=True
        )
        p0, p1 = probs[n, :, 0:BLK], probs[n, :, BLK:]
        sl0 = (p0 * (dot(g, b0[BLK : 2 * BLK, lanes], NT) - delta)).astype(BF)
        sl1 = (p1 * (dot(g, vb[win, lanes], NT) - delta)).astype(BF)
        out = dot(sl0, b0[0:BLK, lanes]) + dot(sl1, kb[win, lanes])
        dq[toks, lanes] = (out * SCALE).astype(BF)
        qq = q2[toks, lanes]
        dk[win, lanes] += dot(sl1, qq, TN)
        dv[win, lanes] += dot(p1.astype(BF), g, TN)
        d0[0, :, lanes] += dot(sl0, qq, TN)
        d0[1, :, lanes] += dot(p0.astype(BF), g, TN)
        return carry

    edges, q_out, locals_out = [[], []], [], []

    def leave(head, n):
        acc, factor = ((dk, SCALE), (dv, 1.0))[n]
        lanes = slice(128 * head, 128 * (head + 1))
        dke[head, n, 0] = (acc[0:512, lanes] * factor).astype(BF)
        dke[head, n, 1] = (acc[1024:1536, lanes] * factor).astype(BF)
        pair = (
            net.make(dke.at[head, n, 0], dk_r.at[head, n, 1], cd),
            net.make(dke.at[head, n, 1], dk_r.at[head, n, 0], cu),
        )
        edges[head] += pair
        if (head, n) == (0, 0):
            pair[0].start()
            pair[1].start()
        else:
            pl.when(z != 0)(pair[0].start)
            pl.when(z != NZ - 1)(pair[1].start)

    def leave_row(head, n, row):
        pl.when(z == row)(edges[head][2 * n + (row != 0)].start)

    def leave_q(head):
        lanes = slice(128 * head, 128 * (head + 1))
        cols = rows(256 * ylo + 128 * head, 128)
        q_out.append(go(dq.at[other, lanes], o_dq.at[:, cols], mate))
        locals_out.append(here_now(dq.at[mine, lanes], o_dq.at[:, cols]))

    def sum_x(off):
        w2u[off][0].wait_recv()
        w2d[off][0].wait_recv()
        add(wg_x.at[off], piece(x, off), wg_r2.at[0, off], wg_r2.at[1, off])

    def z_step(s, up, dn):
        tu, td = 5 - s, 3 + s
        up.wait_recv()
        if s == 2:
            add(wz_s.at[0, 1, 0:128, :], wg_x.at[tu, 0:128, :], wz_r.at[0, 0, 0:128, :])
            add(wz_s.at[0, 1, 128:256, :], wg_x.at[tu, 128:256, :])
        else:
            add(wz_s.at[0, s - 1], wg_x.at[tu], wz_r.at[0, s - 2])
        up = go(wz_s.at[0, s - 1], wz_r.at[0, s - 1], zu)
        dn.wait_recv()
        if s == 2:
            add(wz_s.at[1, 1, 128:256, :], wg_x.at[td, 128:256, :], wz_r.at[1, 0, 128:256, :])
            add(wz_s.at[1, 1, 0:128, :], wg_x.at[td, 0:128, :])
        else:
            add(wz_s.at[1, s - 1], wg_x.at[td], wz_r.at[1, s - 2])
        dn = go(wz_s.at[1, s - 1], wz_r.at[1, s - 1], zd)
        return up, dn

    lax.fori_loop(0, 4, backward, 0)
    for off in (6, 1, 7, 0):
        relay(off)
    leave(0, 0)
    leave_q(0)
    lax.fori_loop(4, 8, backward, 0)

    d0_b[0:BLK, :] = (d0[0] * SCALE).astype(BF)
    d0_b[BLK : 2 * BLK, :] = d0[1].astype(BF)
    d0_x = [
        go(
            d0_b.at[rows(64 * ((x + d) % NX), 64), :],
            d0_xr.at[d - 1],
            device((x + d) % NX, z, y, core),
        )
        for d in range(1, NX)
    ]
    z_send = net.numbers()
    net.n_recv += NZ - 2
    d0_z = [
        net.make(d0_s, d0_zr.at[d - 1], device(x, 0, y, core), (z_send[0], z_send[1] + d - 1))
        for d in range(1, NZ)
    ]
    o_send = net.numbers()
    d0_o = [
        net.make(d0_t, d0_q.at[d - 1], device(0, z, y, core), (o_send[0], o_send[1] + d - 1))
        for d in range(1, NX)
    ]
    net.n_recv += NX - 2

    sum_x(4)
    add(wz_s.at[0, 0, 0:128, :], wg_x.at[4, 0:128, :])
    up = go(wz_s.at[0, 0, 0:128, :], wz_r.at[0, 0, 0:128, :], zu)
    add(wz_s.at[1, 0, 128:256, :], wg_x.at[4, 128:256, :])
    dn = go(wz_s.at[1, 0, 128:256, :], wz_r.at[1, 0, 128:256, :], zd)
    leave(0, 1)
    leave_q(1)
    sum_x(3)
    sum_x(5)
    up, dn = z_step(2, up, dn)
    leave_row(0, 1, 0)
    leave_row(0, 1, NZ - 1)
    leave(1, 0)

    a1n.wait_recv()
    to_mate = at_core.at[0, 0:128, :]
    add(to_mate, at_sum.at[y_mate, 0:128, :], at_r1.at[0])
    a2m.append(go(to_mate, at_r2.at[0, 0:128, :], mate))
    a1m.wait_recv()
    to_next = at_core.at[1, 128:256, :]
    add(to_next, at_sum.at[y_next, 128:256, :], at_r1.at[1])
    a2n.append(go(to_next, at_r2.at[1, 128:256, :], nxt))

    sum_x(2)
    sum_x(6)
    up, dn = z_step(3, up, dn)
    leave(1, 1)
    leave_row(1, 0, 0)

    kv_mate, kv_here = [[], []], [[], []]

    def finish(head):
        for c in edges[head]:
            c.wait_recv()
        lanes = slice(128 * head, 128 * (head + 1))
        cols = rows(256 * ylo + 128 * head, 128)
        for n, (acc, factor) in enumerate(((dk, SCALE), (dv, 1.0))):
            dkv_s[n, :, lanes] = (
                acc[512:1024, lanes] * factor
                + dk_r[head, n, 0].astype(F32)
                + dk_r[head, n, 1].astype(F32)
            )
            out = (o_dk, o_dv)[n]
            for r in (0, BLK):
                src = d_out.at[n, rows(256 * (1 - ylo) + r, BLK), lanes]
                kv_mate[head].append(net.make(src, out.at[r : r + BLK, cols], mate))
            kv_here[head].append(here(d_out.at[n, mine, lanes], out.at[:, cols]))

        d_out[:, :, lanes] = dkv_s[:, :, lanes].astype(BF)
        for m, c in enumerate(kv_mate[head]):
            if m % 2 == 1:
                c.start()
            else:
                pl.when((cell != 0) | (ylo == 0))(c.start)
        for c in kv_here[head]:
            pl.when(cell != 0)(c.start)

    for c in d0_x:
        c.wait_recv()
    add(d0_s, d0_b.at[quarter, :], *[d0_xr.at[d] for d in range(3)])
    for d in range(1, NZ):

        @pl.when(z == d)
        def _():
            d0_z[d - 1].start()

    leave_row(1, 0, NZ - 1)
    sum_x(1)
    sum_x(7)
    up, dn = z_step(4, up, dn)
    leave_row(1, 1, 0)
    leave_row(1, 1, NZ - 1)
    finish(0)

    @pl.when(z == 0)
    def _():
        for c in d0_z:
            c.wait_recv()
        add(d0_t, d0_s, *[d0_zr.at[d] for d in range(NZ - 1)])
        for d in range(1, NX):

            @pl.when(x == d)
            def _():
                d0_o[d - 1].start()

    sum_x(0)
    w_last = net.make(w_out.at[rows(64 * (1 - ylo), 64), :], o_wg.at[:, mine], mate)
    w_here = here(w_out.at[rows(64 * ylo, 64), :], o_wg.at[:, mine])
    locals_out.append(w_here)

    def last_sum():
        up.wait_recv()
        dn.wait_recv()
        add(wg_x.at[0], wg_x.at[0], wz_r.at[0, 3], wz_r.at[1, 3])
        w_out[...] = wg_x[0].T
        w_last.start()
        w_here.start()

    edge_row = (z == 0) | (z == NZ - 1)
    pl.when(edge_row)(last_sum)
    finish(1)
    pl.when(jnp.logical_not(edge_row))(last_sum)

    @pl.when(cell == 0)
    def _():
        for c in d0_o:
            c.wait_recv()
        for m in range(4):
            part = d0_t[...] if m == 0 else d0_q[m - 1]
            dkv_s[m // 2, 64 * (m % 2) : 64 * (m % 2) + 64, :] += part.astype(F32)
        d_out[:, 0:BLK, :] = dkv_s[:, 0:BLK, :].astype(BF)

        @pl.when(ylo == 1)
        def _():
            for head in range(2):
                for c in kv_mate[head][0::2]:
                    c.start()

        for c in kv_here[0] + kv_here[1]:
            c.start()

    for c in a2m + a2n:
        c.wait_recv()
    add(at_o, at_sum.at[y], at_r2.at[0], at_r2.at[1])
    locals_out.append(here_now(at_o, o_at))

    for c in kv_mate[0] + kv_mate[1] + q_out + [w_last]:
        c.wait_recv()
    for c in locals_out + kv_here[0] + kv_here[1]:
        c.wait()
    net.drain()
    assert (net.n_send, net.n_recv, n_local[0]) == COUNTS, (net.n_send, net.n_recv, n_local)
    for c in kv_mate[0] + kv_mate[1] + edges[0] + edges[1] + [w_last]:
        c.wait_send()
    for pair in x_fwd:
        either(pair[0], lambda c: c.wait_send(), pair[1], pair[2])
    for off in first_group + second_group:
        either_way(off, w1[off][1].wait_send, w1[off][2].wait_send)
        w2u[off][0].wait_send()
        w2d[off][0].wait_send()

    @pl.when(cell == 0)
    def _():
        @pl.when(ylo == 0)
        def _():
            for c in b_mate:
                c.wait_send()

        for c in b_to_x:
            c.wait_send()

    to_x_peers(lambda c: c.wait_send())

    @pl.when(z == 0)
    def _():
        for c in b_along_z:
            c.wait_send()

        for d in range(1, NX):

            @pl.when(x == d)
            def _():
                d0_o[d - 1].wait_send()

    for d in range(1, NZ):

        @pl.when(z == d)
        def _():
            d0_z[d - 1].wait_send()


def hand_over_kernel(*refs):
    n = 5
    ins, outs, bufs, sem = refs[:n], refs[n : 2 * n], refs[2 * n : 3 * n], refs[3 * n]
    reads = [pltpu.make_async_copy(ins[i], bufs[i], sem.at[0, i]) for i in range(n)]
    writes = [pltpu.make_async_copy(bufs[i], outs[i], sem.at[1, i]) for i in range(n)]
    for c in reads:
        c.start()
    for i in range(n):
        reads[i].wait()
        writes[i].start()
    for c in writes:
        c.wait()


def anywhere(n):
    return [pl.BlockSpec(memory_space=pl.ANY)] * n


def local(queries, key_heads, value_heads, out_weight, block_lists, out_grad):
    results = (
        jax.ShapeDtypeStruct((256, 1024), BF),
        jax.ShapeDtypeStruct((256, 512), BF),
        jax.ShapeDtypeStruct((256, 512), BF),
        jax.ShapeDtypeStruct((256, 512), BF),
        jax.ShapeDtypeStruct((64, 512), F32),
    )
    b, f = (lambda *s: pltpu.VMEM(s, BF)), (lambda *s: pltpu.VMEM(s, F32))
    scratch = [
        pltpu.SMEM((3, 128), jnp.int32),
        b(512, 256),
        b(1536, 256),
        b(1536, 256),
        b(256, 256),
        b(NX, NZ, 128, 256),
        b(2, 4, 256, 1024),
        b(2, 4, 256, 1024),
        b(4, 8, 256, 128),
        f(8, 128, 1280),
        b(512, 256),
        b(512, 256),
        f(1536, 256),
        f(1536, 256),
        f(2, 128, 256),
        b(512, 256),
        b(4, 256, 1024),
        b(4, 256, 1024),
        b(2, 128, 1024),
        b(2, 256, 1024),
        b(256, 1024),
        b(8, 256, 128),
        b(8, 256, 128),
        b(2, 8, 256, 128),
        f(8, 256, 128),
        b(2, 4, 256, 128),
        b(2, 4, 256, 128),
        f(128, 256),
        b(2, 2, 2, 512, 128),
        b(2, 2, 2, 512, 128),
        b(256, 256),
        b(3, 64, 256),
        b(64, 256),
        b(7, 64, 256),
        b(64, 256),
        b(3, 64, 256),
        f(2, 512, 256),
        b(2, 512, 256),
        pltpu.SemaphoreType.DMA((N_SEND,)),
        pltpu.SemaphoreType.DMA((N_RECV,)),
        pltpu.SemaphoreType.DMA((N_LOCAL,)),
    ]
    outs = pl.pallas_call(
        layer_kernel,
        out_shape=results,
        in_specs=anywhere(6),
        out_specs=tuple(anywhere(5)),
        scratch_shapes=scratch,
        compiler_params=pltpu.CompilerParams(
            collective_id=0, has_side_effects=True, vmem_limit_bytes=60 * 1024 * 1024
        ),
        name="layer",
    )(queries, key_heads, value_heads, out_weight, block_lists.T, out_grad)
    return pl.pallas_call(
        hand_over_kernel,
        out_shape=results,
        in_specs=anywhere(5),
        out_specs=tuple(anywhere(5)),
        scratch_shapes=[pltpu.VMEM(r.shape, r.dtype) for r in results]
        + [pltpu.SemaphoreType.DMA((2, 5))],
        name="hand_over",
    )(*outs)


def solution(mesh):
    placed = P("ctx", "head")
    return jax.shard_map(
        local,
        mesh=mesh,
        in_specs=(placed, placed, placed, placed, P(), placed),
        out_specs=(placed,) * 5,
        check_vma=False,
    )
```

```python
import jax
import jax.numpy as jnp
from jax import lax
from jax.experimental import pallas as pl
from jax.experimental.pallas import tpu as pltpu
from jax.sharding import PartitionSpec as P

HD = 128
BLK = 128
SCALE = HD ** -0.5
BF = jnp.bfloat16
F32 = jnp.float32
NX, NZ, NY = 4, 8, 4
POOL = 64
COUNTS = N_SEND, N_RECV, N_LOCAL = 81, 122, 16


def place():
    i = lax.axis_index("ctx")
    h = lax.axis_index("head")
    cell = i // 2
    return cell // NZ, cell % NZ, (h // 2) * 2 + i % 2, h % 2, cell


def device(x, z, y, core):
    return ((x * NZ + z) * 2 + y % 2, (y // 2) * 2 + core)


def rows(start, size):
    return pl.ds(pl.multiple_of(start, size), size)


class Copies:
    def __init__(self, send, recv):
        self.send, self.recv = send, recv
        self.n_send, self.n_recv, self.live = POOL, 0, []

    def new_send(self):
        self.n_send += 1
        return self.n_send - 1

    def new_recv(self):
        self.n_recv += 1
        return self.n_recv - 1

    def numbers(self, k_send=None, k_recv=None):
        k_send = self.new_send() if k_send is None else k_send
        return k_send, self.new_recv() if k_recv is None else k_recv

    def make(self, src, dst, target, numbers=None):
        k_send, k_recv = numbers or self.numbers()
        return pltpu.make_async_remote_copy(
            src_ref=src,
            dst_ref=dst,
            send_sem=self.send.at[k_send],
            recv_sem=self.recv.at[k_recv],
            device_id=target,
            device_id_type=pl.DeviceIdType.MESH,
        )

    def start(self, src, dst, target, k_recv=None):
        k_send = len(self.live)
        if k_send == POOL:
            k_send, oldest = self.live.pop(0)
            oldest.wait_send()
        c = self.make(src, dst, target, self.numbers(k_send, k_recv))
        c.start()
        self.live.append((k_send, c))
        return c

    def drain(self):
        for _, c in self.live:
            c.wait_send()


def greet(peers):
    barrier = pltpu.get_barrier_semaphore()
    for peer in peers:
        pl.semaphore_signal(
            barrier, inc=1, device_id=peer, device_id_type=pl.DeviceIdType.MESH
        )
    pl.semaphore_wait(barrier, len(peers))


def all_peers(x, z, y, core, cell):
    up, down = (cell + 1) % (NX * NZ), (cell + NX * NZ - 1) % (NX * NZ)
    peers = [device((x + d) % NX, z, y, core) for d in range(1, NX)]
    peers += [device(x, (z + d) % NZ, y, core) for d in range(1, NZ)]
    peers += [device(x, z, (y + d) % NY, core) for d in (1, NY - 1)]
    peers += [device(x, z, y, 1 - core)]
    peers += [device(c // NZ, c % NZ, y, core) for c in (up, down)]
    return peers


def dot(a, b, dims=(((1,), (0,)), ((), ()))):
    return lax.dot_general(a, b, dims, preferred_element_type=F32)


NT = (((1,), (1,)), ((), ()))
TN = (((0,), (0,)), ((), ()))


def add(dst, *srcs):
    n, lanes = dst.shape
    step = min(n, 16384 // lanes)

    def body(i, carry):
        r = rows(step * i, step)
        total = srcs[0][r, :].astype(F32)
        for s in srcs[1:]:
            total = total + s[r, :].astype(F32)
        dst[r, :] = total.astype(dst.dtype)
        return carry

    lax.fori_loop(0, n // step, body, 0)


def layer_kernel(
    q, k, v, w, lists_hbm, og,
    o_at, o_dq, o_dk, o_dv, o_wg,
    lists, q2, kb, vb, b0, wf, ogf, at, wg, probs, mixed, mgrad, dk, dv, d0, dq,
    at_core, at_sum, at_r1, at_r2, at_o, wg_r1, wg_s, wg_r2, wg_x, wz_s, wz_r, w_out,
    dke, dk_r, d0_b, d0_xr, d0_s, d0_zr, d0_t, d0_q, dkv_s, d_out, send, recv, lsem,
):
    x, z, y, core, cell = place()
    ylo = y % 2
    h = (y // 2) * 2 + core
    x_up, x_dn, x_far = (x + 1) % NX, (x + NX - 1) % NX, (x + 2) % NX
    z_up, z_dn = (z + 1) % NZ, (z + NZ - 1) % NZ
    c_up, c_dn = (cell + 1) % (NX * NZ), (cell + NX * NZ - 1) % (NX * NZ)
    y_mate = y + 1 - 2 * ylo
    y_next = (y + NY - 1 + 2 * ylo) % NY
    y_far = (y + 2) % NY
    mate, nxt = device(x, z, y_mate, core), device(x, z, y_next, core)
    twin = device(x, z, y, 1 - core)
    xu, xd = device(x_up, z, y, core), device(x_dn, z, y, core)
    zu, zd = device(x, z_up, y, core), device(x, z_dn, y, core)
    cu, cd = device(c_up // NZ, c_up % NZ, y, core), device(c_dn // NZ, c_dn % NZ, y, core)
    net = Copies(send, recv)
    mine, other = rows(256 * ylo, 256), rows(256 * (1 - ylo), 256)
    band_mine, band_other = rows(512 + 256 * ylo, 256), rows(512 + 256 * (1 - ylo), 256)
    lo_mine, lo_other = mine, other
    hi_mine, hi_other = rows(1024 + 256 * ylo, 256), rows(1024 + 256 * (1 - ylo), 256)
    n_local = [0]

    def go(src, dst, target, k_recv=None):
        return net.start(src, dst, target, k_recv)

    def total_of(ref, k_recv=None, k_send=None):
        return net.make(ref, ref, mate, (k_send or 0, k_recv or 0))

    kv_send, edge_send, w1_send, w2_send, fwd_send, b_send = (net.new_send() for _ in range(6))
    k_halo, v_halo, d0x_recv, d0z_recv, d0o_recv = (net.new_recv() for _ in range(5))
    edge_recv = [[net.new_recv() for _ in range(2)] for _ in range(2)]

    def here(src, dst):
        c = pltpu.make_async_copy(src, dst, lsem.at[n_local[0]])
        n_local[0] += 1
        return c

    def here_now(src, dst):
        c = here(src, dst)
        c.start()
        return c

    w_loc = here_now(w.at[:, mine], wf.at[x, z, rows(64 * ylo, 64), :])
    k_loc = here_now(k.at[:, mine], kb.at[band_mine, :])
    v_loc = here_now(v.at[:, mine], vb.at[band_mine, :])
    og_loc = here_now(og, ogf.at[ylo, h])
    q_loc = here_now(q.at[:, mine], q2.at[mine, :])
    list_loc = here_now(lists_hbm, lists)
    greet(all_peers(x, z, y, core, cell))

    quarter = rows(64 * x, 64)
    b_mate = [
        net.make(k.at[0:BLK, other], b0.at[0:BLK, :], mate),
        net.make(v.at[0:BLK, other], b0.at[BLK : 2 * BLK, :], mate),
    ]
    b_loc = [
        here(k.at[0:BLK, mine], b0.at[0:BLK, :]),
        here(v.at[0:BLK, mine], b0.at[BLK : 2 * BLK, :]),
    ]
    b_to_x = [
        net.make(
            b0.at[rows(64 * ((x + d) % NX), 64), :],
            b0.at[rows(64 * ((x + d) % NX), 64), :],
            device((x + d) % NX, z, y, core),
        )
        for d in range(1, NX)
    ]
    b_along_z = [
        net.make(
            b0.at[quarter, :],
            b0.at[quarter, :],
            device(x, (z + d) % NZ, y, core),
            net.numbers(b_send),
        )
        for d in range(1, NZ)
    ]

    @pl.when((cell == 0) & (ylo == 0))
    def _():
        for c in b_mate + b_loc:
            c.start()

    w_mate = go(w.at[:, other], wf.at[x, z, rows(64 * ylo, 64), :], mate)
    k_mate = go(k.at[:, other], kb.at[band_mine, :], mate)
    v_mate = go(v.at[:, other], vb.at[band_mine, :], mate)
    og_next = go(og, ogf.at[ylo, h], nxt)
    half, cut = 160, 208
    og_here = ogf.at[ylo, h]
    og_mate = [go(og.at[0:half, :], og_here.at[0:half, :], mate)]
    q_mate = go(q.at[:, other], q2.at[mine, :], mate)
    og_mate.append(go(og.at[half:256, :], og_here.at[half:256, :], mate))
    og_tw = [go(og, og_here, twin)]

    own_half, mate_half = rows(64 * ylo, 64), rows(64 * (1 - ylo), 64)
    first = [go(w.at[:, mine], wf.at[x, z, own_half, :], t) for t in (zu, zd, xu, xd)]
    halo = [
        go(k.at[:, mine], kb.at[lo_mine, :], cu, k_halo),
        go(k.at[:, mine], kb.at[hi_mine, :], cd, k_halo),
    ]
    w_mate.wait_recv()
    w_loc.wait()

    x_plus, x_minus, x_fwd = {}, {}, []

    def to_x(off):
        zz = (z + off) % NZ
        x_plus[off] = go(wf.at[x, zz], wf.at[x, zz], xu)
        x_minus[off] = go(wf.at[x, zz], wf.at[x, zz], xd)

    def either(cond, fn, then, other):
        @pl.when(cond)
        def _():
            fn(then)

        @pl.when(jnp.logical_not(cond))
        def _():
            fn(other)

    def goes_up(is_up):
        return (z == 7) | (z != 0) if is_up else z == 7

    def pass_x(off):
        zz = (z + off) % NZ
        if off == 0:
            first[2].wait_recv()
            first[3].wait_recv()
        x_plus[off].wait_recv()
        x_minus[off].wait_recv()
        ks = net.numbers(fwd_send)
        pair = (
            goes_up(off in (0, 6, 2, 4)),
            net.make(wf.at[x_dn, zz], wf.at[x_dn, zz], xu, ks),
            net.make(wf.at[x_up, zz], wf.at[x_up, zz], xd, ks),
        )
        either(pair[0], lambda c: c.start(), pair[1], pair[2])
        x_fwd.append(pair)

    def ring_step(s, up, dn):
        zm, zp = (z + NZ - s) % NZ, (z + s) % NZ
        if s == 1:
            first[0].wait_recv()
            first[1].wait_recv()
        up.wait_recv()
        if s < 3:
            up = go(wf.at[x, zm], wf.at[x, zm], zu)
        else:
            up = go(wf.at[x, zm, 0:64, :], wf.at[x, zm, 0:64, :], zu)
        to_x(NZ - s)
        dn.wait_recv()
        if s < 3:
            dn = go(wf.at[x, zp], wf.at[x, zp], zd)
        else:
            dn = go(wf.at[x, zp, 64:128, :], wf.at[x, zp, 64:128, :], zd)
        to_x(s)
        return up, dn

    second = wf.at[x, z, mate_half, :]
    up = go(second, second, zu)
    dn = go(second, second, zd)
    x_plus[0] = go(second, second, xu)
    x_minus[0] = go(second, second, xd)

    @pl.when(cell == 0)
    def _():
        @pl.when(ylo == 0)
        def _():
            for c in b_loc:
                c.wait()

        @pl.when(ylo == 1)
        def _():
            for c in b_mate:
                c.wait_recv()

        for c in b_to_x:
            c.start()

    up, dn = ring_step(1, up, dn)

    @pl.when(z == 0)
    def _():
        for d in range(1, NX):

            @pl.when(x == d)
            def _():
                b_to_x[d - 1].wait_recv()

        for n in (3, 4, 2, 5, 1, 6, 0):
            b_along_z[n].start()

    halo += [
        go(v.at[:, mine], vb.at[lo_mine, :], cu, v_halo),
        go(v.at[:, mine], vb.at[hi_mine, :], cd, v_halo),
    ]
    k_mate.wait_recv()
    k_loc.wait()
    up, dn = ring_step(2, up, dn)
    halo += [
        go(kb.at[band_other, :], kb.at[lo_other, :], cu, k_halo),
        go(kb.at[band_other, :], kb.at[hi_other, :], cd, k_halo),
    ]
    pass_x(0)
    for d in range(1, NZ):

        @pl.when(z == d)
        def _():
            b_along_z[d - 1].wait_recv()

    b_along_x = [
        net.make(b0.at[quarter, :], b0.at[quarter, :], device((x + d) % NX, z, y, core))
        for d in range(1, NX)
    ]

    def to_x_peers(fn):
        for d in range(1, NX):

            @pl.when((z != 0) | ((x + d) % NX != 0))
            def _():
                fn(b_along_x[d - 1])

    to_x_peers(lambda c: c.start())

    v_mate.wait_recv()
    v_loc.wait()
    up, dn = ring_step(3, up, dn)
    halo += [
        go(vb.at[band_other, :], vb.at[lo_other, :], cu, v_halo),
        go(vb.at[band_other, :], vb.at[hi_other, :], cd, v_halo),
    ]
    from_mate = ogf.at[y_mate % 2, (y_mate // 2) * 2 + core]
    from_next = ogf.at[y_next % 2, (y_next // 2) * 2 + core]
    far = ogf.at[y_far % 2, (y_far // 2) * 2 + core]
    og_mate[0].wait_recv()
    fwd_next = [go(from_mate.at[0:half, :], from_mate.at[0:half, :], nxt)]
    og_tw.append(go(from_mate.at[0:half, :], from_mate.at[0:half, :], twin))
    og_next.wait_recv()
    fwd_mate = go(from_next.at[cut:256, :], from_next.at[cut:256, :], mate)
    og_tw.append(go(from_next, from_next, twin))
    pass_x(7)
    up.wait_recv()
    dn.wait_recv()
    to_x(4)
    pass_x(1)
    q_mate.wait_recv()
    q_loc.wait()
    list_loc.wait()

    @pl.when(cell != 0)
    def _():
        for d in range(1, NX):
            b_along_x[d - 1].wait_recv()

    total_of(kb.at[0:1024, :], k_halo).wait_recv()
    total_of(vb.at[0:1024, :], v_halo).wait_recv()

    def window(n):
        i, head = n % 4, n // 4
        return i, head, rows(128 * i, 128), pl.ds(pl.multiple_of(128 * i, 128), 1152), rows(128 * head, 128)

    def forward(n, carry):
        i, head, toks, win, lanes = window(n)
        b = 4 * cell + i
        bias = []
        for j in range(9):
            kbl = b - 4 + j
            good = (kbl >= 1) & (kbl <= 127)
            if j not in (3, 4, 5):
                named = (lists[0, b] == kbl) | (lists[1, b] == kbl) | (lists[2, b] == kbl)
                good = good & named
            bias.append(jnp.full((1, BLK), jnp.where(good, 0.0, -jnp.inf), F32))
        bias = jnp.concatenate(bias, axis=1)
        qq = q2[toks, lanes]
        s0 = dot(qq, b0[0:BLK, lanes], NT) * SCALE
        s1 = dot(qq, kb[win, lanes], NT) * SCALE + bias
        top = jnp.maximum(jnp.max(s0, axis=1, keepdims=True), jnp.max(s1, axis=1, keepdims=True))
        e0, e1 = jnp.exp(s0 - top), jnp.exp(s1 - top)
        inv = 1.0 / (jnp.sum(e0, axis=1, keepdims=True) + jnp.sum(e1, axis=1, keepdims=True))
        p0, p1 = e0 * inv, e1 * inv
        probs[n, :, 0:BLK] = p0
        probs[n, :, BLK:] = p1
        out = dot(p0.astype(BF), b0[BLK : 2 * BLK, lanes]) + dot(p1.astype(BF), vb[win, lanes])
        mixed[toks, lanes] = out.astype(BF)
        return carry

    lax.fori_loop(0, 1, forward, 0)
    pass_x(6)
    og_mate[1].wait_recv()
    fwd_next.append(go(from_mate.at[half:cut, :], from_mate.at[half:cut, :], nxt))
    og_tw.append(go(from_mate.at[half:256, :], from_mate.at[half:256, :], twin))
    pass_x(2)
    lax.fori_loop(1, 3, forward, 0)
    pass_x(5)
    pass_x(3)
    lax.fori_loop(3, 5, forward, 0)
    pass_x(4)
    fwd_mate.wait_recv()
    og_tw.append(go(far.at[cut:256, :], far.at[cut:256, :], twin))
    fwd_next[0].wait_recv()
    og_tw.append(go(far.at[0:half, :], far.at[0:half, :], twin))
    lax.fori_loop(5, 8, forward, 0)
    fwd_next[1].wait_recv()
    og_tw.append(go(far.at[half:cut, :], far.at[half:cut, :], twin))
    og_loc.wait()
    for c in og_tw:
        c.wait_recv()

    def weight_part(xx):
        total = dot(mixed[0:256, :], ogf[0, xx], TN) + dot(mixed[256:512, :], ogf[1, xx], TN)
        for n in range(8):
            wg[xx, n] = total[:, 128 * n : 128 * (n + 1)].astype(BF)

    def attended_part(t, c):
        hh = (t // 2) * 2 + c
        part = dot(mixed[rows(256 * (t % 2), 256), :], wf[hh].reshape(1024, 256), NT)
        at[t % 2, hh] = part.astype(BF)

    w1, w2u, w2d, w2_recv = {}, {}, {}, {}

    def piece(xx, off):
        return wg.at[xx, (z + off) % NZ]

    first_group, second_group = (4, 3, 5, 2), (6, 1, 7, 0)
    for off in first_group + second_group:
        ks = net.numbers(w1_send)
        ku = kd = net.numbers(w2_send)
        w2_recv[off] = ku[1]
        w1[off] = (
            off >= 4 if off in first_group else goes_up(off >= 4),
            net.make(piece(x_far, off), wg_r1.at[off], xu, ks),
            net.make(piece(x_far, off), wg_r1.at[off], xd, ks),
        )
        w2u[off] = (
            net.make(piece(x_up, off), wg_r2.at[0, off], xu, ku),
            net.make(wg_s.at[off], wg_r2.at[0, off], xu, ku),
        )
        w2d[off] = (
            net.make(piece(x_dn, off), wg_r2.at[1, off], xd, kd),
            net.make(wg_s.at[off], wg_r2.at[1, off], xd, kd),
        )

    def either_way(off, up_way, down_way):
        is_up = w1[off][0]
        if isinstance(is_up, bool):
            (up_way if is_up else down_way)()
        else:
            pl.when(is_up)(up_way)
            pl.when(jnp.logical_not(is_up))(down_way)

    def straight(off):
        either_way(off, w2d[off][0].start, w2u[off][0].start)

    def relay(off):
        def up_way():
            w1[off][1].wait_recv()
            add(wg_s.at[off], piece(x_up, off), wg_r1.at[off])
            w2u[off][1].start()

        def down_way():
            w1[off][2].wait_recv()
            add(wg_s.at[off], piece(x_dn, off), wg_r1.at[off])
            w2d[off][1].start()

        either_way(off, up_way, down_way)

    def backward(n, carry):
        i, head, toks, win, lanes = window(n)
        g = mgrad[toks, lanes]
        delta = jnp.sum(
            g.astype(F32) * mixed[toks, lanes].astype(F32), axis=1, keepdims=True
        )
        p0, p1 = probs[n, :, 0:BLK], probs[n, :, BLK:]
        sl0 = (p0 * (dot(g, b0[BLK : 2 * BLK, lanes], NT) - delta)).astype(BF)
        sl1 = (p1 * (dot(g, vb[win, lanes], NT) - delta)).astype(BF)
        out = dot(sl0, b0[0:BLK, lanes]) + dot(sl1, kb[win, lanes])
        dq[toks, lanes] = (out * SCALE).astype(BF)
        qq = q2[toks, lanes]
        dk[win, lanes] += dot(sl1, qq, TN)
        dv[win, lanes] += dot(p1.astype(BF), g, TN)
        d0[0, :, lanes] += dot(sl0, qq, TN)
        d0[1, :, lanes] += dot(p0.astype(BF), g, TN)
        return carry

    edges, q_out, locals_out = [[], []], [], []

    def leave(head, n):
        acc, factor = ((dk, SCALE), (dv, 1.0))[n]
        lanes = slice(128 * head, 128 * (head + 1))
        dke[head, n, 0] = (acc[0:512, lanes] * factor).astype(BF)
        dke[head, n, 1] = (acc[1024:1536, lanes] * factor).astype(BF)
        pair = (
            net.make(dke.at[head, n, 0], dk_r.at[head, n, 1], cd, (edge_send, edge_recv[head][n])),
            net.make(dke.at[head, n, 1], dk_r.at[head, n, 0], cu, (edge_send, edge_recv[head][n])),
        )
        edges[head] += pair
        pair[0].start()
        pair[1].start()

    def leave_q(head):
        lanes = slice(128 * head, 128 * (head + 1))
        cols = rows(256 * ylo + 128 * head, 128)
        q_out.append(go(dq.at[other, lanes], o_dq.at[:, cols], mate))
        locals_out.append(here_now(dq.at[mine, lanes], o_dq.at[:, cols]))

    def sum_x(off):
        total_of(wg_r2.at[:, off], w2_recv[off]).wait_recv()
        add(wg_x.at[off], piece(x, off), wg_r2.at[0, off], wg_r2.at[1, off])

    def z_step(s, up, dn):
        tu, td = 5 - s, 3 + s
        up.wait_recv()
        if s == 2:
            add(wz_s.at[0, 1, 0:128, :], wg_x.at[tu, 0:128, :], wz_r.at[0, 0, 0:128, :])
            add(wz_s.at[0, 1, 128:256, :], wg_x.at[tu, 128:256, :])
        else:
            add(wz_s.at[0, s - 1], wg_x.at[tu], wz_r.at[0, s - 2])
        up = go(wz_s.at[0, s - 1], wz_r.at[0, s - 1], zu)
        dn.wait_recv()
        if s == 2:
            add(wz_s.at[1, 1, 128:256, :], wg_x.at[td, 128:256, :], wz_r.at[1, 0, 128:256, :])
            add(wz_s.at[1, 1, 0:128, :], wg_x.at[td, 0:128, :])
        else:
            add(wz_s.at[1, s - 1], wg_x.at[td], wz_r.at[1, s - 2])
        dn = go(wz_s.at[1, s - 1], wz_r.at[1, s - 1], zd)
        return up, dn

    weight_part(x_far)
    for off in first_group + second_group:
        either_way(off, w1[off][1].start, w1[off][2].start)
    for pair in x_fwd:
        either(pair[0], lambda c: c.wait_recv(), pair[1], pair[2])
    order = (y_far, y_mate, y_next, y)
    cores = []
    for t in order:
        attended_part(t, 1 - core)
        cores.append(go(at.at[t % 2, (t // 2) * 2 + 1 - core], at_core.at[t], twin))
    weight_part(x_up)
    weight_part(x_dn)
    for off in first_group:
        straight(off)
    for t in range(2):
        total = jnp.zeros((256, 256), F32)
        for hh in range(4):
            total = total + dot(ogf[t, hh], wf[hh].reshape(1024, 256))
        mgrad[256 * t : 256 * (t + 1), :] = total.astype(BF)
    dk[...] = jnp.zeros_like(dk)
    dv[...] = jnp.zeros_like(dv)
    d0[...] = jnp.zeros_like(d0)
    lax.fori_loop(0, 4, backward, 0)
    leave(0, 0)
    leave(0, 1)
    leave_q(0)
    for off in first_group:
        relay(off)
    lax.fori_loop(4, 8, backward, 0)
    leave(1, 0)

    d0_b[0:BLK, :] = (d0[0] * SCALE).astype(BF)
    d0_b[BLK : 2 * BLK, :] = d0[1].astype(BF)
    d0_x = [
        go(
            d0_b.at[rows(64 * ((x + d) % NX), 64), :],
            d0_xr.at[d - 1],
            device((x + d) % NX, z, y, core),
            d0x_recv,
        )
        for d in range(1, NX)
    ]
    z_send, o_send = net.new_send(), net.new_send()
    d0_z = [
        net.make(d0_s, d0_zr.at[d - 1], device(x, 0, y, core), (z_send, d0z_recv))
        for d in range(1, NZ)
    ]
    d0_o = [
        net.make(d0_t, d0_q.at[d - 1], device(0, z, y, core), (o_send, d0o_recv))
        for d in range(1, NX)
    ]

    for off in second_group:
        straight(off)
    for t in order:
        attended_part(t, core)
    weight_part(x)
    for n, t in enumerate(order):
        cores[n].wait_recv()
        add(at_sum.at[t], at.at[t % 2, (t // 2) * 2 + core], at_core.at[t])
        if n == 0:
            a1n = go(at_sum.at[t, 0:128, :], at_r1.at[0], nxt)
            a1m = go(at_sum.at[t, 128:256, :], at_r1.at[1], mate)
        if n == 1:
            a2m = [go(at_sum.at[t, 128:256, :], at_r2.at[0, 128:256, :], mate)]
        if n == 2:
            a2n = [go(at_sum.at[t, 0:128, :], at_r2.at[1, 0:128, :], nxt)]
    for off in second_group:
        relay(off)

    sum_x(4)
    add(wz_s.at[0, 0, 0:128, :], wg_x.at[4, 0:128, :])
    up = go(wz_s.at[0, 0, 0:128, :], wz_r.at[0, 0, 0:128, :], zu)
    add(wz_s.at[1, 0, 128:256, :], wg_x.at[4, 128:256, :])
    dn = go(wz_s.at[1, 0, 128:256, :], wz_r.at[1, 0, 128:256, :], zd)
    leave_q(1)
    sum_x(3)
    sum_x(5)
    up, dn = z_step(2, up, dn)
    leave(1, 1)

    a1n.wait_recv()
    to_mate = at_core.at[0, 0:128, :]
    add(to_mate, at_sum.at[y_mate, 0:128, :], at_r1.at[0])
    a2m.append(go(to_mate, at_r2.at[0, 0:128, :], mate))
    a1m.wait_recv()
    to_next = at_core.at[1, 128:256, :]
    add(to_next, at_sum.at[y_next, 128:256, :], at_r1.at[1])
    a2n.append(go(to_next, at_r2.at[1, 128:256, :], nxt))

    sum_x(2)
    sum_x(6)
    up, dn = z_step(3, up, dn)

    kv_mate, kv_here = [[], []], [[], []]

    def finish(head, n):
        total_of(dk_r.at[head, n], edge_recv[head][n]).wait_recv()
        acc, factor = ((dk, SCALE), (dv, 1.0))[n]
        out = (o_dk, o_dv)[n]
        lanes = slice(128 * head, 128 * (head + 1))
        cols = rows(256 * ylo + 128 * head, 128)
        dkv_s[n, :, lanes] = (
            acc[512:1024, lanes] * factor
            + dk_r[head, n, 0].astype(F32)
            + dk_r[head, n, 1].astype(F32)
        )
        d_out[n, :, lanes] = dkv_s[n, :, lanes].astype(BF)
        for r in (0, BLK):
            src = d_out.at[n, rows(256 * (1 - ylo) + r, BLK), lanes]
            c = net.make(src, out.at[r : r + BLK, cols], mate, net.numbers(kv_send))
            kv_mate[head].append(c)
            if r == 0:
                pl.when((cell != 0) | (ylo == 0))(c.start)
            else:
                c.start()
        c = here(d_out.at[n, mine, lanes], out.at[:, cols])
        kv_here[head].append(c)
        pl.when(cell != 0)(c.start)

    total_of(d0_xr, d0x_recv).wait_recv()
    add(d0_s, d0_b.at[quarter, :], *[d0_xr.at[d] for d in range(3)])
    for d in range(1, NZ):

        @pl.when(z == d)
        def _():
            d0_z[d - 1].start()

    sum_x(1)
    sum_x(7)
    up, dn = z_step(4, up, dn)
    finish(0, 0)
    finish(0, 1)

    @pl.when(z == 0)
    def _():
        total_of(d0_zr, d0z_recv).wait_recv()
        add(d0_t, d0_s, *[d0_zr.at[d] for d in range(NZ - 1)])
        for d in range(1, NX):

            @pl.when(x == d)
            def _():
                d0_o[d - 1].start()

    sum_x(0)
    w_last = net.make(w_out.at[rows(64 * (1 - ylo), 64), :], o_wg.at[:, mine], mate)
    w_here = here(w_out.at[rows(64 * ylo, 64), :], o_wg.at[:, mine])
    locals_out.append(w_here)

    def last_sum():
        up.wait_recv()
        dn.wait_recv()
        add(wg_x.at[0], wg_x.at[0], wz_r.at[0, 3], wz_r.at[1, 3])
        w_out[...] = wg_x[0].T
        w_last.start()
        w_here.start()

    edge_row = (z == 0) | (z == NZ - 1)
    pl.when(edge_row)(last_sum)
    finish(1, 0)

    finish(1, 1)

    pl.when(jnp.logical_not(edge_row))(last_sum)

    @pl.when(cell == 0)
    def _():
        total_of(d0_q, d0o_recv).wait_recv()
        for m in range(4):
            part = d0_t[...] if m == 0 else d0_q[m - 1]
            dkv_s[m // 2, 64 * (m % 2) : 64 * (m % 2) + 64, :] += part.astype(F32)
        d_out[:, 0:BLK, :] = dkv_s[:, 0:BLK, :].astype(BF)

        @pl.when(ylo == 1)
        def _():
            for head in range(2):
                for c in kv_mate[head][0::2]:
                    c.start()

        for c in kv_here[0] + kv_here[1]:
            c.start()

    for c in a2m + a2n:
        c.wait_recv()
    add(at_o, at_sum.at[y], at_r2.at[0], at_r2.at[1])
    locals_out.append(here_now(at_o, o_at))

    for c in kv_mate[0] + kv_mate[1] + q_out + [w_last]:
        c.wait_recv()
    for c in locals_out + kv_here[0] + kv_here[1]:
        c.wait()
    net.drain()
    assert (net.n_send, net.n_recv, n_local[0]) == COUNTS, (net.n_send, net.n_recv, n_local)
    w_last.wait_send()
    total_of(d_out.at[:, 0:256, :], k_send=kv_send).wait_send()
    for sent, k_send in ((dke, edge_send), (wg_r1, w1_send), (wg_r2, w2_send), (wf.at[0], fwd_send)):
        total_of(sent, k_send=k_send).wait_send()

    @pl.when(cell == 0)
    def _():
        @pl.when(ylo == 0)
        def _():
            for c in b_mate:
                c.wait_send()

        for c in b_to_x:
            c.wait_send()

    to_x_peers(lambda c: c.wait_send())

    @pl.when(z == 0)
    def _():
        total_of(d0_zr, k_send=b_send).wait_send()

        for d in range(1, NX):

            @pl.when(x == d)
            def _():
                d0_o[d - 1].wait_send()

    for d in range(1, NZ):

        @pl.when(z == d)
        def _():
            d0_z[d - 1].wait_send()


def hand_over_kernel(*refs):
    n = 5
    ins, outs, bufs, sem = refs[:n], refs[n : 2 * n], refs[2 * n : 3 * n], refs[3 * n]
    reads = [pltpu.make_async_copy(ins[i], bufs[i], sem.at[0, i]) for i in range(n)]
    writes = [pltpu.make_async_copy(bufs[i], outs[i], sem.at[1, i]) for i in range(n)]
    for c in reads:
        c.start()
    for i in range(n):
        reads[i].wait()
        writes[i].start()
    for c in writes:
        c.wait()


def anywhere(n):
    return [pl.BlockSpec(memory_space=pl.ANY)] * n


def local(queries, key_heads, value_heads, out_weight, block_lists, out_grad):
    results = (
        jax.ShapeDtypeStruct((256, 1024), BF),
        jax.ShapeDtypeStruct((256, 512), BF),
        jax.ShapeDtypeStruct((256, 512), BF),
        jax.ShapeDtypeStruct((256, 512), BF),
        jax.ShapeDtypeStruct((64, 512), F32),
    )
    b, f = (lambda *s: pltpu.VMEM(s, BF)), (lambda *s: pltpu.VMEM(s, F32))
    scratch = [
        pltpu.SMEM((3, 128), jnp.int32),
        b(512, 256),
        b(1536, 256),
        b(1536, 256),
        b(256, 256),
        b(NX, NZ, 128, 256),
        b(2, 4, 256, 1024),
        b(2, 4, 256, 1024),
        b(4, 8, 256, 128),
        f(8, 128, 1280),
        b(512, 256),
        b(512, 256),
        f(1536, 256),
        f(1536, 256),
        f(2, 128, 256),
        b(512, 256),
        b(4, 256, 1024),
        b(4, 256, 1024),
        b(2, 128, 1024),
        b(2, 256, 1024),
        b(256, 1024),
        b(8, 256, 128),
        b(8, 256, 128),
        b(2, 8, 256, 128),
        f(8, 256, 128),
        b(2, 4, 256, 128),
        b(2, 4, 256, 128),
        f(128, 256),
        b(2, 2, 2, 512, 128),
        b(2, 2, 2, 512, 128),
        b(256, 256),
        b(3, 64, 256),
        b(64, 256),
        b(7, 64, 256),
        b(64, 256),
        b(3, 64, 256),
        f(2, 512, 256),
        b(2, 512, 256),
        pltpu.SemaphoreType.DMA((N_SEND,)),
        pltpu.SemaphoreType.DMA((N_RECV,)),
        pltpu.SemaphoreType.DMA((N_LOCAL,)),
    ]
    outs = pl.pallas_call(
        layer_kernel,
        out_shape=results,
        in_specs=anywhere(6),
        out_specs=tuple(anywhere(5)),
        scratch_shapes=scratch,
        compiler_params=pltpu.CompilerParams(
            collective_id=0, has_side_effects=True, vmem_limit_bytes=60 * 1024 * 1024
        ),
        name="layer",
    )(queries, key_heads, value_heads, out_weight, block_lists.T, out_grad)
    return pl.pallas_call(
        hand_over_kernel,
        out_shape=results,
        in_specs=anywhere(5),
        out_specs=tuple(anywhere(5)),
        scratch_shapes=[pltpu.VMEM(r.shape, r.dtype) for r in results]
        + [pltpu.SemaphoreType.DMA((2, 5))],
        name="hand_over",
    )(*outs)


def solution(mesh):
    placed = P("ctx", "head")
    return jax.shard_map(
        local,
        mesh=mesh,
        in_specs=(placed, placed, placed, placed, P(), placed),
        out_specs=(placed,) * 5,
        check_vma=False,
    )
```

```python
import jax
import jax.numpy as jnp
from jax import lax
from jax.experimental import pallas as pl
from jax.experimental.pallas import tpu as pltpu
from jax.sharding import PartitionSpec as P

HD = 128
BLK = 128
SCALE = HD ** -0.5
BF = jnp.bfloat16
F32 = jnp.float32
NX, NZ, NY = 4, 8, 4
POOL = 64
COUNTS = N_SEND, N_RECV, N_LOCAL = 81, 122, 16


def place():
    i = lax.axis_index("ctx")
    h = lax.axis_index("head")
    cell = i // 2
    return cell // NZ, cell % NZ, (h // 2) * 2 + i % 2, h % 2, cell


def device(x, z, y, core):
    return ((x * NZ + z) * 2 + y % 2, (y // 2) * 2 + core)


def rows(start, size):
    return pl.ds(pl.multiple_of(start, size), size)


class Copies:
    def __init__(self, send, recv):
        self.send, self.recv = send, recv
        self.n_send, self.n_recv, self.live = POOL, 0, []

    def new_send(self):
        self.n_send += 1
        return self.n_send - 1

    def new_recv(self):
        self.n_recv += 1
        return self.n_recv - 1

    def numbers(self, k_send=None, k_recv=None):
        k_send = self.new_send() if k_send is None else k_send
        return k_send, self.new_recv() if k_recv is None else k_recv

    def make(self, src, dst, target, numbers=None):
        k_send, k_recv = numbers or self.numbers()
        return pltpu.make_async_remote_copy(
            src_ref=src,
            dst_ref=dst,
            send_sem=self.send.at[k_send],
            recv_sem=self.recv.at[k_recv],
            device_id=target,
            device_id_type=pl.DeviceIdType.MESH,
        )

    def start(self, src, dst, target, k_recv=None):
        k_send = len(self.live)
        if k_send == POOL:
            k_send, oldest = self.live.pop(0)
            oldest.wait_send()
        c = self.make(src, dst, target, self.numbers(k_send, k_recv))
        c.start()
        self.live.append((k_send, c))
        return c

    def drain(self):
        for _, c in self.live:
            c.wait_send()


def greet(peers):
    barrier = pltpu.get_barrier_semaphore()
    for peer in peers:
        pl.semaphore_signal(
            barrier, inc=1, device_id=peer, device_id_type=pl.DeviceIdType.MESH
        )
    pl.semaphore_wait(barrier, len(peers))


def all_peers(x, z, y, core, cell):
    up, down = (cell + 1) % (NX * NZ), (cell + NX * NZ - 1) % (NX * NZ)
    peers = [device((x + d) % NX, z, y, core) for d in range(1, NX)]
    peers += [device(x, (z + d) % NZ, y, core) for d in range(1, NZ)]
    peers += [device(x, z, (y + d) % NY, core) for d in (1, NY - 1)]
    peers += [device(x, z, y, 1 - core)]
    peers += [device(c // NZ, c % NZ, y, core) for c in (up, down)]
    return peers


def dot(a, b, dims=(((1,), (0,)), ((), ()))):
    return lax.dot_general(a, b, dims, preferred_element_type=F32)


NT = (((1,), (1,)), ((), ()))
TN = (((0,), (0,)), ((), ()))


def add(dst, *srcs):
    n, lanes = dst.shape
    step = min(n, 16384 // lanes)

    def body(i, carry):
        r = rows(step * i, step)
        total = srcs[0][r, :].astype(F32)
        for s in srcs[1:]:
            total = total + s[r, :].astype(F32)
        dst[r, :] = total.astype(dst.dtype)
        return carry

    lax.fori_loop(0, n // step, body, 0)


def layer_kernel(
    q, k, v, w, lists_hbm, og,
    o_at, o_dq, o_dk, o_dv, o_wg,
    lists, q2, kb, vb, b0, wf, ogf, at, wg, probs, mixed, mgrad, dk, dv, d0, dq,
    at_core, at_sum, at_r1, at_r2, at_o, wg_r1, wg_s, wg_r2, wg_x, wz_s, wz_r, w_out,
    dke, dk_r, d0_b, d0_xr, d0_s, d0_zr, d0_t, d0_q, dkv_s, d_out, send, recv, lsem,
):
    x, z, y, core, cell = place()
    ylo = y % 2
    h = (y // 2) * 2 + core
    x_up, x_dn, x_far = (x + 1) % NX, (x + NX - 1) % NX, (x + 2) % NX
    z_up, z_dn = (z + 1) % NZ, (z + NZ - 1) % NZ
    c_up, c_dn = (cell + 1) % (NX * NZ), (cell + NX * NZ - 1) % (NX * NZ)
    y_mate = y + 1 - 2 * ylo
    y_next = (y + NY - 1 + 2 * ylo) % NY
    y_far = (y + 2) % NY
    mate, nxt = device(x, z, y_mate, core), device(x, z, y_next, core)
    twin = device(x, z, y, 1 - core)
    xu, xd = device(x_up, z, y, core), device(x_dn, z, y, core)
    zu, zd = device(x, z_up, y, core), device(x, z_dn, y, core)
    cu, cd = device(c_up // NZ, c_up % NZ, y, core), device(c_dn // NZ, c_dn % NZ, y, core)
    net = Copies(send, recv)
    mine, other = rows(256 * ylo, 256), rows(256 * (1 - ylo), 256)
    band_mine, band_other = rows(512 + 256 * ylo, 256), rows(512 + 256 * (1 - ylo), 256)
    lo_mine, lo_other = mine, other
    hi_mine, hi_other = rows(1024 + 256 * ylo, 256), rows(1024 + 256 * (1 - ylo), 256)
    n_local = [0]

    def go(src, dst, target, k_recv=None):
        return net.start(src, dst, target, k_recv)

    def total_of(ref, k_recv=None, k_send=None):
        return net.make(ref, ref, mate, (k_send or 0, k_recv or 0))

    kv_send, edge_send, w1_send, w2_send, fwd_send, b_send = (net.new_send() for _ in range(6))
    k_halo, v_halo, d0x_recv, d0z_recv, d0o_recv = (net.new_recv() for _ in range(5))
    edge_recv = [[net.new_recv() for _ in range(2)] for _ in range(2)]

    def here(src, dst):
        c = pltpu.make_async_copy(src, dst, lsem.at[n_local[0]])
        n_local[0] += 1
        return c

    def here_now(src, dst):
        c = here(src, dst)
        c.start()
        return c

    w_loc = here_now(w.at[:, mine], wf.at[x, z, rows(64 * ylo, 64), :])
    k_loc = here_now(k.at[:, mine], kb.at[band_mine, :])
    v_loc = here_now(v.at[:, mine], vb.at[band_mine, :])
    og_loc = here_now(og, ogf.at[ylo, h])
    q_loc = here_now(q.at[:, mine], q2.at[mine, :])
    list_loc = here_now(lists_hbm, lists)
    greet(all_peers(x, z, y, core, cell))

    quarter = rows(64 * x, 64)
    b_mate = [
        net.make(k.at[0:BLK, other], b0.at[0:BLK, :], mate),
        net.make(v.at[0:BLK, other], b0.at[BLK : 2 * BLK, :], mate),
    ]
    b_loc = [
        here(k.at[0:BLK, mine], b0.at[0:BLK, :]),
        here(v.at[0:BLK, mine], b0.at[BLK : 2 * BLK, :]),
    ]
    b_to_x = [
        net.make(
            b0.at[rows(64 * ((x + d) % NX), 64), :],
            b0.at[rows(64 * ((x + d) % NX), 64), :],
            device((x + d) % NX, z, y, core),
        )
        for d in range(1, NX)
    ]
    b_along_z = [
        net.make(
            b0.at[quarter, :],
            b0.at[quarter, :],
            device(x, (z + d) % NZ, y, core),
            net.numbers(b_send),
        )
        for d in range(1, NZ)
    ]

    @pl.when((cell == 0) & (ylo == 0))
    def _():
        for c in b_mate + b_loc:
            c.start()

    w_mate = go(w.at[:, other], wf.at[x, z, rows(64 * ylo, 64), :], mate)
    k_mate = go(k.at[:, other], kb.at[band_mine, :], mate)
    v_mate = go(v.at[:, other], vb.at[band_mine, :], mate)
    og_next = go(og, ogf.at[ylo, h], nxt)
    half, cut = 160, 208
    og_here = ogf.at[ylo, h]
    og_mate = [go(og.at[0:half, :], og_here.at[0:half, :], mate)]
    q_mate = go(q.at[:, other], q2.at[mine, :], mate)
    og_mate.append(go(og.at[half:256, :], og_here.at[half:256, :], mate))
    og_tw = [go(og, og_here, twin)]

    own_half, mate_half = rows(64 * ylo, 64), rows(64 * (1 - ylo), 64)
    first = [go(w.at[:, mine], wf.at[x, z, own_half, :], t) for t in (zu, zd, xu, xd)]
    halo = [
        go(k.at[:, mine], kb.at[lo_mine, :], cu, k_halo),
        go(k.at[:, mine], kb.at[hi_mine, :], cd, k_halo),
    ]
    w_mate.wait_recv()
    w_loc.wait()

    x_plus, x_minus, x_fwd = {}, {}, []

    def to_x(off):
        zz = (z + off) % NZ
        x_plus[off] = go(wf.at[x, zz], wf.at[x, zz], xu)
        x_minus[off] = go(wf.at[x, zz], wf.at[x, zz], xd)

    def either(cond, fn, then, other):
        @pl.when(cond)
        def _():
            fn(then)

        @pl.when(jnp.logical_not(cond))
        def _():
            fn(other)

    def goes_up(is_up):
        return (z == 7) | (z != 0) if is_up else z == 7

    def pass_x(off):
        zz = (z + off) % NZ
        if off == 0:
            first[2].wait_recv()
            first[3].wait_recv()
        x_plus[off].wait_recv()
        x_minus[off].wait_recv()
        ks = net.numbers(fwd_send)
        pair = (
            goes_up(off in (0, 6, 2, 4)),
            net.make(wf.at[x_dn, zz], wf.at[x_dn, zz], xu, ks),
            net.make(wf.at[x_up, zz], wf.at[x_up, zz], xd, ks),
        )
        either(pair[0], lambda c: c.start(), pair[1], pair[2])
        x_fwd.append(pair)

    def ring_step(s, up, dn):
        zm, zp = (z + NZ - s) % NZ, (z + s) % NZ
        if s == 1:
            first[0].wait_recv()
            first[1].wait_recv()
        up.wait_recv()
        if s < 3:
            up = go(wf.at[x, zm], wf.at[x, zm], zu)
        else:
            up = go(wf.at[x, zm, 0:64, :], wf.at[x, zm, 0:64, :], zu)
        to_x(NZ - s)
        dn.wait_recv()
        if s < 3:
            dn = go(wf.at[x, zp], wf.at[x, zp], zd)
        else:
            dn = go(wf.at[x, zp, 64:128, :], wf.at[x, zp, 64:128, :], zd)
        to_x(s)
        return up, dn

    second = wf.at[x, z, mate_half, :]
    up = go(second, second, zu)
    dn = go(second, second, zd)
    x_plus[0] = go(second, second, xu)
    x_minus[0] = go(second, second, xd)

    @pl.when(cell == 0)
    def _():
        @pl.when(ylo == 0)
        def _():
            for c in b_loc:
                c.wait()

        @pl.when(ylo == 1)
        def _():
            for c in b_mate:
                c.wait_recv()

        for c in b_to_x:
            c.start()

    up, dn = ring_step(1, up, dn)

    @pl.when(z == 0)
    def _():
        for d in range(1, NX):

            @pl.when(x == d)
            def _():
                b_to_x[d - 1].wait_recv()

        for n in (3, 4, 2, 5, 1, 6, 0):
            b_along_z[n].start()

    halo += [
        go(v.at[:, mine], vb.at[lo_mine, :], cu, v_halo),
        go(v.at[:, mine], vb.at[hi_mine, :], cd, v_halo),
    ]
    k_mate.wait_recv()
    k_loc.wait()
    up, dn = ring_step(2, up, dn)
    halo += [
        go(kb.at[band_other, :], kb.at[lo_other, :], cu, k_halo),
        go(kb.at[band_other, :], kb.at[hi_other, :], cd, k_halo),
    ]
    pass_x(0)
    for d in range(1, NZ):

        @pl.when(z == d)
        def _():
            b_along_z[d - 1].wait_recv()

    b_along_x = [
        net.make(b0.at[quarter, :], b0.at[quarter, :], device((x + d) % NX, z, y, core))
        for d in range(1, NX)
    ]

    def to_x_peers(fn):
        for d in range(1, NX):

            @pl.when((z != 0) | ((x + d) % NX != 0))
            def _():
                fn(b_along_x[d - 1])

    to_x_peers(lambda c: c.start())

    v_mate.wait_recv()
    v_loc.wait()
    up, dn = ring_step(3, up, dn)
    halo += [
        go(vb.at[band_other, :], vb.at[lo_other, :], cu, v_halo),
        go(vb.at[band_other, :], vb.at[hi_other, :], cd, v_halo),
    ]
    from_mate = ogf.at[y_mate % 2, (y_mate // 2) * 2 + core]
    from_next = ogf.at[y_next % 2, (y_next // 2) * 2 + core]
    far = ogf.at[y_far % 2, (y_far // 2) * 2 + core]
    og_mate[0].wait_recv()
    fwd_next = [go(from_mate.at[0:half, :], from_mate.at[0:half, :], nxt)]
    og_tw.append(go(from_mate.at[0:half, :], from_mate.at[0:half, :], twin))
    og_next.wait_recv()
    fwd_mate = go(from_next.at[cut:256, :], from_next.at[cut:256, :], mate)
    og_tw.append(go(from_next, from_next, twin))
    pass_x(7)
    up.wait_recv()
    dn.wait_recv()
    to_x(4)
    pass_x(1)
    q_mate.wait_recv()
    q_loc.wait()
    list_loc.wait()

    @pl.when(cell != 0)
    def _():
        for d in range(1, NX):
            b_along_x[d - 1].wait_recv()

    total_of(kb.at[0:1024, :], k_halo).wait_recv()
    total_of(vb.at[0:1024, :], v_halo).wait_recv()

    def window(n):
        i, head = n % 4, n // 4
        return i, head, rows(128 * i, 128), pl.ds(pl.multiple_of(128 * i, 128), 1152), rows(128 * head, 128)

    def forward(n, carry):
        i, head, toks, win, lanes = window(n)
        b = 4 * cell + i
        bias = []
        for j in range(9):
            kbl = b - 4 + j
            good = (kbl >= 1) & (kbl <= 127)
            if j not in (3, 4, 5):
                named = (lists[0, b] == kbl) | (lists[1, b] == kbl) | (lists[2, b] == kbl)
                good = good & named
            bias.append(jnp.full((1, BLK), jnp.where(good, 0.0, -jnp.inf), F32))
        bias = jnp.concatenate(bias, axis=1)
        qq = q2[toks, lanes]
        s0 = dot(qq, b0[0:BLK, lanes], NT) * SCALE
        s1 = dot(qq, kb[win, lanes], NT) * SCALE + bias
        top = jnp.maximum(jnp.max(s0, axis=1, keepdims=True), jnp.max(s1, axis=1, keepdims=True))
        e0, e1 = jnp.exp(s0 - top), jnp.exp(s1 - top)
        inv = 1.0 / (jnp.sum(e0, axis=1, keepdims=True) + jnp.sum(e1, axis=1, keepdims=True))
        p0, p1 = e0 * inv, e1 * inv
        probs[n, :, 0:BLK] = p0
        probs[n, :, BLK:] = p1
        out = dot(p0.astype(BF), b0[BLK : 2 * BLK, lanes]) + dot(p1.astype(BF), vb[win, lanes])
        mixed[toks, lanes] = out.astype(BF)
        return carry

    lax.fori_loop(0, 1, forward, 0)
    pass_x(6)
    og_mate[1].wait_recv()
    fwd_next.append(go(from_mate.at[half:cut, :], from_mate.at[half:cut, :], nxt))
    og_tw.append(go(from_mate.at[half:256, :], from_mate.at[half:256, :], twin))
    pass_x(2)
    lax.fori_loop(1, 3, forward, 0)
    pass_x(5)
    pass_x(3)
    lax.fori_loop(3, 5, forward, 0)
    pass_x(4)
    fwd_mate.wait_recv()
    og_tw.append(go(far.at[cut:256, :], far.at[cut:256, :], twin))
    fwd_next[0].wait_recv()
    og_tw.append(go(far.at[0:half, :], far.at[0:half, :], twin))
    lax.fori_loop(5, 8, forward, 0)
    fwd_next[1].wait_recv()
    og_tw.append(go(far.at[half:cut, :], far.at[half:cut, :], twin))
    og_loc.wait()
    for c in og_tw:
        c.wait_recv()

    def weight_part(xx):
        total = dot(mixed[0:256, :], ogf[0, xx], TN) + dot(mixed[256:512, :], ogf[1, xx], TN)
        for n in range(8):
            wg[xx, n] = total[:, 128 * n : 128 * (n + 1)].astype(BF)

    def attended_part(t, c):
        hh = (t // 2) * 2 + c
        part = dot(mixed[rows(256 * (t % 2), 256), :], wf[hh].reshape(1024, 256), NT)
        at[t % 2, hh] = part.astype(BF)

    w1, w2u, w2d, w2_recv = {}, {}, {}, {}

    def piece(xx, off):
        return wg.at[xx, (z + off) % NZ]

    first_group, second_group = (4, 3, 5, 2), (6, 1, 7, 0)
    for off in first_group + second_group:
        ks = net.numbers(w1_send)
        ku = kd = net.numbers(w2_send)
        w2_recv[off] = ku[1]
        w1[off] = (
            goes_up(off >= 4),
            net.make(piece(x_far, off), wg_r1.at[off], xu, ks),
            net.make(piece(x_far, off), wg_r1.at[off], xd, ks),
        )
        w2u[off] = (
            net.make(piece(x_up, off), wg_r2.at[0, off], xu, ku),
            net.make(wg_s.at[off], wg_r2.at[0, off], xu, ku),
        )
        w2d[off] = (
            net.make(piece(x_dn, off), wg_r2.at[1, off], xd, kd),
            net.make(wg_s.at[off], wg_r2.at[1, off], xd, kd),
        )

    def either_way(off, up_way, down_way):
        pl.when(w1[off][0])(up_way)
        pl.when(jnp.logical_not(w1[off][0]))(down_way)

    def straight(off):
        either_way(off, w2d[off][0].start, w2u[off][0].start)

    def relay(off):
        def up_way():
            w1[off][1].wait_recv()
            add(wg_s.at[off], piece(x_up, off), wg_r1.at[off])
            w2u[off][1].start()

        def down_way():
            w1[off][2].wait_recv()
            add(wg_s.at[off], piece(x_dn, off), wg_r1.at[off])
            w2d[off][1].start()

        either_way(off, up_way, down_way)

    def backward(n, carry):
        i, head, toks, win, lanes = window(n)
        g = mgrad[toks, lanes]
        delta = jnp.sum(
            g.astype(F32) * mixed[toks, lanes].astype(F32), axis=1, keepdims=True
        )
        p0, p1 = probs[n, :, 0:BLK], probs[n, :, BLK:]
        sl0 = (p0 * (dot(g, b0[BLK : 2 * BLK, lanes], NT) - delta)).astype(BF)
        sl1 = (p1 * (dot(g, vb[win, lanes], NT) - delta)).astype(BF)
        out = dot(sl0, b0[0:BLK, lanes]) + dot(sl1, kb[win, lanes])
        dq[toks, lanes] = (out * SCALE).astype(BF)
        qq = q2[toks, lanes]
        dk[win, lanes] += dot(sl1, qq, TN)
        dv[win, lanes] += dot(p1.astype(BF), g, TN)
        d0[0, :, lanes] += dot(sl0, qq, TN)
        d0[1, :, lanes] += dot(p0.astype(BF), g, TN)
        return carry

    edges, q_out, locals_out = [[], []], [], []

    def leave(head, n):
        acc, factor = ((dk, SCALE), (dv, 1.0))[n]
        lanes = slice(128 * head, 128 * (head + 1))
        dke[head, n, 0] = (acc[0:512, lanes] * factor).astype(BF)
        dke[head, n, 1] = (acc[1024:1536, lanes] * factor).astype(BF)
        pair = (
            net.make(dke.at[head, n, 0], dk_r.at[head, n, 1], cd, (edge_send, edge_recv[head][n])),
            net.make(dke.at[head, n, 1], dk_r.at[head, n, 0], cu, (edge_send, edge_recv[head][n])),
        )
        edges[head] += pair
        pair[0].start()
        pair[1].start()

    def leave_q(head):
        lanes = slice(128 * head, 128 * (head + 1))
        cols = rows(256 * ylo + 128 * head, 128)
        q_out.append(go(dq.at[other, lanes], o_dq.at[:, cols], mate))
        locals_out.append(here_now(dq.at[mine, lanes], o_dq.at[:, cols]))

    def sum_x(off):
        total_of(wg_r2.at[:, off], w2_recv[off]).wait_recv()
        add(wg_x.at[off], piece(x, off), wg_r2.at[0, off], wg_r2.at[1, off])

    def z_step(s, up, dn):
        tu, td = 5 - s, 3 + s
        up.wait_recv()
        if s == 2:
            add(wz_s.at[0, 1, 0:128, :], wg_x.at[tu, 0:128, :], wz_r.at[0, 0, 0:128, :])
            add(wz_s.at[0, 1, 128:256, :], wg_x.at[tu, 128:256, :])
        else:
            add(wz_s.at[0, s - 1], wg_x.at[tu], wz_r.at[0, s - 2])
        up = go(wz_s.at[0, s - 1], wz_r.at[0, s - 1], zu)
        dn.wait_recv()
        if s == 2:
            add(wz_s.at[1, 1, 128:256, :], wg_x.at[td, 128:256, :], wz_r.at[1, 0, 128:256, :])
            add(wz_s.at[1, 1, 0:128, :], wg_x.at[td, 0:128, :])
        else:
            add(wz_s.at[1, s - 1], wg_x.at[td], wz_r.at[1, s - 2])
        dn = go(wz_s.at[1, s - 1], wz_r.at[1, s - 1], zd)
        return up, dn

    weight_part(x_far)
    for off in first_group + second_group:
        either_way(off, w1[off][1].start, w1[off][2].start)
    for pair in x_fwd:
        either(pair[0], lambda c: c.wait_recv(), pair[1], pair[2])
    order = (y_far, y_mate, y_next, y)
    cores = []
    for t in order:
        attended_part(t, 1 - core)
        cores.append(go(at.at[t % 2, (t // 2) * 2 + 1 - core], at_core.at[t], twin))
    weight_part(x_up)
    weight_part(x_dn)
    for off in first_group:
        straight(off)
    for t in range(2):
        total = jnp.zeros((256, 256), F32)
        for hh in range(4):
            total = total + dot(ogf[t, hh], wf[hh].reshape(1024, 256))
        mgrad[256 * t : 256 * (t + 1), :] = total.astype(BF)
    dk[...] = jnp.zeros_like(dk)
    dv[...] = jnp.zeros_like(dv)
    d0[...] = jnp.zeros_like(d0)
    lax.fori_loop(0, 4, backward, 0)
    leave(0, 0)
    leave(0, 1)
    leave_q(0)
    for off in first_group:
        relay(off)
    lax.fori_loop(4, 8, backward, 0)
    leave(1, 0)

    d0_b[0:BLK, :] = (d0[0] * SCALE).astype(BF)
    d0_b[BLK : 2 * BLK, :] = d0[1].astype(BF)
    d0_x = [
        go(
            d0_b.at[rows(64 * ((x + d) % NX), 64), :],
            d0_xr.at[d - 1],
            device((x + d) % NX, z, y, core),
            d0x_recv,
        )
        for d in range(1, NX)
    ]
    z_send, o_send = net.new_send(), net.new_send()
    d0_z = [
        net.make(d0_s, d0_zr.at[d - 1], device(x, 0, y, core), (z_send, d0z_recv))
        for d in range(1, NZ)
    ]
    d0_o = [
        net.make(d0_t, d0_q.at[d - 1], device(0, z, y, core), (o_send, d0o_recv))
        for d in range(1, NX)
    ]

    for off in second_group:
        straight(off)
    for t in order:
        attended_part(t, core)
    weight_part(x)
    for n, t in enumerate(order):
        cores[n].wait_recv()
        add(at_sum.at[t], at.at[t % 2, (t // 2) * 2 + core], at_core.at[t])
        if n == 0:
            a1n = go(at_sum.at[t, 0:128, :], at_r1.at[0], nxt)
            a1m = go(at_sum.at[t, 128:256, :], at_r1.at[1], mate)
        if n == 1:
            a2m = [go(at_sum.at[t, 128:256, :], at_r2.at[0, 128:256, :], mate)]
        if n == 2:
            a2n = [go(at_sum.at[t, 0:128, :], at_r2.at[1, 0:128, :], nxt)]
    for off in second_group:
        relay(off)

    sum_x(4)
    add(wz_s.at[0, 0, 0:128, :], wg_x.at[4, 0:128, :])
    up = go(wz_s.at[0, 0, 0:128, :], wz_r.at[0, 0, 0:128, :], zu)
    add(wz_s.at[1, 0, 128:256, :], wg_x.at[4, 128:256, :])
    dn = go(wz_s.at[1, 0, 128:256, :], wz_r.at[1, 0, 128:256, :], zd)
    leave_q(1)
    sum_x(3)
    sum_x(5)
    up, dn = z_step(2, up, dn)
    leave(1, 1)

    a1n.wait_recv()
    to_mate = at_core.at[0, 0:128, :]
    add(to_mate, at_sum.at[y_mate, 0:128, :], at_r1.at[0])
    a2m.append(go(to_mate, at_r2.at[0, 0:128, :], mate))
    a1m.wait_recv()
    to_next = at_core.at[1, 128:256, :]
    add(to_next, at_sum.at[y_next, 128:256, :], at_r1.at[1])
    a2n.append(go(to_next, at_r2.at[1, 128:256, :], nxt))

    sum_x(2)
    sum_x(6)
    up, dn = z_step(3, up, dn)

    kv_mate, kv_here = [[], []], [[], []]

    def finish(head, n):
        total_of(dk_r.at[head, n], edge_recv[head][n]).wait_recv()
        acc, factor = ((dk, SCALE), (dv, 1.0))[n]
        out = (o_dk, o_dv)[n]
        lanes = slice(128 * head, 128 * (head + 1))
        cols = rows(256 * ylo + 128 * head, 128)
        dkv_s[n, :, lanes] = (
            acc[512:1024, lanes] * factor
            + dk_r[head, n, 0].astype(F32)
            + dk_r[head, n, 1].astype(F32)
        )
        d_out[n, :, lanes] = dkv_s[n, :, lanes].astype(BF)
        for r in (0, BLK):
            src = d_out.at[n, rows(256 * (1 - ylo) + r, BLK), lanes]
            c = net.make(src, out.at[r : r + BLK, cols], mate, net.numbers(kv_send))
            kv_mate[head].append(c)
            if r == 0:
                pl.when((cell != 0) | (ylo == 0))(c.start)
            else:
                c.start()
        c = here(d_out.at[n, mine, lanes], out.at[:, cols])
        kv_here[head].append(c)
        pl.when(cell != 0)(c.start)

    total_of(d0_xr, d0x_recv).wait_recv()
    add(d0_s, d0_b.at[quarter, :], *[d0_xr.at[d] for d in range(3)])
    for d in range(1, NZ):

        @pl.when(z == d)
        def _():
            d0_z[d - 1].start()

    finish(0, 0)
    finish(0, 1)
    sum_x(1)
    sum_x(7)
    up, dn = z_step(4, up, dn)
    @pl.when(z == 0)
    def _():
        total_of(d0_zr, d0z_recv).wait_recv()
        add(d0_t, d0_s, *[d0_zr.at[d] for d in range(NZ - 1)])
        for d in range(1, NX):

            @pl.when(x == d)
            def _():
                d0_o[d - 1].start()

    sum_x(0)
    w_last = net.make(w_out.at[rows(64 * (1 - ylo), 64), :], o_wg.at[:, mine], mate)
    w_here = here(w_out.at[rows(64 * ylo, 64), :], o_wg.at[:, mine])
    locals_out.append(w_here)

    def last_sum():
        up.wait_recv()
        dn.wait_recv()
        add(wg_x.at[0], wg_x.at[0], wz_r.at[0, 3], wz_r.at[1, 3])
        w_out[...] = wg_x[0].T
        w_last.start()
        w_here.start()

    edge_row = (z == 0) | (z == NZ - 1)
    pl.when(edge_row)(last_sum)
    finish(1, 0)

    finish(1, 1)

    pl.when(jnp.logical_not(edge_row))(last_sum)

    @pl.when(cell == 0)
    def _():
        total_of(d0_q, d0o_recv).wait_recv()
        for m in range(4):
            part = d0_t[...] if m == 0 else d0_q[m - 1]
            dkv_s[m // 2, 64 * (m % 2) : 64 * (m % 2) + 64, :] += part.astype(F32)
        d_out[:, 0:BLK, :] = dkv_s[:, 0:BLK, :].astype(BF)

        @pl.when(ylo == 1)
        def _():
            for head in range(2):
                for c in kv_mate[head][0::2]:
                    c.start()

        for c in kv_here[0] + kv_here[1]:
            c.start()

    for c in a2m + a2n:
        c.wait_recv()
    add(at_o, at_sum.at[y], at_r2.at[0], at_r2.at[1])
    locals_out.append(here_now(at_o, o_at))

    for c in kv_mate[0] + kv_mate[1] + q_out + [w_last]:
        c.wait_recv()
    for c in locals_out + kv_here[0] + kv_here[1]:
        c.wait()
    net.drain()
    assert (net.n_send, net.n_recv, n_local[0]) == COUNTS, (net.n_send, net.n_recv, n_local)
    w_last.wait_send()
    total_of(d_out.at[:, 0:256, :], k_send=kv_send).wait_send()
    for sent, k_send in ((dke, edge_send), (wg_r1, w1_send), (wg_r2, w2_send), (wf.at[0], fwd_send)):
        total_of(sent, k_send=k_send).wait_send()

    @pl.when(cell == 0)
    def _():
        @pl.when(ylo == 0)
        def _():
            for c in b_mate:
                c.wait_send()

        for c in b_to_x:
            c.wait_send()

    to_x_peers(lambda c: c.wait_send())

    @pl.when(z == 0)
    def _():
        total_of(d0_zr, k_send=b_send).wait_send()

        for d in range(1, NX):

            @pl.when(x == d)
            def _():
                d0_o[d - 1].wait_send()

    for d in range(1, NZ):

        @pl.when(z == d)
        def _():
            d0_z[d - 1].wait_send()


def hand_over_kernel(*refs):
    n = 5
    ins, outs, bufs, sem = refs[:n], refs[n : 2 * n], refs[2 * n : 3 * n], refs[3 * n]
    reads = [pltpu.make_async_copy(ins[i], bufs[i], sem.at[0, i]) for i in range(n)]
    writes = [pltpu.make_async_copy(bufs[i], outs[i], sem.at[1, i]) for i in range(n)]
    for c in reads:
        c.start()
    for i in range(n):
        reads[i].wait()
        writes[i].start()
    for c in writes:
        c.wait()


def anywhere(n):
    return [pl.BlockSpec(memory_space=pl.ANY)] * n


def local(queries, key_heads, value_heads, out_weight, block_lists, out_grad):
    results = (
        jax.ShapeDtypeStruct((256, 1024), BF),
        jax.ShapeDtypeStruct((256, 512), BF),
        jax.ShapeDtypeStruct((256, 512), BF),
        jax.ShapeDtypeStruct((256, 512), BF),
        jax.ShapeDtypeStruct((64, 512), F32),
    )
    b, f = (lambda *s: pltpu.VMEM(s, BF)), (lambda *s: pltpu.VMEM(s, F32))
    scratch = [
        pltpu.SMEM((3, 128), jnp.int32),
        b(512, 256),
        b(1536, 256),
        b(1536, 256),
        b(256, 256),
        b(NX, NZ, 128, 256),
        b(2, 4, 256, 1024),
        b(2, 4, 256, 1024),
        b(4, 8, 256, 128),
        f(8, 128, 1280),
        b(512, 256),
        b(512, 256),
        f(1536, 256),
        f(1536, 256),
        f(2, 128, 256),
        b(512, 256),
        b(4, 256, 1024),
        b(4, 256, 1024),
        b(2, 128, 1024),
        b(2, 256, 1024),
        b(256, 1024),
        b(8, 256, 128),
        b(8, 256, 128),
        b(2, 8, 256, 128),
        f(8, 256, 128),
        b(2, 4, 256, 128),
        b(2, 4, 256, 128),
        f(128, 256),
        b(2, 2, 2, 512, 128),
        b(2, 2, 2, 512, 128),
        b(256, 256),
        b(3, 64, 256),
        b(64, 256),
        b(7, 64, 256),
        b(64, 256),
        b(3, 64, 256),
        f(2, 512, 256),
        b(2, 512, 256),
        pltpu.SemaphoreType.DMA((N_SEND,)),
        pltpu.SemaphoreType.DMA((N_RECV,)),
        pltpu.SemaphoreType.DMA((N_LOCAL,)),
    ]
    outs = pl.pallas_call(
        layer_kernel,
        out_shape=results,
        in_specs=anywhere(6),
        out_specs=tuple(anywhere(5)),
        scratch_shapes=scratch,
        compiler_params=pltpu.CompilerParams(
            collective_id=0, has_side_effects=True, vmem_limit_bytes=60 * 1024 * 1024
        ),
        name="layer",
    )(queries, key_heads, value_heads, out_weight, block_lists.T, out_grad)
    return pl.pallas_call(
        hand_over_kernel,
        out_shape=results,
        in_specs=anywhere(5),
        out_specs=tuple(anywhere(5)),
        scratch_shapes=[pltpu.VMEM(r.shape, r.dtype) for r in results]
        + [pltpu.SemaphoreType.DMA((2, 5))],
        name="hand_over",
    )(*outs)


def solution(mesh):
    placed = P("ctx", "head")
    return jax.shard_map(
        local,
        mesh=mesh,
        in_specs=(placed, placed, placed, placed, P(), placed),
        out_specs=(placed,) * 5,
        check_vma=False,
    )
```

```python
import jax
import jax.numpy as jnp
from jax import lax
from jax.experimental import pallas as pl
from jax.experimental.pallas import tpu as pltpu
from jax.sharding import PartitionSpec as P

HD = 128
BLK = 128
SCALE = HD ** -0.5
BF = jnp.bfloat16
F32 = jnp.float32
NX, NZ, NY = 4, 8, 4
POOL = 64
COUNTS = N_SEND, N_RECV, N_LOCAL = 81, 122, 16


def place():
    i = lax.axis_index("ctx")
    h = lax.axis_index("head")
    cell = i // 2
    return cell // NZ, cell % NZ, (h // 2) * 2 + i % 2, h % 2, cell


def device(x, z, y, core):
    return ((x * NZ + z) * 2 + y % 2, (y // 2) * 2 + core)


def rows(start, size):
    return pl.ds(pl.multiple_of(start, size), size)


class Copies:
    def __init__(self, send, recv):
        self.send, self.recv = send, recv
        self.n_send, self.n_recv, self.live = POOL, 0, []

    def new_send(self):
        self.n_send += 1
        return self.n_send - 1

    def new_recv(self):
        self.n_recv += 1
        return self.n_recv - 1

    def numbers(self, k_send=None, k_recv=None):
        k_send = self.new_send() if k_send is None else k_send
        return k_send, self.new_recv() if k_recv is None else k_recv

    def make(self, src, dst, target, numbers=None):
        k_send, k_recv = numbers or self.numbers()
        return pltpu.make_async_remote_copy(
            src_ref=src,
            dst_ref=dst,
            send_sem=self.send.at[k_send],
            recv_sem=self.recv.at[k_recv],
            device_id=target,
            device_id_type=pl.DeviceIdType.MESH,
        )

    def start(self, src, dst, target, k_recv=None):
        k_send = len(self.live)
        if k_send == POOL:
            k_send, oldest = self.live.pop(0)
            oldest.wait_send()
        c = self.make(src, dst, target, self.numbers(k_send, k_recv))
        c.start()
        self.live.append((k_send, c))
        return c

    def drain(self):
        for _, c in self.live:
            c.wait_send()


def greet(peers):
    barrier = pltpu.get_barrier_semaphore()
    for peer in peers:
        pl.semaphore_signal(
            barrier, inc=1, device_id=peer, device_id_type=pl.DeviceIdType.MESH
        )
    pl.semaphore_wait(barrier, len(peers))


def all_peers(x, z, y, core, cell):
    up, down = (cell + 1) % (NX * NZ), (cell + NX * NZ - 1) % (NX * NZ)
    peers = [device((x + d) % NX, z, y, core) for d in range(1, NX)]
    peers += [device(x, (z + d) % NZ, y, core) for d in range(1, NZ)]
    peers += [device(x, z, (y + d) % NY, core) for d in (1, NY - 1)]
    peers += [device(x, z, y, 1 - core)]
    peers += [device(c // NZ, c % NZ, y, core) for c in (up, down)]
    return peers


def dot(a, b, dims=(((1,), (0,)), ((), ()))):
    return lax.dot_general(a, b, dims, preferred_element_type=F32)


NT = (((1,), (1,)), ((), ()))
TN = (((0,), (0,)), ((), ()))


def add(dst, *srcs):
    n, lanes = dst.shape
    step = min(n, 16384 // lanes)

    def body(i, carry):
        r = rows(step * i, step)
        total = srcs[0][r, :].astype(F32)
        for s in srcs[1:]:
            total = total + s[r, :].astype(F32)
        dst[r, :] = total.astype(dst.dtype)
        return carry

    lax.fori_loop(0, n // step, body, 0)


def layer_kernel(
    q, k, v, w, lists_hbm, og,
    o_at, o_dq, o_dk, o_dv, o_wg,
    lists, q2, kb, vb, b0, wf, ogf, at, wg, probs, mixed, mgrad, dk, dv, d0, dq,
    at_core, at_sum, at_r1, at_r2, at_o, wg_r1, wg_s, wg_r2, wg_x, wz_s, wz_r, w_out,
    dke, dk_r, d0_b, d0_xr, d0_s, d0_zr, d0_t, d0_q, dkv_s, d_out, send, recv, lsem,
):
    x, z, y, core, cell = place()
    ylo = y % 2
    h = (y // 2) * 2 + core
    x_up, x_dn, x_far = (x + 1) % NX, (x + NX - 1) % NX, (x + 2) % NX
    z_up, z_dn = (z + 1) % NZ, (z + NZ - 1) % NZ
    c_up, c_dn = (cell + 1) % (NX * NZ), (cell + NX * NZ - 1) % (NX * NZ)
    y_mate = y + 1 - 2 * ylo
    y_next = (y + NY - 1 + 2 * ylo) % NY
    y_far = (y + 2) % NY
    mate, nxt = device(x, z, y_mate, core), device(x, z, y_next, core)
    twin = device(x, z, y, 1 - core)
    xu, xd = device(x_up, z, y, core), device(x_dn, z, y, core)
    zu, zd = device(x, z_up, y, core), device(x, z_dn, y, core)
    cu, cd = device(c_up // NZ, c_up % NZ, y, core), device(c_dn // NZ, c_dn % NZ, y, core)
    net = Copies(send, recv)
    mine, other = rows(256 * ylo, 256), rows(256 * (1 - ylo), 256)
    band_mine, band_other = rows(512 + 256 * ylo, 256), rows(512 + 256 * (1 - ylo), 256)
    lo_mine, lo_other = mine, other
    hi_mine, hi_other = rows(1024 + 256 * ylo, 256), rows(1024 + 256 * (1 - ylo), 256)
    n_local = [0]

    def go(src, dst, target, k_recv=None):
        return net.start(src, dst, target, k_recv)

    def total_of(ref, k_recv=None, k_send=None):
        return net.make(ref, ref, mate, (k_send or 0, k_recv or 0))

    kv_send, edge_send, w1_send, w2_send, fwd_send, b_send = (net.new_send() for _ in range(6))
    k_halo, v_halo, d0x_recv, d0z_recv, d0o_recv = (net.new_recv() for _ in range(5))
    edge_recv = [[net.new_recv() for _ in range(2)] for _ in range(2)]

    def here(src, dst):
        c = pltpu.make_async_copy(src, dst, lsem.at[n_local[0]])
        n_local[0] += 1
        return c

    def here_now(src, dst):
        c = here(src, dst)
        c.start()
        return c

    w_loc = here_now(w.at[:, mine], wf.at[x, z, rows(64 * ylo, 64), :])
    k_loc = here_now(k.at[:, mine], kb.at[band_mine, :])
    v_loc = here_now(v.at[:, mine], vb.at[band_mine, :])
    og_loc = here_now(og, ogf.at[ylo, h])
    q_loc = here_now(q.at[:, mine], q2.at[mine, :])
    list_loc = here_now(lists_hbm, lists)
    greet(all_peers(x, z, y, core, cell))

    quarter = rows(64 * x, 64)
    b_mate = [
        net.make(k.at[0:BLK, other], b0.at[0:BLK, :], mate),
        net.make(v.at[0:BLK, other], b0.at[BLK : 2 * BLK, :], mate),
    ]
    b_loc = [
        here(k.at[0:BLK, mine], b0.at[0:BLK, :]),
        here(v.at[0:BLK, mine], b0.at[BLK : 2 * BLK, :]),
    ]
    b_to_x = [
        net.make(
            b0.at[rows(64 * ((x + d) % NX), 64), :],
            b0.at[rows(64 * ((x + d) % NX), 64), :],
            device((x + d) % NX, z, y, core),
        )
        for d in range(1, NX)
    ]
    b_along_z = [
        net.make(
            b0.at[quarter, :],
            b0.at[quarter, :],
            device(x, (z + d) % NZ, y, core),
            net.numbers(b_send),
        )
        for d in range(1, NZ)
    ]

    @pl.when((cell == 0) & (ylo == 0))
    def _():
        for c in b_mate + b_loc:
            c.start()

    w_mate = go(w.at[:, other], wf.at[x, z, rows(64 * ylo, 64), :], mate)
    k_mate = go(k.at[:, other], kb.at[band_mine, :], mate)
    v_mate = go(v.at[:, other], vb.at[band_mine, :], mate)
    og_next = go(og, ogf.at[ylo, h], nxt)
    half, cut = 176, 208
    og_here = ogf.at[ylo, h]
    og_mate = [go(og.at[0:half, :], og_here.at[0:half, :], mate)]
    q_mate = go(q.at[:, other], q2.at[mine, :], mate)
    og_mate.append(go(og.at[half:256, :], og_here.at[half:256, :], mate))
    og_tw = [go(og, og_here, twin)]

    own_half, mate_half = rows(64 * ylo, 64), rows(64 * (1 - ylo), 64)
    first = [go(w.at[:, mine], wf.at[x, z, own_half, :], t) for t in (zu, zd, xu, xd)]
    halo = [
        go(k.at[:, mine], kb.at[lo_mine, :], cu, k_halo),
        go(k.at[:, mine], kb.at[hi_mine, :], cd, k_halo),
    ]
    w_mate.wait_recv()
    w_loc.wait()

    x_plus, x_minus, x_fwd = {}, {}, []

    def to_x(off):
        zz = (z + off) % NZ
        x_plus[off] = go(wf.at[x, zz], wf.at[x, zz], xu)
        x_minus[off] = go(wf.at[x, zz], wf.at[x, zz], xd)

    def either(cond, fn, then, other):
        @pl.when(cond)
        def _():
            fn(then)

        @pl.when(jnp.logical_not(cond))
        def _():
            fn(other)

    def goes_up(is_up):
        return (z == 7) | (z != 0) if is_up else z == 7

    def pass_x(off):
        zz = (z + off) % NZ
        if off == 0:
            first[2].wait_recv()
            first[3].wait_recv()
        x_plus[off].wait_recv()
        x_minus[off].wait_recv()
        ks = net.numbers(fwd_send)
        pair = (
            goes_up(off in (0, 6, 2, 4)),
            net.make(wf.at[x_dn, zz], wf.at[x_dn, zz], xu, ks),
            net.make(wf.at[x_up, zz], wf.at[x_up, zz], xd, ks),
        )
        either(pair[0], lambda c: c.start(), pair[1], pair[2])
        x_fwd.append(pair)

    def ring_step(s, up, dn):
        zm, zp = (z + NZ - s) % NZ, (z + s) % NZ
        if s == 1:
            first[0].wait_recv()
            first[1].wait_recv()
        up.wait_recv()
        if s < 3:
            up = go(wf.at[x, zm], wf.at[x, zm], zu)
        else:
            up = go(wf.at[x, zm, 0:64, :], wf.at[x, zm, 0:64, :], zu)
        to_x(NZ - s)
        dn.wait_recv()
        if s < 3:
            dn = go(wf.at[x, zp], wf.at[x, zp], zd)
        else:
            dn = go(wf.at[x, zp, 64:128, :], wf.at[x, zp, 64:128, :], zd)
        to_x(s)
        return up, dn

    second = wf.at[x, z, mate_half, :]
    up = go(second, second, zu)
    dn = go(second, second, zd)
    x_plus[0] = go(second, second, xu)
    x_minus[0] = go(second, second, xd)

    @pl.when(cell == 0)
    def _():
        @pl.when(ylo == 0)
        def _():
            for c in b_loc:
                c.wait()

        @pl.when(ylo == 1)
        def _():
            for c in b_mate:
                c.wait_recv()

        for c in b_to_x:
            c.start()

    up, dn = ring_step(1, up, dn)

    @pl.when(z == 0)
    def _():
        for d in range(1, NX):

            @pl.when(x == d)
            def _():
                b_to_x[d - 1].wait_recv()

        for n in (3, 4, 2, 5, 1, 6, 0):
            b_along_z[n].start()

    halo += [
        go(v.at[:, mine], vb.at[lo_mine, :], cu, v_halo),
        go(v.at[:, mine], vb.at[hi_mine, :], cd, v_halo),
    ]
    k_mate.wait_recv()
    k_loc.wait()
    up, dn = ring_step(2, up, dn)
    halo += [
        go(kb.at[band_other, :], kb.at[lo_other, :], cu, k_halo),
        go(kb.at[band_other, :], kb.at[hi_other, :], cd, k_halo),
    ]
    pass_x(0)
    for d in range(1, NZ):

        @pl.when(z == d)
        def _():
            b_along_z[d - 1].wait_recv()

    b_along_x = [
        net.make(b0.at[quarter, :], b0.at[quarter, :], device((x + d) % NX, z, y, core))
        for d in range(1, NX)
    ]

    def to_x_peers(fn):
        for d in range(1, NX):

            @pl.when((z != 0) | ((x + d) % NX != 0))
            def _():
                fn(b_along_x[d - 1])

    to_x_peers(lambda c: c.start())

    v_mate.wait_recv()
    v_loc.wait()
    up, dn = ring_step(3, up, dn)
    halo += [
        go(vb.at[band_other, :], vb.at[lo_other, :], cu, v_halo),
        go(vb.at[band_other, :], vb.at[hi_other, :], cd, v_halo),
    ]
    from_mate = ogf.at[y_mate % 2, (y_mate // 2) * 2 + core]
    from_next = ogf.at[y_next % 2, (y_next // 2) * 2 + core]
    far = ogf.at[y_far % 2, (y_far // 2) * 2 + core]
    og_mate[0].wait_recv()
    fwd_next = [go(from_mate.at[0:half, :], from_mate.at[0:half, :], nxt)]
    og_tw.append(go(from_mate.at[0:half, :], from_mate.at[0:half, :], twin))
    og_next.wait_recv()
    fwd_mate = go(from_next.at[cut:256, :], from_next.at[cut:256, :], mate)
    og_tw.append(go(from_next, from_next, twin))
    pass_x(7)
    up.wait_recv()
    dn.wait_recv()
    to_x(4)
    pass_x(1)
    q_mate.wait_recv()
    q_loc.wait()
    list_loc.wait()

    @pl.when(cell != 0)
    def _():
        for d in range(1, NX):
            b_along_x[d - 1].wait_recv()

    total_of(kb.at[0:1024, :], k_halo).wait_recv()
    total_of(vb.at[0:1024, :], v_halo).wait_recv()

    def window(n):
        i, head = n % 4, n // 4
        return i, head, rows(128 * i, 128), pl.ds(pl.multiple_of(128 * i, 128), 1152), rows(128 * head, 128)

    def forward(n, carry):
        i, head, toks, win, lanes = window(n)
        b = 4 * cell + i
        bias = []
        for j in range(9):
            kbl = b - 4 + j
            good = (kbl >= 1) & (kbl <= 127)
            if j not in (3, 4, 5):
                named = (lists[0, b] == kbl) | (lists[1, b] == kbl) | (lists[2, b] == kbl)
                good = good & named
            bias.append(jnp.full((1, BLK), jnp.where(good, 0.0, -jnp.inf), F32))
        bias = jnp.concatenate(bias, axis=1)
        qq = q2[toks, lanes]
        s0 = dot(qq, b0[0:BLK, lanes], NT) * SCALE
        s1 = dot(qq, kb[win, lanes], NT) * SCALE + bias
        top = jnp.maximum(jnp.max(s0, axis=1, keepdims=True), jnp.max(s1, axis=1, keepdims=True))
        e0, e1 = jnp.exp(s0 - top), jnp.exp(s1 - top)
        inv = 1.0 / (jnp.sum(e0, axis=1, keepdims=True) + jnp.sum(e1, axis=1, keepdims=True))
        p0, p1 = e0 * inv, e1 * inv
        probs[n, :, 0:BLK] = p0
        probs[n, :, BLK:] = p1
        out = dot(p0.astype(BF), b0[BLK : 2 * BLK, lanes]) + dot(p1.astype(BF), vb[win, lanes])
        mixed[toks, lanes] = out.astype(BF)
        return carry

    lax.fori_loop(0, 1, forward, 0)
    pass_x(6)
    og_mate[1].wait_recv()
    fwd_next.append(go(from_mate.at[half:cut, :], from_mate.at[half:cut, :], nxt))
    og_tw.append(go(from_mate.at[half:256, :], from_mate.at[half:256, :], twin))
    pass_x(2)
    lax.fori_loop(1, 3, forward, 0)
    pass_x(5)
    pass_x(3)
    lax.fori_loop(3, 5, forward, 0)
    pass_x(4)
    fwd_mate.wait_recv()
    og_tw.append(go(far.at[cut:256, :], far.at[cut:256, :], twin))
    fwd_next[0].wait_recv()
    og_tw.append(go(far.at[0:half, :], far.at[0:half, :], twin))
    lax.fori_loop(5, 8, forward, 0)
    fwd_next[1].wait_recv()
    og_tw.append(go(far.at[half:cut, :], far.at[half:cut, :], twin))
    og_loc.wait()
    for c in og_tw:
        c.wait_recv()

    def weight_part(xx):
        total = dot(mixed[0:256, :], ogf[0, xx], TN) + dot(mixed[256:512, :], ogf[1, xx], TN)
        for n in range(8):
            wg[xx, n] = total[:, 128 * n : 128 * (n + 1)].astype(BF)

    def attended_part(t, c):
        hh = (t // 2) * 2 + c
        part = dot(mixed[rows(256 * (t % 2), 256), :], wf[hh].reshape(1024, 256), NT)
        at[t % 2, hh] = part.astype(BF)

    w1, w2u, w2d, w2_recv = {}, {}, {}, {}

    def piece(xx, off):
        return wg.at[xx, (z + off) % NZ]

    first_group, second_group = (4, 3, 5, 2), (6, 1, 7, 0)
    for off in first_group + second_group:
        ks = net.numbers(w1_send)
        ku = kd = net.numbers(w2_send)
        w2_recv[off] = ku[1]
        w1[off] = (
            goes_up(off >= 4),
            net.make(piece(x_far, off), wg_r1.at[off], xu, ks),
            net.make(piece(x_far, off), wg_r1.at[off], xd, ks),
        )
        w2u[off] = (
            net.make(piece(x_up, off), wg_r2.at[0, off], xu, ku),
            net.make(wg_s.at[off], wg_r2.at[0, off], xu, ku),
        )
        w2d[off] = (
            net.make(piece(x_dn, off), wg_r2.at[1, off], xd, kd),
            net.make(wg_s.at[off], wg_r2.at[1, off], xd, kd),
        )

    def either_way(off, up_way, down_way):
        pl.when(w1[off][0])(up_way)
        pl.when(jnp.logical_not(w1[off][0]))(down_way)

    def straight(off):
        either_way(off, w2d[off][0].start, w2u[off][0].start)

    def relay(off):
        def up_way():
            w1[off][1].wait_recv()
            add(wg_s.at[off], piece(x_up, off), wg_r1.at[off])
            w2u[off][1].start()

        def down_way():
            w1[off][2].wait_recv()
            add(wg_s.at[off], piece(x_dn, off), wg_r1.at[off])
            w2d[off][1].start()

        either_way(off, up_way, down_way)

    def backward(n, carry):
        i, head, toks, win, lanes = window(n)
        g = mgrad[toks, lanes]
        delta = jnp.sum(
            g.astype(F32) * mixed[toks, lanes].astype(F32), axis=1, keepdims=True
        )
        p0, p1 = probs[n, :, 0:BLK], probs[n, :, BLK:]
        sl0 = (p0 * (dot(g, b0[BLK : 2 * BLK, lanes], NT) - delta)).astype(BF)
        sl1 = (p1 * (dot(g, vb[win, lanes], NT) - delta)).astype(BF)
        out = dot(sl0, b0[0:BLK, lanes]) + dot(sl1, kb[win, lanes])
        dq[toks, lanes] = (out * SCALE).astype(BF)
        qq = q2[toks, lanes]
        dk[win, lanes] += dot(sl1, qq, TN)
        dv[win, lanes] += dot(p1.astype(BF), g, TN)
        d0[0, :, lanes] += dot(sl0, qq, TN)
        d0[1, :, lanes] += dot(p0.astype(BF), g, TN)
        return carry

    edges, q_out, locals_out = [[], []], [], []

    def leave(head, n):
        acc, factor = ((dk, SCALE), (dv, 1.0))[n]
        lanes = slice(128 * head, 128 * (head + 1))
        dke[head, n, 0] = (acc[0:512, lanes] * factor).astype(BF)
        dke[head, n, 1] = (acc[1024:1536, lanes] * factor).astype(BF)
        pair = (
            net.make(dke.at[head, n, 0], dk_r.at[head, n, 1], cd, (edge_send, edge_recv[head][n])),
            net.make(dke.at[head, n, 1], dk_r.at[head, n, 0], cu, (edge_send, edge_recv[head][n])),
        )
        edges[head] += pair
        pair[0].start()
        pair[1].start()

    def leave_q(head):
        lanes = slice(128 * head, 128 * (head + 1))
        cols = rows(256 * ylo + 128 * head, 128)
        q_out.append(go(dq.at[other, lanes], o_dq.at[:, cols], mate))
        locals_out.append(here_now(dq.at[mine, lanes], o_dq.at[:, cols]))

    def sum_x(off):
        total_of(wg_r2.at[:, off], w2_recv[off]).wait_recv()
        add(wg_x.at[off], piece(x, off), wg_r2.at[0, off], wg_r2.at[1, off])

    def z_step(s, up, dn):
        tu, td = 5 - s, 3 + s
        up.wait_recv()
        if s == 2:
            add(wz_s.at[0, 1, 0:128, :], wg_x.at[tu, 0:128, :], wz_r.at[0, 0, 0:128, :])
            add(wz_s.at[0, 1, 128:256, :], wg_x.at[tu, 128:256, :])
        else:
            add(wz_s.at[0, s - 1], wg_x.at[tu], wz_r.at[0, s - 2])
        up = go(wz_s.at[0, s - 1], wz_r.at[0, s - 1], zu)
        dn.wait_recv()
        if s == 2:
            add(wz_s.at[1, 1, 128:256, :], wg_x.at[td, 128:256, :], wz_r.at[1, 0, 128:256, :])
            add(wz_s.at[1, 1, 0:128, :], wg_x.at[td, 0:128, :])
        else:
            add(wz_s.at[1, s - 1], wg_x.at[td], wz_r.at[1, s - 2])
        dn = go(wz_s.at[1, s - 1], wz_r.at[1, s - 1], zd)
        return up, dn

    weight_part(x_far)
    for off in first_group + second_group:
        either_way(off, w1[off][1].start, w1[off][2].start)
    for pair in x_fwd:
        either(pair[0], lambda c: c.wait_recv(), pair[1], pair[2])
    order = (y_far, y_mate, y_next, y)
    cores = []
    for t in order:
        attended_part(t, 1 - core)
        cores.append(go(at.at[t % 2, (t // 2) * 2 + 1 - core], at_core.at[t], twin))
    weight_part(x_up)
    weight_part(x_dn)
    for off in first_group:
        straight(off)
    for t in range(2):
        total = jnp.zeros((256, 256), F32)
        for hh in range(4):
            total = total + dot(ogf[t, hh], wf[hh].reshape(1024, 256))
        mgrad[256 * t : 256 * (t + 1), :] = total.astype(BF)
    dk[...] = jnp.zeros_like(dk)
    dv[...] = jnp.zeros_like(dv)
    d0[...] = jnp.zeros_like(d0)
    lax.fori_loop(0, 4, backward, 0)
    leave(0, 0)
    leave(0, 1)
    leave_q(0)
    for off in first_group:
        relay(off)
    lax.fori_loop(4, 8, backward, 0)
    leave(1, 0)

    d0_b[0:BLK, :] = (d0[0] * SCALE).astype(BF)
    d0_b[BLK : 2 * BLK, :] = d0[1].astype(BF)
    d0_x = [
        go(
            d0_b.at[rows(64 * ((x + d) % NX), 64), :],
            d0_xr.at[d - 1],
            device((x + d) % NX, z, y, core),
            d0x_recv,
        )
        for d in range(1, NX)
    ]
    z_send, o_send = net.new_send(), net.new_send()
    d0_z = [
        net.make(d0_s, d0_zr.at[d - 1], device(x, 0, y, core), (z_send, d0z_recv))
        for d in range(1, NZ)
    ]
    d0_o = [
        net.make(d0_t, d0_q.at[d - 1], device(0, z, y, core), (o_send, d0o_recv))
        for d in range(1, NX)
    ]

    for off in second_group:
        straight(off)
    for t in order:
        attended_part(t, core)
    weight_part(x)
    for n, t in enumerate(order):
        cores[n].wait_recv()
        add(at_sum.at[t], at.at[t % 2, (t // 2) * 2 + core], at_core.at[t])
        if n == 0:
            a1n = go(at_sum.at[t, 0:128, :], at_r1.at[0], nxt)
            a1m = go(at_sum.at[t, 128:256, :], at_r1.at[1], mate)
        if n == 1:
            a2m = [go(at_sum.at[t, 128:256, :], at_r2.at[0, 128:256, :], mate)]
        if n == 2:
            a2n = [go(at_sum.at[t, 0:128, :], at_r2.at[1, 0:128, :], nxt)]
    for off in second_group:
        relay(off)

    sum_x(4)
    add(wz_s.at[0, 0, 0:128, :], wg_x.at[4, 0:128, :])
    up = go(wz_s.at[0, 0, 0:128, :], wz_r.at[0, 0, 0:128, :], zu)
    add(wz_s.at[1, 0, 128:256, :], wg_x.at[4, 128:256, :])
    dn = go(wz_s.at[1, 0, 128:256, :], wz_r.at[1, 0, 128:256, :], zd)
    leave_q(1)
    sum_x(3)
    sum_x(5)
    up, dn = z_step(2, up, dn)
    leave(1, 1)

    a1n.wait_recv()
    to_mate = at_core.at[0, 0:128, :]
    add(to_mate, at_sum.at[y_mate, 0:128, :], at_r1.at[0])
    a2m.append(go(to_mate, at_r2.at[0, 0:128, :], mate))
    a1m.wait_recv()
    to_next = at_core.at[1, 128:256, :]
    add(to_next, at_sum.at[y_next, 128:256, :], at_r1.at[1])
    a2n.append(go(to_next, at_r2.at[1, 128:256, :], nxt))

    sum_x(2)
    sum_x(6)
    up, dn = z_step(3, up, dn)

    kv_mate, kv_here = [[], []], [[], []]

    def finish(head, n):
        total_of(dk_r.at[head, n], edge_recv[head][n]).wait_recv()
        acc, factor = ((dk, SCALE), (dv, 1.0))[n]
        out = (o_dk, o_dv)[n]
        lanes = slice(128 * head, 128 * (head + 1))
        cols = rows(256 * ylo + 128 * head, 128)
        dkv_s[n, :, lanes] = (
            acc[512:1024, lanes] * factor
            + dk_r[head, n, 0].astype(F32)
            + dk_r[head, n, 1].astype(F32)
        )
        d_out[n, :, lanes] = dkv_s[n, :, lanes].astype(BF)
        for r in (0, BLK):
            src = d_out.at[n, rows(256 * (1 - ylo) + r, BLK), lanes]
            c = net.make(src, out.at[r : r + BLK, cols], mate, net.numbers(kv_send))
            kv_mate[head].append(c)
            if r == 0:
                pl.when((cell != 0) | (ylo == 0))(c.start)
            else:
                c.start()
        c = here(d_out.at[n, mine, lanes], out.at[:, cols])
        kv_here[head].append(c)
        pl.when(cell != 0)(c.start)

    total_of(d0_xr, d0x_recv).wait_recv()
    add(d0_s, d0_b.at[quarter, :], *[d0_xr.at[d] for d in range(3)])
    for d in range(1, NZ):

        @pl.when(z == d)
        def _():
            d0_z[d - 1].start()

    finish(0, 0)
    finish(0, 1)
    sum_x(1)
    sum_x(7)
    up, dn = z_step(4, up, dn)
    @pl.when(z == 0)
    def _():
        total_of(d0_zr, d0z_recv).wait_recv()
        add(d0_t, d0_s, *[d0_zr.at[d] for d in range(NZ - 1)])
        for d in range(1, NX):

            @pl.when(x == d)
            def _():
                d0_o[d - 1].start()

    sum_x(0)
    w_last = net.make(w_out.at[rows(64 * (1 - ylo), 64), :], o_wg.at[:, mine], mate)
    w_here = here(w_out.at[rows(64 * ylo, 64), :], o_wg.at[:, mine])
    locals_out.append(w_here)

    def last_sum():
        up.wait_recv()
        dn.wait_recv()
        add(wg_x.at[0], wg_x.at[0], wz_r.at[0, 3], wz_r.at[1, 3])
        w_out[...] = wg_x[0].T
        w_last.start()
        w_here.start()

    edge_row = (z == 0) | (z == NZ - 1)
    pl.when(edge_row)(last_sum)
    finish(1, 0)

    finish(1, 1)

    pl.when(jnp.logical_not(edge_row))(last_sum)

    @pl.when(cell == 0)
    def _():
        total_of(d0_q, d0o_recv).wait_recv()
        for m in range(4):
            part = d0_t[...] if m == 0 else d0_q[m - 1]
            dkv_s[m // 2, 64 * (m % 2) : 64 * (m % 2) + 64, :] += part.astype(F32)
        d_out[:, 0:BLK, :] = dkv_s[:, 0:BLK, :].astype(BF)

        @pl.when(ylo == 1)
        def _():
            for head in range(2):
                for c in kv_mate[head][0::2]:
                    c.start()

        for c in kv_here[0] + kv_here[1]:
            c.start()

    for c in a2m + a2n:
        c.wait_recv()
    add(at_o, at_sum.at[y], at_r2.at[0], at_r2.at[1])
    locals_out.append(here_now(at_o, o_at))

    for c in kv_mate[0] + kv_mate[1] + q_out + [w_last]:
        c.wait_recv()
    for c in locals_out + kv_here[0] + kv_here[1]:
        c.wait()
    net.drain()
    assert (net.n_send, net.n_recv, n_local[0]) == COUNTS, (net.n_send, net.n_recv, n_local)
    w_last.wait_send()
    total_of(d_out.at[:, 0:256, :], k_send=kv_send).wait_send()
    for sent, k_send in ((dke, edge_send), (wg_r1, w1_send), (wg_r2, w2_send), (wf.at[0], fwd_send)):
        total_of(sent, k_send=k_send).wait_send()

    @pl.when(cell == 0)
    def _():
        @pl.when(ylo == 0)
        def _():
            for c in b_mate:
                c.wait_send()

        for c in b_to_x:
            c.wait_send()

    to_x_peers(lambda c: c.wait_send())

    @pl.when(z == 0)
    def _():
        total_of(d0_zr, k_send=b_send).wait_send()

        for d in range(1, NX):

            @pl.when(x == d)
            def _():
                d0_o[d - 1].wait_send()

    for d in range(1, NZ):

        @pl.when(z == d)
        def _():
            d0_z[d - 1].wait_send()


def hand_over_kernel(*refs):
    n = 5
    ins, outs, bufs, sem = refs[:n], refs[n : 2 * n], refs[2 * n : 3 * n], refs[3 * n]
    reads = [pltpu.make_async_copy(ins[i], bufs[i], sem.at[0, i]) for i in range(n)]
    writes = [pltpu.make_async_copy(bufs[i], outs[i], sem.at[1, i]) for i in range(n)]
    for c in reads:
        c.start()
    for i in range(n):
        reads[i].wait()
        writes[i].start()
    for c in writes:
        c.wait()


def anywhere(n):
    return [pl.BlockSpec(memory_space=pl.ANY)] * n


def local(queries, key_heads, value_heads, out_weight, block_lists, out_grad):
    results = (
        jax.ShapeDtypeStruct((256, 1024), BF),
        jax.ShapeDtypeStruct((256, 512), BF),
        jax.ShapeDtypeStruct((256, 512), BF),
        jax.ShapeDtypeStruct((256, 512), BF),
        jax.ShapeDtypeStruct((64, 512), F32),
    )
    b, f = (lambda *s: pltpu.VMEM(s, BF)), (lambda *s: pltpu.VMEM(s, F32))
    scratch = [
        pltpu.SMEM((3, 128), jnp.int32),
        b(512, 256),
        b(1536, 256),
        b(1536, 256),
        b(256, 256),
        b(NX, NZ, 128, 256),
        b(2, 4, 256, 1024),
        b(2, 4, 256, 1024),
        b(4, 8, 256, 128),
        f(8, 128, 1280),
        b(512, 256),
        b(512, 256),
        f(1536, 256),
        f(1536, 256),
        f(2, 128, 256),
        b(512, 256),
        b(4, 256, 1024),
        b(4, 256, 1024),
        b(2, 128, 1024),
        b(2, 256, 1024),
        b(256, 1024),
        b(8, 256, 128),
        b(8, 256, 128),
        b(2, 8, 256, 128),
        f(8, 256, 128),
        b(2, 4, 256, 128),
        b(2, 4, 256, 128),
        f(128, 256),
        b(2, 2, 2, 512, 128),
        b(2, 2, 2, 512, 128),
        b(256, 256),
        b(3, 64, 256),
        b(64, 256),
        b(7, 64, 256),
        b(64, 256),
        b(3, 64, 256),
        f(2, 512, 256),
        b(2, 512, 256),
        pltpu.SemaphoreType.DMA((N_SEND,)),
        pltpu.SemaphoreType.DMA((N_RECV,)),
        pltpu.SemaphoreType.DMA((N_LOCAL,)),
    ]
    outs = pl.pallas_call(
        layer_kernel,
        out_shape=results,
        in_specs=anywhere(6),
        out_specs=tuple(anywhere(5)),
        scratch_shapes=scratch,
        compiler_params=pltpu.CompilerParams(
            collective_id=0, has_side_effects=True, vmem_limit_bytes=60 * 1024 * 1024
        ),
        name="layer",
    )(queries, key_heads, value_heads, out_weight, block_lists.T, out_grad)
    return pl.pallas_call(
        hand_over_kernel,
        out_shape=results,
        in_specs=anywhere(5),
        out_specs=tuple(anywhere(5)),
        scratch_shapes=[pltpu.VMEM(r.shape, r.dtype) for r in results]
        + [pltpu.SemaphoreType.DMA((2, 5))],
        name="hand_over",
    )(*outs)


def solution(mesh):
    placed = P("ctx", "head")
    return jax.shard_map(
        local,
        mesh=mesh,
        in_specs=(placed, placed, placed, placed, P(), placed),
        out_specs=(placed,) * 5,
        check_vma=False,
    )
```
